128 devices in a mesh: facet: 16 (over x, y), sub: 8 (over z, core).
Axes of the slice: x: 4, y: 4, z: 4, core: 2. Of those that a mesh axis runs over, the one named last changes fastest.
Arguments:
- model_image: float32 [16, 128, 8192], P('facet'), may hold values from -6 to 6
- step_sizes: float32 [2], replicated, may hold values from 0.3 to 1
- facet_offsets: int32 [2, 16], replicated, may hold values from 0 to 57344
- col_offsets: int32 [8], P('sub'), may hold values from 0 to 65280
- row_offsets: int32 [8, 16], P('sub'), may hold values from 0 to 65280
- counts: int32 [8, 16], P('sub'), may hold values from 1024 to 4096, as said below
- vis_uv: int32 [2, 8, 16, 4096], P(None, 'sub', 'facet'), may hold values from 32 to 2015
- vis_obs: bfloat16 [2, 8, 16, 4096], P(None, 'sub', 'facet'), may hold values from -6 to 6
- vis_weight: bfloat16 [8, 16, 4096], P('sub', 'facet'), may hold values from 0.25 to 4
Outputs:
- updated_image: float32 [16, 128, 8192], P('facet')
- residual_vis: float32 [2, 8, 16, 4096], P(None, 'sub', 'facet')
The draws below stay inside these ranges and needn't reach their ends.
Inputs may be any that keep to these rules, and one draw needn't show every extreme that they name: The visibilities of a subgrid fill its first counts slots; every draw has a subgrid with exactly 4096 visibilities and one with exactly 1024.
All inputs are finite; a program needn't handle non-finite values.
Results may differ from the reference program's by a relative error of at most 0.017.
Values may be sent and summed in bfloat16 or wider, within the bound.
No kernel may reach another device: no remote copies, remote signals or barrier semaphores. Data moves between devices by JAX's collectives and lax.ppermute only.
A program may use at most 64 MiB of HBM per device.

```python
import math
import jax
import jax.numpy as jnp
from jax import lax

NIMG = 65536
FW = 8192
FROWS = 128
SGW = 256
VCAP = 4096
VMIN = 1024
VB = 512
OS = 8
KSUP = 4
ITERS = 2
FACETS = 16
NCOL = 8
NROWSG = 16


def draw_counts(key, part):
    subgrid_total = NCOL * NROWSG
    draws_raw = jax.random.randint(jax.random.fold_in(key, 11), (subgrid_total,), 0, 1025, dtype=jnp.int32)
    cubed_raw = draws_raw * draws_raw // 1024 * draws_raw // 1024
    values = VMIN + cubed_raw * (VCAP - VMIN) // 1024
    top_slot = jax.random.randint(jax.random.fold_in(key, 12), (), 0, subgrid_total, dtype=jnp.int32)
    low_shift = jax.random.randint(jax.random.fold_in(key, 13), (), 1, subgrid_total, dtype=jnp.int32)
    low_slot = (top_slot + low_shift) % subgrid_total
    slot_ids = jnp.arange(subgrid_total, dtype=jnp.int32)
    values = jnp.where(slot_ids == top_slot, VCAP, values)
    values = jnp.where(slot_ids == low_slot, VMIN, values)
    return values.reshape(NCOL, NROWSG).astype(jnp.int32)


def plant(array, key, low, top_value):
    longest = array.shape.index(max(array.shape))
    spots = []
    for shift in (0, 1):
        where = [jax.random.randint(jax.random.fold_in(key, axis), (), 0, length) for axis, length in enumerate(array.shape)]
        where[longest] = (where[longest] + shift) % array.shape[longest]
        spots.append(tuple(where))
    return array.at[spots[0]].set(low).at[spots[1]].set(top_value)


def shard_levels(key, extent, pieces, smallest, high):
    def one(axis_at, parts):
        steps = jax.random.uniform(jax.random.fold_in(jax.random.fold_in(key, 6), axis_at), (parts,), jnp.float32, smallest / len(pieces), high / len(pieces))
        return jnp.repeat(jnp.exp(steps), extent[axis_at] // parts).reshape((-1,) + (1,) * (len(extent) - axis_at - 1))

    level = one(*pieces[0])
    for cut in pieces[1:]:
        level = level * one(*cut)
    return level


def bell_draw(rng, shape, spread, limit, pieces=(), kind=jnp.bfloat16):
    array = spread * jax.random.normal(rng, shape, jnp.float32)
    if pieces:
        array = array * shard_levels(rng, shape, pieces, -0.22, 0.18)
    return jnp.clip(array, -limit, limit).astype(kind)


def setup_inputs(seed: int = 0) -> dict:
    key_of = jax.random.split(jax.random.key(seed), 10)
    model_image = bell_draw(key_of[0], (FACETS, FROWS, FW), 1.0, 6.0, ((0, 16),), jnp.float32)
    step_sizes = jnp.clip(jnp.exp(jax.random.uniform(key_of[1], (ITERS,), jnp.float32, math.log(0.3), math.log(1.0))), 0.3, 1.0)
    facet_offsets = plant(jax.random.randint(key_of[2], (2, FACETS), 0, NIMG - FW + 1), jax.random.fold_in(key_of[2], 1), 0, NIMG - FW).astype(jnp.int32)
    col_offsets = plant(jax.random.randint(key_of[3], (NCOL,), 0, NIMG - SGW + 1), jax.random.fold_in(key_of[3], 1), 0, NIMG - SGW).astype(jnp.int32)
    row_offsets = plant(jax.random.randint(key_of[4], (NCOL, NROWSG), 0, NIMG - SGW + 1), jax.random.fold_in(key_of[4], 1), 0, NIMG - SGW).astype(jnp.int32)
    counts = draw_counts(jax.random.fold_in(key_of[9], 71), 0)
    vis_uv = plant(jax.random.randint(key_of[6], (2, NCOL, NROWSG, VCAP), OS * KSUP, OS * (SGW - KSUP)), jax.random.fold_in(key_of[6], 1), OS * KSUP, (OS * (SGW - KSUP)) - 1).astype(jnp.int32)
    vis_obs = bell_draw(key_of[7], (2, NCOL, NROWSG, VCAP), 1.0, 6.0, ((1, 8), (2, 16)))
    vis_weight = jnp.clip(jnp.exp(math.log(4.0) - 2.7725887 * jax.random.uniform(key_of[8], (NCOL, NROWSG, VCAP), jnp.float32) ** shard_levels(key_of[8], (NCOL, NROWSG, VCAP), ((0, 8), (1, 16)), -0.2, 0.2)), 0.25, 4.0).astype(jnp.bfloat16)
    return {"model_image": model_image, "step_sizes": step_sizes, "facet_offsets": facet_offsets, "col_offsets": col_offsets, "row_offsets": row_offsets, "counts": counts, "vis_uv": vis_uv, "vis_obs": vis_obs, "vis_weight": vis_weight}


two_pi = 2.0 * math.pi

def phase_index(frequency, pixels):
    pixel_low = pixels % 256
    pixel_high = pixels // 256
    return (frequency * pixel_low + frequency * pixel_high % (NIMG // 256) * 256) % NIMG

def row_table(frequency_start, pixel_start):
    frequency = frequency_start + jnp.arange(SGW, dtype=jnp.int32)
    pixels = pixel_start + jnp.arange(FROWS, dtype=jnp.int32)
    angles = phase_index(frequency[:, None], pixels[None, :]).astype(jnp.float32) * (two_pi / NIMG)
    return jnp.concatenate([jnp.cos(angles), jnp.sin(angles)], axis=1).astype(jnp.bfloat16)

def row_tables(frequency_starts, pixel_start):
    return jax.vmap(lambda single: row_table(single, pixel_start))(frequency_starts)

def column_table(frequency_start, pixel_start):
    frequency = frequency_start + jnp.arange(SGW, dtype=jnp.int32)
    pixels = pixel_start + jnp.arange(FW, dtype=jnp.int32)
    angles = phase_index(frequency[None, :], pixels[:, None]).astype(jnp.float32) * (two_pi / NIMG)
    return jnp.concatenate([jnp.cos(angles), -jnp.sin(angles)], axis=1).astype(jnp.bfloat16)

def expand_section(section_rows):
    real_half = section_rows[:, :SGW]
    imag_half = section_rows[:, SGW:]
    lower_rows = jnp.concatenate([imag_half, -real_half], axis=1)
    return jnp.concatenate([section_rows, lower_rows], axis=0)

def fold_back(back_rows):
    real_part = back_rows[..., :FROWS, :SGW] - back_rows[..., FROWS:, SGW:]
    imag_part = back_rows[..., :FROWS, SGW:] + back_rows[..., FROWS:, :SGW]
    return jnp.concatenate([real_part, imag_part], axis=-1)

def kernel_rows(position):
    offset = (jnp.arange(SGW, dtype=jnp.int32) * OS + OS // 2)[None, :] - position[:, None]
    distance = offset.astype(jnp.float32) / OS
    inside = jnp.abs(offset) <= KSUP * OS
    return jnp.where(inside, jnp.exp(-0.5 * distance * distance), 0.0).astype(jnp.bfloat16)

def block_pass(grid_bf, row_positions, column_positions, observed, weight, is_live):
    row_kernel = kernel_rows(row_positions)
    column_kernel = kernel_rows(column_positions)
    sampled = jnp.dot(row_kernel, grid_bf, preferred_element_type=jnp.float32)
    column_float = column_kernel.astype(jnp.float32)
    predicted_real = lax.optimization_barrier(jnp.sum(sampled[:, :SGW] * column_float, axis=1))
    predicted_imag = lax.optimization_barrier(jnp.sum(sampled[:, SGW:] * column_float, axis=1))
    weight_float = weight.astype(jnp.float32)
    residual_real = jnp.where(is_live, weight_float * (observed[0].astype(jnp.float32) - predicted_real), 0.0)
    residual_imag = jnp.where(is_live, weight_float * (observed[1].astype(jnp.float32) - predicted_imag), 0.0)
    weighted = jnp.concatenate([residual_real[:, None] * column_float, residual_imag[:, None] * column_float], axis=1).astype(jnp.bfloat16)
    block_grid = lax.dot_general(row_kernel, weighted, (((0,), (0,)), ((), ())), preferred_element_type=jnp.float32)
    return (block_grid, jnp.stack([residual_real, residual_imag]))

def sweep_blocks(grid_bf, positions, observed, weight, live_total, blocks):
    length = positions.shape[1]

    def one_block(block_index, running):
        grid_sum, residual = running
        first_row = (block_index * VB).astype(jnp.int32)
        position_part = lax.dynamic_slice_in_dim(positions, first_row, VB, 1)
        observed_part = lax.dynamic_slice_in_dim(observed, first_row, VB, 1)
        weight_part = lax.dynamic_slice_in_dim(weight, first_row, VB, 0)
        is_live = first_row + jnp.arange(VB, dtype=jnp.int32) < live_total
        block_grid, values = block_pass(grid_bf, position_part[0], position_part[1], observed_part, weight_part, is_live)
        residual = lax.dynamic_update_slice(residual, values, (jnp.int32(0), first_row))
        return (grid_sum + block_grid, residual)
    starting = (jnp.zeros((SGW, 2 * SGW), jnp.float32), jnp.zeros((2, length), jnp.float32))
    return lax.fori_loop(0, blocks, one_block, starting)

def reference(model_image, step_sizes, facet_offsets, col_offsets, row_offsets, counts, vis_uv, vis_obs, vis_weight):
    norm_factor = 1.0 / math.sqrt(FACETS * FROWS * FW)
    subgrid_total = NCOL * NROWSG
    facet_ids = jnp.arange(FACETS, dtype=jnp.int32)
    column_ids = jnp.arange(NCOL, dtype=jnp.int32)
    flat_positions = jnp.moveaxis(vis_uv.reshape(2, subgrid_total, VCAP), 1, 0)
    flat_observed = jnp.moveaxis(vis_obs.reshape(2, subgrid_total, VCAP), 1, 0)
    flat_weight = vis_weight.reshape(subgrid_total, VCAP)
    flat_counts = counts.reshape(subgrid_total)
    model_now = model_image
    residual = jnp.zeros((subgrid_total, 2, VCAP), jnp.float32)
    for cycle_index in range(ITERS):
        model_bf = model_now.astype(jnp.bfloat16)

        def facet_forward(running, facet_id):

            def column_forward(column_id):
                columns_factor = column_table(col_offsets[column_id], facet_offsets[1, facet_id])
                section_rows = jnp.dot(model_bf[facet_id], columns_factor, preferred_element_type=jnp.float32).astype(jnp.bfloat16)
                rows_factor = row_tables(row_offsets[column_id], facet_offsets[0, facet_id])
                product = jnp.dot(rows_factor.reshape(NROWSG * SGW, 2 * FROWS), expand_section(section_rows), preferred_element_type=jnp.float32)
                return product.reshape(NROWSG, SGW, 2 * SGW)
            return (running + lax.map(column_forward, column_ids), None)
        summed, unused = lax.scan(facet_forward, jnp.zeros((NCOL, NROWSG, SGW, 2 * SGW), jnp.float32), facet_ids)
        grids = (norm_factor * summed).astype(jnp.bfloat16).reshape(subgrid_total, SGW, 2 * SGW)

        def subgrid_pass(subgrid_items):
            grid_bf, positions, observed, weight, live_total = subgrid_items
            return sweep_blocks(grid_bf, positions, observed, weight, live_total, (live_total + VB - 1) // VB)
        gridded, residual = lax.map(subgrid_pass, (grids, flat_positions, flat_observed, flat_weight, flat_counts))
        gridded_bf = gridded.astype(jnp.bfloat16).reshape(NCOL, NROWSG, SGW, 2 * SGW)

        def facet_adjoint(facet_id):

            def column_adjoint(running, column_id):
                rows_factor = row_tables(row_offsets[column_id], facet_offsets[0, facet_id])
                back_rows = lax.dot_general(rows_factor.reshape(NROWSG * SGW, 2 * FROWS), gridded_bf[column_id].reshape(NROWSG * SGW, 2 * SGW), (((0,), (0,)), ((), ())), preferred_element_type=jnp.float32)
                adjoint_rows = fold_back(back_rows).astype(jnp.bfloat16)
                columns_factor = column_table(col_offsets[column_id], facet_offsets[1, facet_id])
                term = lax.dot_general(adjoint_rows, columns_factor, (((1,), (1,)), ((), ())), preferred_element_type=jnp.float32)
                return (running + term, None)
            total_rows, unused_rows = lax.scan(column_adjoint, jnp.zeros((FROWS, FW), jnp.float32), column_ids)
            return norm_factor * total_rows
        gradient = lax.map(facet_adjoint, facet_ids)
        model_now = model_now + step_sizes[cycle_index] * gradient
    residual_out = jnp.moveaxis(residual, 0, 1).reshape(2, NCOL, NROWSG, VCAP)
    return (model_now, residual_out)
```

```python
import math

import jax
import jax.numpy as jnp
from jax import lax
from jax.experimental import pallas as pl
from jax.experimental.pallas import tpu as pltpu
from jax.sharding import PartitionSpec as P

NIMG = 65536
FW = 8192
FROWS = 128
SGW = 256
VCAP = 4096
OS = 8
KSUP = 4
ITERS = 2
FACETS = 16
NCOL = 8
NROWSG = 16
SLICE = SGW // FACETS

STEP1 = 256
HIGH1 = FW // STEP1
STEP5 = 512
HIGH5 = FW // STEP5
PAIR5 = 2
VBLOCK = 1024

BF = jnp.bfloat16
F32 = jnp.float32
I32 = jnp.int32
NORM = 1.0 / math.sqrt(FACETS * FROWS * FW)
UNIT = 2.0 * math.pi / NIMG
PARAMS = pltpu.CompilerParams(vmem_limit_bytes=56 << 20)
SMEM_SPEC = pl.BlockSpec(memory_space=pltpu.SMEM)
VMEM_SPEC = pl.BlockSpec(memory_space=pltpu.VMEM)


def cos_sin(index):
    quadrant = (index + NIMG // 8) >> 14
    angle = (index - (quadrant << 14)).astype(F32) * UNIT
    square = angle * angle
    sine = angle * (1.0 + square * (-1.0 / 6 + square * (1.0 / 120 + square * (-1.0 / 5040 + square / 362880))))
    cosine = 1.0 + square * (-0.5 + square * (1.0 / 24 + square * (-1.0 / 720 + square / 40320)))
    swapped = (quadrant & 1) != 0
    c = jnp.where(swapped, sine, cosine)
    s = jnp.where(swapped, cosine, sine)
    c = jnp.where(((quadrant + 1) & 2) != 0, -c, c)
    s = jnp.where((quadrant & 2) != 0, -s, s)
    return c, s


def phase(frequency, pixel):
    return cos_sin((frequency * pixel) & (NIMG - 1))


def iota(shape, dim):
    return lax.broadcasted_iota(I32, shape, dim)


def section_kernel(scalars, model_ref, out_ref, table_ref, pc_ref, ps_ref):
    column_start = scalars[0]
    pixel_start = scalars[1]
    freq = column_start + iota((STEP1, SGW), 1)
    c, s = phase(freq, iota((STEP1, SGW), 0))
    table_ref[:, :SGW] = c.astype(BF)
    table_ref[:, SGW:] = (-s).astype(BF)
    freq = column_start + iota((HIGH1, SGW), 1)
    c, s = phase(freq, pixel_start + STEP1 * iota((HIGH1, SGW), 0))
    pc_ref[...] = c
    ps_ref[...] = s
    acc_re = jnp.zeros((FROWS, SGW), F32)
    acc_im = jnp.zeros((FROWS, SGW), F32)
    for high in range(HIGH1):
        block = model_ref[:, high * STEP1 : (high + 1) * STEP1].astype(BF)
        product = jnp.dot(block, table_ref[...], preferred_element_type=F32)
        re = product[:, :SGW]
        im = product[:, SGW:]
        pc = pc_ref[high : high + 1, :]
        ps = ps_ref[high : high + 1, :]
        acc_re = acc_re + (re * pc + im * ps)
        acc_im = acc_im + (im * pc - re * ps)
    re = acc_re.T.astype(BF)
    im = acc_im.T.astype(BF)
    out_ref[:, :SLICE, :] = re.reshape(FACETS, SLICE, FROWS)
    out_ref[:, SLICE:, :] = im.reshape(FACETS, SLICE, FROWS)


def section(scalars, model):
    return pl.pallas_call(
        section_kernel,
        out_shape=jax.ShapeDtypeStruct((FACETS, 2 * SLICE, FROWS), BF),
        in_specs=[SMEM_SPEC, VMEM_SPEC],
        out_specs=VMEM_SPEC,
        scratch_shapes=[
            pltpu.VMEM((STEP1, 2 * SGW), BF),
            pltpu.VMEM((HIGH1, SGW), F32),
            pltpu.VMEM((HIGH1, SGW), F32),
        ],
        compiler_params=PARAMS,
        name="section",
    )(scalars, model)


def fill_row_phases(facet_starts, row_starts_ref, c2_ref, s2_ref, c1_ref, s1_ref):
    rows = row_starts_ref[...]
    freq = rows + iota((NROWSG, SGW), 1)
    for f in range(FACETS):
        c, s = phase(freq, facet_starts[f])
        c2_ref[f] = c
        s2_ref[f] = s
    c, s = phase(jnp.broadcast_to(rows, (NROWSG, FROWS)), iota((NROWSG, FROWS), 1))
    c1_ref[...] = c
    s1_ref[...] = s


ROW_SCRATCH = [
    pltpu.VMEM((FACETS, NROWSG, SGW), F32),
    pltpu.VMEM((FACETS, NROWSG, SGW), F32),
    pltpu.VMEM((NROWSG, FROWS), F32),
    pltpu.VMEM((NROWSG, FROWS), F32),
]


def grid_kernel(facet_starts, row_starts_ref, in_ref, out_ref, w_ref, c2_ref, s2_ref, c1_ref, s1_ref):
    fill_row_phases(facet_starts, row_starts_ref, c2_ref, s2_ref, c1_ref, s1_ref)
    c, s = phase(iota((FROWS, SGW), 0), iota((FROWS, SGW), 1))
    w_ref[:FROWS, :SGW] = c.astype(BF)
    w_ref[:FROWS, SGW:] = (-s).astype(BF)
    w_ref[FROWS:, :SGW] = s.astype(BF)
    w_ref[FROWS:, SGW:] = c.astype(BF)

    def one(r, carry):
        c1 = c1_ref[pl.ds(r, 1), :]
        s1 = s1_ref[pl.ds(r, 1), :]
        re = in_ref[:, :SLICE, :].reshape(FACETS * SLICE, FROWS).astype(F32)
        im = in_ref[:, SLICE:, :].reshape(FACETS * SLICE, FROWS).astype(F32)
        turned = jnp.concatenate([re * c1 + im * s1, im * c1 - re * s1], axis=1).astype(BF)
        product = jnp.dot(turned, w_ref[...], preferred_element_type=F32)
        acc_re = jnp.zeros((SLICE, SGW), F32)
        acc_im = jnp.zeros((SLICE, SGW), F32)
        for f in range(FACETS):
            re = product[f * SLICE : (f + 1) * SLICE, :SGW]
            im = product[f * SLICE : (f + 1) * SLICE, SGW:]
            c2 = c2_ref[f, pl.ds(r, 1), :]
            s2 = s2_ref[f, pl.ds(r, 1), :]
            acc_re = acc_re + (re * c2 + im * s2)
            acc_im = acc_im + (im * c2 - re * s2)
        out_ref[r, :SLICE, :] = (NORM * acc_re).astype(BF)
        out_ref[r, SLICE:, :] = (NORM * acc_im).astype(BF)
        return carry

    lax.fori_loop(0, NROWSG, one, 0, unroll=4)


def grids(facet_starts, row_starts, sections):
    return pl.pallas_call(
        grid_kernel,
        out_shape=jax.ShapeDtypeStruct((NROWSG, 2 * SLICE, SGW), BF),
        in_specs=[SMEM_SPEC, VMEM_SPEC, VMEM_SPEC],
        out_specs=VMEM_SPEC,
        scratch_shapes=[pltpu.VMEM((2 * FROWS, 2 * SGW), BF)] + ROW_SCRATCH,
        compiler_params=PARAMS,
        name="grids",
    )(facet_starts, row_starts, sections)


def adjoint_kernel(facet_starts, row_starts_ref, in_ref, out_ref, w_ref, c2_ref, s2_ref, c1_ref, s1_ref):
    fill_row_phases(facet_starts, row_starts_ref, c2_ref, s2_ref, c1_ref, s1_ref)
    c, s = phase(iota((SGW, FROWS), 0), iota((SGW, FROWS), 1))
    w_ref[:SGW, :FROWS] = c.astype(BF)
    w_ref[:SGW, FROWS:] = s.astype(BF)
    w_ref[SGW:, :FROWS] = (-s).astype(BF)
    w_ref[SGW:, FROWS:] = c.astype(BF)

    def one(f, carry):
        lines_re = []
        lines_im = []
        for r in range(NROWSG):
            re = in_ref[r, :SLICE, :].astype(F32)
            im = in_ref[r, SLICE:, :].astype(F32)
            c2 = c2_ref[f, pl.ds(r, 1), :]
            s2 = s2_ref[f, pl.ds(r, 1), :]
            lines_re.append((re * c2 - im * s2).astype(BF))
            lines_im.append((im * c2 + re * s2).astype(BF))
        turned = jnp.concatenate(
            [jnp.concatenate(lines_re, axis=0), jnp.concatenate(lines_im, axis=0)], axis=1
        )
        product = jnp.dot(turned, w_ref[...], preferred_element_type=F32)
        acc_re = jnp.zeros((SLICE, FROWS), F32)
        acc_im = jnp.zeros((SLICE, FROWS), F32)
        for r in range(NROWSG):
            re = product[r * SLICE : (r + 1) * SLICE, :FROWS]
            im = product[r * SLICE : (r + 1) * SLICE, FROWS:]
            c1 = c1_ref[r : r + 1, :]
            s1 = s1_ref[r : r + 1, :]
            acc_re = acc_re + (re * c1 - im * s1)
            acc_im = acc_im + (im * c1 + re * s1)
        out_ref[f, :SLICE, :] = acc_re.astype(BF)
        out_ref[f, SLICE:, :] = acc_im.astype(BF)
        return carry

    lax.fori_loop(0, FACETS, one, 0, unroll=4)


def adjoint(facet_starts, row_starts, gridded):
    return pl.pallas_call(
        adjoint_kernel,
        out_shape=jax.ShapeDtypeStruct((FACETS, 2 * SLICE, FROWS), BF),
        in_specs=[SMEM_SPEC, VMEM_SPEC, VMEM_SPEC],
        out_specs=VMEM_SPEC,
        scratch_shapes=[pltpu.VMEM((2 * SGW, 2 * FROWS), BF)] + ROW_SCRATCH,
        compiler_params=PARAMS,
        name="adjoint",
    )(facet_starts, row_starts, gridded)


def kernel_columns(position):
    cells = iota((SGW, position.shape[1]), 0) * OS + OS // 2
    offset = cells - position
    distance = offset.astype(F32) * (1.0 / OS)
    inside = jnp.abs(offset) <= KSUP * OS
    return jnp.where(inside, jnp.exp(-0.5 * distance * distance), 0.0).astype(BF)


def visibility_kernel(count_ref, uv_ref, obs_ref, weight_ref, in_ref, gridded_ref, res_ref, acc_ref):
    count = count_ref[0]
    grid_re = in_ref[:, :SLICE, :].reshape(SGW, SGW)
    grid_im = in_ref[:, SLICE:, :].reshape(SGW, SGW)
    for block in range(VCAP // VBLOCK):
        cut = slice(block * VBLOCK, (block + 1) * VBLOCK)
        ku = kernel_columns(uv_ref[0:1, cut])
        kv = kernel_columns(uv_ref[1:2, cut])
        kvf = kv.astype(F32)
        live = block * VBLOCK + iota((1, VBLOCK), 1) < count
        weight = weight_ref[0:1, cut].astype(F32)
        for part, grid in ((0, grid_re), (1, grid_im)):
            sampled = jnp.dot(grid, ku, preferred_element_type=F32)
            predicted = jnp.sum(sampled * kvf, axis=0, keepdims=True)
            observed = obs_ref[part : part + 1, cut].astype(F32)
            residual = jnp.where(live, weight * (observed - predicted), 0.0)
            res_ref[part : part + 1, cut] = residual
            weighted = (residual * kvf).astype(BF)
            total = lax.dot_general(
                weighted, ku, (((1,), (1,)), ((), ())), preferred_element_type=F32
            )
            if block:
                total = total + acc_ref[part]
            if block + 1 < VCAP // VBLOCK:
                acc_ref[part] = total
            else:
                lines = total.astype(BF).reshape(FACETS, SLICE, SGW)
                gridded_ref[:, part * SLICE : (part + 1) * SLICE, :] = lines


def visibilities(count, uv, obs, weight, grid):
    return pl.pallas_call(
        visibility_kernel,
        out_shape=(
            jax.ShapeDtypeStruct((FACETS, 2 * SLICE, SGW), BF),
            jax.ShapeDtypeStruct((2, VCAP), F32),
        ),
        in_specs=[SMEM_SPEC] + [VMEM_SPEC] * 4,
        out_specs=(VMEM_SPEC, VMEM_SPEC),
        scratch_shapes=[pltpu.VMEM((2, SGW, SGW), F32)],
        compiler_params=PARAMS,
        name="visibilities",
    )(count, uv, obs, weight, grid)


def update_kernel(step_ref, adj_ref, tc_ref, ts_ref, pc_ref, ps_ref, model_ref, out_ref, re_ref, im_ref, turned_ref):
    columns = NCOL * SGW

    @pl.when(pl.program_id(0) == 0)
    def _():
        re = adj_ref[:, :SLICE, :].reshape(columns, FROWS).astype(F32)
        im = adj_ref[:, SLICE:, :].reshape(columns, FROWS).astype(F32)
        re_ref[...] = re.T
        im_ref[...] = im.T

    re = re_ref[...]
    im = im_ref[...]
    for p in range(PAIR5):
        pc = pc_ref[pl.ds(pl.program_id(0) * PAIR5 + p, 1), :]
        ps = ps_ref[pl.ds(pl.program_id(0) * PAIR5 + p, 1), :]
        turned_ref[p * FROWS : (p + 1) * FROWS, :columns] = (re * pc - im * ps).astype(BF)
        turned_ref[p * FROWS : (p + 1) * FROWS, columns:] = (im * pc + re * ps).astype(BF)
    gradient = jnp.dot(turned_ref[:, :columns], tc_ref[...], preferred_element_type=F32)
    gradient = gradient + jnp.dot(turned_ref[:, columns:], ts_ref[...], preferred_element_type=F32)
    step = step_ref[0] * NORM
    for p in range(PAIR5):
        cut = slice(p * STEP5, (p + 1) * STEP5)
        out_ref[:, cut] = model_ref[:, cut] + step * gradient[p * FROWS : (p + 1) * FROWS]


def update(step, adj, tables, model):
    columns = NCOL * SGW
    wide = pl.BlockSpec((FROWS, PAIR5 * STEP5), lambda i: (0, i))
    return pl.pallas_call(
        update_kernel,
        grid=(HIGH5 // PAIR5,),
        out_shape=jax.ShapeDtypeStruct((FROWS, FW), F32),
        in_specs=[SMEM_SPEC] + [VMEM_SPEC] * 5 + [wide],
        out_specs=wide,
        scratch_shapes=[
            pltpu.VMEM((FROWS, columns), F32),
            pltpu.VMEM((FROWS, columns), F32),
            pltpu.VMEM((PAIR5 * FROWS, 2 * columns), BF),
        ],
        compiler_params=PARAMS,
        name="update",
    )(step, adj, *tables, model)


def update_tables(column_starts, pixel_start):
    first = column_starts[None, :, None] + SLICE * jnp.arange(FACETS, dtype=I32)[:, None, None]
    freq = (first + jnp.arange(SLICE, dtype=I32)).reshape(-1)
    c, s = phase(freq[:, None], jnp.arange(STEP5, dtype=I32)[None, :])
    pc, ps = phase(freq[None, :], pixel_start + STEP5 * jnp.arange(HIGH5, dtype=I32)[:, None])
    return c.astype(BF), (-s).astype(BF), pc, ps


def exchange(value):
    return lax.all_to_all(value, "facet", split_axis=0, concat_axis=0, tiled=True)


def to_facets(value):
    copies = jnp.broadcast_to(value[:, None], (FACETS, NCOL, *value.shape[1:]))
    copies = copies.reshape(FACETS * NCOL, *value.shape[1:])
    return lax.all_to_all(copies, ("facet", "sub"), split_axis=0, concat_axis=0, tiled=True)


def local(
    model_image,
    step_sizes,
    facet_offsets,
    col_offsets,
    row_offsets,
    counts,
    vis_uv,
    vis_obs,
    vis_weight,
):
    my_facet = lax.axis_index("facet")
    column_starts = lax.all_gather(col_offsets, "sub", axis=0, tiled=True)
    pixel_start = facet_offsets[1, my_facet]
    scalars = jnp.stack([col_offsets[0], pixel_start])
    facet_starts = facet_offsets[0]
    row_starts = row_offsets.reshape(NROWSG, 1)
    count = lax.dynamic_slice_in_dim(counts[0], my_facet, 1, 0)
    uv = vis_uv.reshape(2, VCAP)
    obs = vis_obs.reshape(2, VCAP)
    weight = vis_weight.reshape(1, VCAP)
    tables = update_tables(column_starts, pixel_start)
    model = model_image[0]
    for cycle in range(ITERS):
        grid = exchange(grids(facet_starts, row_starts, exchange(section(scalars, model))))
        gridded, residual = visibilities(count, uv, obs, weight, grid)
        adj = to_facets(adjoint(facet_starts, row_starts, exchange(gridded)))
        model = update(lax.dynamic_slice_in_dim(step_sizes, cycle, 1, 0), adj, tables, model)
    return model[None], residual.reshape(2, 1, 1, VCAP)


def solution(mesh):
    in_specs = (
        P("facet", None, None),
        P(),
        P(),
        P("sub"),
        P("sub", None),
        P("sub", None),
        P(None, "sub", "facet", None),
        P(None, "sub", "facet", None),
        P("sub", "facet", None),
    )
    out_specs = (P("facet", None, None), P(None, "sub", "facet", None))
    return jax.shard_map(local, mesh=mesh, in_specs=in_specs, out_specs=out_specs, check_vma=False)
```

```python
import math

import jax
import jax.numpy as jnp
from jax import lax
from jax.experimental import pallas as pl
from jax.experimental.pallas import tpu as pltpu
from jax.sharding import PartitionSpec as P

NIMG = 65536
FW = 8192
FROWS = 128
SGW = 256
VCAP = 4096
OS = 8
KSUP = 4
FACETS = 16
NCOL = 8
NROWSG = 16
SLICE = SGW // FACETS
COLUMNS = NCOL * SGW

STEP1 = 256
HIGH1 = FW // STEP1
PARTS1 = 4
STEP5 = 512
HIGH5 = FW // STEP5
PAIR5 = 2
VBLOCK = 1024
CHUNK = 4

BF = jnp.bfloat16
F32 = jnp.float32
I32 = jnp.int32
NORM = 1.0 / math.sqrt(FACETS * FROWS * FW)
PARAMS = pltpu.CompilerParams(vmem_limit_bytes=56 << 20)
SMEM_SPEC = pl.BlockSpec(memory_space=pltpu.SMEM)
VMEM_SPEC = pl.BlockSpec(memory_space=pltpu.VMEM)


def cos_sin(index, bits=16):
    quadrant = (index + (1 << (bits - 3))) >> (bits - 2)
    angle = (index - (quadrant << (bits - 2))).astype(F32) * (2.0 * math.pi / (1 << bits))
    square = angle * angle
    sine = angle * (1.0 + square * (-1.0 / 6 + square * (1.0 / 120 + square * (-1.0 / 5040 + square / 362880))))
    cosine = 1.0 + square * (-0.5 + square * (1.0 / 24 + square * (-1.0 / 720 + square / 40320)))
    swapped = (quadrant & 1) != 0
    c = jnp.where(swapped, sine, cosine)
    s = jnp.where(swapped, cosine, sine)
    c = jnp.where(((quadrant + 1) & 2) != 0, -c, c)
    s = jnp.where((quadrant & 2) != 0, -s, s)
    return c, s


def phase(frequency, pixel):
    return cos_sin((frequency * pixel) & (NIMG - 1))


def iota(shape, dim):
    return lax.broadcasted_iota(I32, shape, dim)


def column_of(ref, count, lanes):
    row = iota((count, lanes), 0)
    value = jnp.zeros((count, lanes), I32)
    for i in range(count):
        value = jnp.where(row == i, ref[i], value)
    return value


def section_kernel(column_ref, offsets_ref, model_ref, out_ref, table_ref, pc_ref, ps_ref, re_ref, im_ref):
    part = pl.program_id(0)
    highs = HIGH1 // PARTS1

    @pl.when(part == 0)
    def _():
        column_start = column_ref[0]
        pixel_start = offsets_ref[1, lax.axis_index("facet")]
        freq = column_start + iota((STEP1, SGW), 1)
        c, s = phase(freq, iota((STEP1, SGW), 0))
        table_ref[:, :SGW] = c.astype(BF)
        table_ref[:, SGW:] = (-s).astype(BF)
        freq = column_start + iota((HIGH1, SGW), 1)
        c, s = phase(freq, pixel_start + STEP1 * iota((HIGH1, SGW), 0))
        pc_ref[...] = c
        ps_ref[...] = s
        re_ref[...] = jnp.zeros((FROWS, SGW), F32)
        im_ref[...] = jnp.zeros((FROWS, SGW), F32)

    acc_re = re_ref[...]
    acc_im = im_ref[...]
    for high in range(highs):
        block = model_ref[:, high * STEP1 : (high + 1) * STEP1].astype(BF)
        product = jnp.dot(block, table_ref[...], preferred_element_type=F32)
        re = product[:, :SGW]
        im = product[:, SGW:]
        pc = pc_ref[pl.ds(part * highs + high, 1), :]
        ps = ps_ref[pl.ds(part * highs + high, 1), :]
        acc_re = acc_re + (re * pc + im * ps)
        acc_im = acc_im + (im * pc - re * ps)
    re_ref[...] = acc_re
    im_ref[...] = acc_im

    @pl.when(part == PARTS1 - 1)
    def _():
        re = re_ref[...].T.astype(BF)
        im = im_ref[...].T.astype(BF)
        out_ref[:, :SLICE, :] = re.reshape(FACETS, SLICE, FROWS)
        out_ref[:, SLICE:, :] = im.reshape(FACETS, SLICE, FROWS)


def section(column_start, offsets, model):
    return pl.pallas_call(
        section_kernel,
        grid=(PARTS1,),
        out_shape=jax.ShapeDtypeStruct((FACETS, 2 * SLICE, FROWS), BF),
        in_specs=[SMEM_SPEC, SMEM_SPEC, pl.BlockSpec((FROWS, FW // PARTS1), lambda i: (0, i))],
        out_specs=VMEM_SPEC,
        scratch_shapes=[
            pltpu.VMEM((STEP1, 2 * SGW), BF),
            pltpu.VMEM((HIGH1, SGW), F32),
            pltpu.VMEM((HIGH1, SGW), F32),
            pltpu.VMEM((FROWS, SGW), F32),
            pltpu.VMEM((FROWS, SGW), F32),
        ],
        compiler_params=PARAMS,
        name="section",
    )(column_start, offsets, model)


def row_table_kernel(offsets_ref, rows_ref, table_ref, c_ref, s_ref):
    f = pl.program_id(0)
    pixel = offsets_ref[0, f] + iota((FROWS, SGW), 0)
    c, s = phase(iota((FROWS, SGW), 1), pixel)
    table_ref[:FROWS, :SGW] = c.astype(BF)
    table_ref[:FROWS, SGW:] = (-s).astype(BF)
    table_ref[FROWS:, :SGW] = s.astype(BF)
    table_ref[FROWS:, SGW:] = c.astype(BF)
    row = iota((NROWSG, FROWS), 0)
    freq = jnp.zeros((NROWSG, FROWS), I32)
    for r in range(NROWSG):
        freq = jnp.where(row == r, rows_ref[0, r], freq)
    c, s = phase(freq, offsets_ref[0, f] + iota((NROWSG, FROWS), 1))
    c_ref[0] = c
    s_ref[0] = s


def row_tables(offsets, rows):
    small = pl.BlockSpec((1, NROWSG, FROWS), lambda f: (f, 0, 0))
    return pl.pallas_call(
        row_table_kernel,
        grid=(FACETS,),
        out_shape=(
            jax.ShapeDtypeStruct((FACETS * 2 * FROWS, 2 * SGW), BF),
            jax.ShapeDtypeStruct((FACETS, NROWSG, FROWS), F32),
            jax.ShapeDtypeStruct((FACETS, NROWSG, FROWS), F32),
        ),
        in_specs=[SMEM_SPEC, SMEM_SPEC],
        out_specs=(pl.BlockSpec((2 * FROWS, 2 * SGW), lambda f: (f, 0)), small, small),
        compiler_params=PARAMS,
        name="row_tables",
    )(offsets, rows)


def grid_kernel(in_ref, c_ref, s_ref, table_ref, out_ref, turned_ref, acc_ref):
    part = pl.program_id(0)
    for k in range(CHUNK):
        f = part * CHUNK + k
        re = in_ref[f, :SLICE, :].astype(F32)
        im = in_ref[f, SLICE:, :].astype(F32)
        left = k * 2 * FROWS
        for r in range(NROWSG):
            c = c_ref[f, r : r + 1, :]
            s = s_ref[f, r : r + 1, :]
            lines = slice(r * SLICE, (r + 1) * SLICE)
            turned_ref[lines, left : left + FROWS] = (re * c + im * s).astype(BF)
            turned_ref[lines, left + FROWS : left + 2 * FROWS] = (im * c - re * s).astype(BF)
    product = jnp.dot(turned_ref[...], table_ref[...], preferred_element_type=F32)
    last = FACETS // CHUNK - 1

    @pl.when(part == 0)
    def _():
        acc_ref[...] = product

    @pl.when((part > 0) & (part < last))
    def _():
        acc_ref[...] += product

    @pl.when(part == last)
    def _():
        total = (NORM * (acc_ref[...] + product)).astype(BF)
        out_ref[:, :SLICE, :] = total[:, :SGW].reshape(NROWSG, SLICE, SGW)
        out_ref[:, SLICE:, :] = total[:, SGW:].reshape(NROWSG, SLICE, SGW)


def grids(sections, tables):
    table, c, s = tables
    return pl.pallas_call(
        grid_kernel,
        grid=(FACETS // CHUNK,),
        out_shape=jax.ShapeDtypeStruct((NROWSG, 2 * SLICE, SGW), BF),
        in_specs=[VMEM_SPEC] * 3 + [pl.BlockSpec((CHUNK * 2 * FROWS, 2 * SGW), lambda i: (i, 0))],
        out_specs=VMEM_SPEC,
        scratch_shapes=[
            pltpu.VMEM((NROWSG * SLICE, CHUNK * 2 * FROWS), BF),
            pltpu.VMEM((NROWSG * SLICE, 2 * SGW), F32),
        ],
        compiler_params=PARAMS,
        name="grids",
    )(sections, c, s, table)


def adjoint_kernel(in_ref, c_ref, s_ref, table_ref, out_ref, lines_ref):
    part = pl.program_id(0)

    @pl.when(part == 0)
    def _():
        lines_ref[:, :SGW] = in_ref[:, :SLICE, :].reshape(NROWSG * SLICE, SGW)
        lines_ref[:, SGW:] = in_ref[:, SLICE:, :].reshape(NROWSG * SLICE, SGW)

    for k in range(CHUNK):
        f = part * CHUNK + k
        table = table_ref[k * 2 * FROWS : (k + 1) * 2 * FROWS, :]
        product = lax.dot_general(
            lines_ref[...], table, (((1,), (1,)), ((), ())), preferred_element_type=F32
        )
        acc_re = jnp.zeros((SLICE, FROWS), F32)
        acc_im = jnp.zeros((SLICE, FROWS), F32)
        for r in range(NROWSG):
            re = product[r * SLICE : (r + 1) * SLICE, :FROWS]
            im = product[r * SLICE : (r + 1) * SLICE, FROWS:]
            c = c_ref[f, r : r + 1, :]
            s = s_ref[f, r : r + 1, :]
            acc_re = acc_re + (re * c - im * s)
            acc_im = acc_im + (im * c + re * s)
        both = jnp.concatenate([acc_re, acc_im], axis=1).astype(BF)
        for copy in range(NCOL):
            out_ref[k, copy] = both


def adjoint(gridded, tables):
    table, c, s = tables
    return pl.pallas_call(
        adjoint_kernel,
        grid=(FACETS // CHUNK,),
        out_shape=jax.ShapeDtypeStruct((FACETS, NCOL, SLICE, 2 * FROWS), BF),
        in_specs=[VMEM_SPEC] * 3 + [pl.BlockSpec((CHUNK * 2 * FROWS, 2 * SGW), lambda i: (i, 0))],
        out_specs=pl.BlockSpec((CHUNK, NCOL, SLICE, 2 * FROWS), lambda i: (i, 0, 0, 0)),
        scratch_shapes=[pltpu.VMEM((NROWSG * SLICE, 2 * SGW), BF)],
        compiler_params=PARAMS,
        name="adjoint",
    )(gridded, c, s, table)


def kernel_columns(position):
    cells = iota((SGW, position.shape[1]), 0) * OS + OS // 2
    offset = cells - position
    distance = offset.astype(F32) * (1.0 / OS)
    inside = jnp.abs(offset) <= KSUP * OS
    return jnp.where(inside, jnp.exp(-0.5 * distance * distance), 0.0).astype(BF)


def vis_table_kernel(uv_ref, ku_ref, kv_ref):
    ku_ref[...] = kernel_columns(uv_ref[0:1, :])
    kv_ref[...] = kernel_columns(uv_ref[1:2, :])


def vis_tables(uv):
    wide = pl.BlockSpec((SGW, VBLOCK), lambda i: (0, i))
    shape = jax.ShapeDtypeStruct((SGW, VCAP), BF)
    return pl.pallas_call(
        vis_table_kernel,
        grid=(VCAP // VBLOCK,),
        out_shape=(shape, shape),
        in_specs=[pl.BlockSpec((2, VBLOCK), lambda i: (0, i))],
        out_specs=(wide, wide),
        compiler_params=PARAMS,
        name="vis_tables",
    )(uv)


def visibility_kernel(counts_ref, obs_ref, weight_ref, in_ref, ku_ref, kv_ref, gridded_ref, res_ref, acc_ref):
    part = pl.program_id(0)
    last = VCAP // VBLOCK - 1
    count = counts_ref[0, lax.axis_index("facet")]
    ku = ku_ref[...]
    kv = kv_ref[...].astype(F32)
    live = part * VBLOCK + iota((1, VBLOCK), 1) < count
    weight = weight_ref[...].astype(F32)
    totals = []
    for half in range(2):
        grid = in_ref[:, half * SLICE : (half + 1) * SLICE, :].reshape(SGW, SGW)
        sampled = jnp.dot(grid, ku, preferred_element_type=F32)
        predicted = jnp.sum(sampled * kv, axis=0, keepdims=True)
        observed = obs_ref[half : half + 1, :].astype(F32)
        residual = jnp.where(live, weight * (observed - predicted), 0.0)
        res_ref[half : half + 1, :] = residual
        weighted = (residual * kv).astype(BF)
        totals.append(
            lax.dot_general(weighted, ku, (((1,), (1,)), ((), ())), preferred_element_type=F32)
        )

    @pl.when(part == 0)
    def _():
        acc_ref[0] = totals[0]
        acc_ref[1] = totals[1]

    @pl.when((part > 0) & (part < last))
    def _():
        acc_ref[0] += totals[0]
        acc_ref[1] += totals[1]

    @pl.when(part == last)
    def _():
        for half in range(2):
            lines = (acc_ref[half] + totals[half]).astype(BF).reshape(FACETS, SLICE, SGW)
            gridded_ref[:, half * SLICE : (half + 1) * SLICE, :] = lines


def visibilities(counts, obs, weight, grid, tables):
    wide = pl.BlockSpec((SGW, VBLOCK), lambda i: (0, i))
    pair = pl.BlockSpec((2, VBLOCK), lambda i: (0, i))
    return pl.pallas_call(
        visibility_kernel,
        grid=(VCAP // VBLOCK,),
        out_shape=(
            jax.ShapeDtypeStruct((FACETS, 2 * SLICE, SGW), BF),
            jax.ShapeDtypeStruct((2, VCAP), F32),
        ),
        in_specs=[SMEM_SPEC, pair, pl.BlockSpec((1, VBLOCK), lambda i: (0, i)), VMEM_SPEC, wide, wide],
        out_specs=(VMEM_SPEC, pair),
        scratch_shapes=[pltpu.VMEM((2, SGW, SGW), F32)],
        compiler_params=PARAMS,
        name="visibilities",
    )(counts, obs, weight, grid, *tables)


def dirichlet(distance, pixel_start):
    distance = ((distance & (NIMG - 1)) ^ (NIMG // 2)) - NIMG // 2
    top = cos_sin((distance * (NIMG // (NIMG // FW * 2))) & (NIMG - 1))[1]
    bottom = cos_sin(distance, 17)[1]
    ratio = jnp.where(distance == 0, float(FW), top / jnp.where(distance == 0, 1.0, bottom))
    c, s = cos_sin((distance * (2 * pixel_start + FW - 1)) & (2 * NIMG - 1), 17)
    return c * ratio, s * ratio


def gram_kernel(step_ref, starts_ref, column_ref, offsets_ref, adj_ref, first_ref, out_ref, flip_ref, v_ref):
    wide = 2 * SGW
    pixel_start = offsets_ref[1, lax.axis_index("facet")]
    own = column_ref[0]
    row = iota((NCOL, wide), 0)
    starts = jnp.zeros((NCOL, wide), I32)
    for c in range(NCOL):
        starts = jnp.where(row == c, starts_ref[c], starts)
    lane = iota((NCOL, wide), 1)
    v_ref[0], v_ref[1] = dirichlet(starts - own + (lane - (SGW - 1)), pixel_start)
    v_ref[2], v_ref[3] = dirichlet(starts + own + (2 * (SGW - 1) - lane), pixel_start)
    anti = (iota((SGW, SGW), 0) + iota((SGW, SGW), 1)) == SGW - 1
    flip_ref[...] = jnp.where(anti, 1.0, 0.0).astype(BF)
    totals = [None] * 4
    for c in range(NCOL):
        lines = adj_ref[:, c].reshape(SGW, 2 * FROWS)
        turned = jnp.dot(flip_ref[...], lines, preferred_element_type=F32).astype(BF)
        for k in range(4):
            spread = jnp.broadcast_to(v_ref[k, c : c + 1, :], (SGW, wide))
            band = pltpu.roll(spread, SGW + 1, 1, stride=1, stride_axis=0)[:, :SGW].astype(BF)
            term = jnp.dot(band, lines if k < 2 else turned, preferred_element_type=F32)
            totals[k] = term if c == 0 else totals[k] + term
    scale = step_ref[0] * (0.5 * NORM)
    p1, p2, p3, p4 = totals
    re = p1[:, :FROWS] - p2[:, FROWS:] + p3[:, :FROWS] - p4[:, FROWS:]
    im = p2[:, :FROWS] + p1[:, FROWS:] - p4[:, :FROWS] - p3[:, FROWS:]
    first = first_ref[...].astype(F32)
    out_ref[:, :SLICE, :] = (first[:, :SLICE] + (scale * re).reshape(FACETS, SLICE, FROWS)).astype(BF)
    out_ref[:, SLICE:, :] = (first[:, SLICE:] + (scale * im).reshape(FACETS, SLICE, FROWS)).astype(BF)


def gram(steps, column_starts, column_start, offsets, adj, first):
    return pl.pallas_call(
        gram_kernel,
        out_shape=jax.ShapeDtypeStruct((FACETS, 2 * SLICE, FROWS), BF),
        in_specs=[SMEM_SPEC] * 4 + [VMEM_SPEC] * 2,
        out_specs=VMEM_SPEC,
        scratch_shapes=[
            pltpu.VMEM((SGW, SGW), BF),
            pltpu.VMEM((4, NCOL, 2 * SGW), F32),
        ],
        compiler_params=PARAMS,
        name="gram",
    )(steps, column_starts, column_start, offsets, adj.reshape(FACETS, NCOL, SLICE, 2 * FROWS), first)


def update_kernel(step_ref, adj0_ref, adj1_ref, tc_ref, ts_ref, pc_ref, ps_ref, model_ref, out_ref, both_ref, turned_ref):
    part = pl.program_id(0)

    @pl.when(part == 0)
    def _():
        first = step_ref[0] * NORM
        second = step_ref[1] * NORM
        for j in range(FACETS):
            lines0 = adj0_ref[j * NCOL : (j + 1) * NCOL].reshape(NCOL * SLICE, 2 * FROWS).astype(F32)
            lines1 = adj1_ref[j * NCOL : (j + 1) * NCOL].reshape(NCOL * SLICE, 2 * FROWS).astype(F32)
            both = first * lines0 + second * lines1
            both_ref[:, j * NCOL * SLICE : (j + 1) * NCOL * SLICE] = both.T

    re = both_ref[:FROWS, :]
    im = both_ref[FROWS:, :]
    for p in range(PAIR5):
        pc = pc_ref[pl.ds(part * PAIR5 + p, 1), :]
        ps = ps_ref[pl.ds(part * PAIR5 + p, 1), :]
        turned_ref[p * FROWS : (p + 1) * FROWS, :COLUMNS] = (re * pc - im * ps).astype(BF)
        turned_ref[p * FROWS : (p + 1) * FROWS, COLUMNS:] = (im * pc + re * ps).astype(BF)
    gradient = jnp.dot(turned_ref[:, :COLUMNS], tc_ref[...], preferred_element_type=F32)
    gradient = gradient + jnp.dot(turned_ref[:, COLUMNS:], ts_ref[...], preferred_element_type=F32)
    for p in range(PAIR5):
        cut = slice(p * STEP5, (p + 1) * STEP5)
        out_ref[:, cut] = model_ref[:, cut] + gradient[p * FROWS : (p + 1) * FROWS]


def update(steps, adj0, adj1, tables, model):
    wide = pl.BlockSpec((FROWS, PAIR5 * STEP5), lambda i: (0, i))
    return pl.pallas_call(
        update_kernel,
        grid=(HIGH5 // PAIR5,),
        out_shape=jax.ShapeDtypeStruct((FROWS, FW), F32),
        in_specs=[SMEM_SPEC] + [VMEM_SPEC] * 6 + [wide],
        out_specs=wide,
        scratch_shapes=[
            pltpu.VMEM((2 * FROWS, COLUMNS), F32),
            pltpu.VMEM((PAIR5 * FROWS, 2 * COLUMNS), BF),
        ],
        compiler_params=PARAMS,
        name="update",
    )(steps, adj0, adj1, *tables, model)


def update_tables(column_starts, pixel_start):
    first = column_starts[None, :, None] + SLICE * jnp.arange(FACETS, dtype=I32)[:, None, None]
    freq = (first + jnp.arange(SLICE, dtype=I32)).reshape(-1)
    c, s = phase(freq[:, None], jnp.arange(STEP5, dtype=I32)[None, :])
    pc, ps = phase(freq[None, :], pixel_start + STEP5 * jnp.arange(HIGH5, dtype=I32)[:, None])
    return c.astype(BF), (-s).astype(BF), pc, ps


def exchange(value):
    return lax.all_to_all(value, "facet", split_axis=0, concat_axis=0, tiled=True)


def to_facets(value):
    copies = value.reshape(FACETS * NCOL, *value.shape[2:])
    return lax.all_to_all(copies, ("facet", "sub"), split_axis=0, concat_axis=0, tiled=True)


def local(
    model_image,
    step_sizes,
    facet_offsets,
    col_offsets,
    row_offsets,
    counts,
    vis_uv,
    vis_obs,
    vis_weight,
):
    lines = jnp.broadcast_to(col_offsets[:, None], (8, 128))
    column_starts = lax.optimization_barrier(lax.all_gather(lines, "sub", axis=0, tiled=True))[::8, 0]
    uv = vis_uv.reshape(2, VCAP)
    obs = vis_obs.reshape(2, VCAP)
    weight = vis_weight.reshape(1, VCAP)
    model = model_image[0]
    first = section(col_offsets, facet_offsets, model)
    rows = row_tables(facet_offsets, row_offsets)
    kernels = vis_tables(uv)
    grid = exchange(grids(exchange(first), rows))
    gridded, residual = visibilities(counts, obs, weight, grid, kernels)
    adj0 = to_facets(adjoint(exchange(gridded), rows))
    tables = update_tables(column_starts, facet_offsets[1, lax.axis_index("facet")])
    second = gram(step_sizes, column_starts, col_offsets, facet_offsets, adj0, first)
    grid = exchange(grids(exchange(second), rows))
    gridded, residual = visibilities(counts, obs, weight, grid, kernels)
    adj1 = to_facets(adjoint(exchange(gridded), rows))
    model = update(step_sizes, adj0, adj1, tables, model)
    return model[None], residual.reshape(2, 1, 1, VCAP)


def solution(mesh):
    in_specs = (
        P("facet", None, None),
        P(),
        P(),
        P("sub"),
        P("sub", None),
        P("sub", None),
        P(None, "sub", "facet", None),
        P(None, "sub", "facet", None),
        P("sub", "facet", None),
    )
    out_specs = (P("facet", None, None), P(None, "sub", "facet", None))
    return jax.shard_map(local, mesh=mesh, in_specs=in_specs, out_specs=out_specs, check_vma=False)
```

```python
import math

import jax
import jax.numpy as jnp
from jax import lax
from jax.experimental import pallas as pl
from jax.experimental.pallas import tpu as pltpu
from jax.sharding import PartitionSpec as P

NIMG = 65536
FW = 8192
FROWS = 128
SGW = 256
VCAP = 4096
OS = 8
KSUP = 4
FACETS = 16
NCOL = 8
NROWSG = 16
SLICE = SGW // FACETS
COLUMNS = NCOL * SGW

STEP1 = 256
HIGH1 = FW // STEP1
PARTS1 = 2
STEP5 = 512
HIGH5 = FW // STEP5
PAIR5 = 2
VBLOCK = 1024
CHUNK = 4
UNROLL4 = 2

BF = jnp.bfloat16
F32 = jnp.float32
I32 = jnp.int32
NORM = 1.0 / math.sqrt(FACETS * FROWS * FW)
PARAMS = pltpu.CompilerParams(vmem_limit_bytes=16 << 20)
WIDE_PARAMS = pltpu.CompilerParams(vmem_limit_bytes=24 << 20)
SMEM_SPEC = pl.BlockSpec(memory_space=pltpu.SMEM)
VMEM_SPEC = pl.BlockSpec(memory_space=pltpu.VMEM)
HBM_SPEC = pl.BlockSpec(memory_space=pltpu.HBM)


def cos_sin(index, bits=16):
    quadrant = (index + (1 << (bits - 3))) >> (bits - 2)
    angle = (index - (quadrant << (bits - 2))).astype(F32) * (2.0 * math.pi / (1 << bits))
    square = angle * angle
    sine = angle * (1.0 + square * (-1.0 / 6 + square * (1.0 / 120 + square * (-1.0 / 5040 + square / 362880))))
    cosine = 1.0 + square * (-0.5 + square * (1.0 / 24 + square * (-1.0 / 720 + square / 40320)))
    swapped = (quadrant & 1) != 0
    c = jnp.where(swapped, sine, cosine)
    s = jnp.where(swapped, cosine, sine)
    c = jnp.where(((quadrant + 1) & 2) != 0, -c, c)
    s = jnp.where((quadrant & 2) != 0, -s, s)
    return c, s


def phase(frequency, pixel):
    return cos_sin((frequency * pixel) & (NIMG - 1))


def on_chip(value):
    return pltpu.with_memory_space_constraint(value, pltpu.VMEM)


def off_chip(value):
    return pltpu.with_memory_space_constraint(value, pltpu.HBM)


def write_out(pairs):
    copies = [pltpu.make_async_copy(source, target, sem) for source, target, sem in pairs]
    for copy in copies:
        copy.start()
    for copy in copies:
        copy.wait()


def iota(shape, dim):
    return lax.broadcasted_iota(I32, shape, dim)


def column_of(ref, count, lanes):
    row = iota((count, lanes), 0)
    value = jnp.zeros((count, lanes), I32)
    for i in range(count):
        value = jnp.where(row == i, ref[i], value)
    return value


def section_kernel(column_ref, offsets_ref, model_ref, out_hbm, table_ref, pc_ref, ps_ref, re_ref, im_ref, out_ref, sem):
    part = pl.program_id(0)
    highs = HIGH1 // PARTS1

    @pl.when(part == 0)
    def _():
        column_start = column_ref[0]
        pixel_start = offsets_ref[1, lax.axis_index("facet")]
        freq = column_start + iota((STEP1, SGW), 1)
        c, s = phase(freq, iota((STEP1, SGW), 0))
        table_ref[:, :SGW] = c.astype(BF)
        table_ref[:, SGW:] = (-s).astype(BF)
        freq = column_start + iota((HIGH1, SGW), 1)
        c, s = phase(freq, pixel_start + STEP1 * iota((HIGH1, SGW), 0))
        pc_ref[...] = c
        ps_ref[...] = s
        re_ref[...] = jnp.zeros((FROWS, SGW), F32)
        im_ref[...] = jnp.zeros((FROWS, SGW), F32)

    acc_re = re_ref[...]
    acc_im = im_ref[...]
    for high in range(highs):
        block = model_ref[:, high * STEP1 : (high + 1) * STEP1].astype(BF)
        product = jnp.dot(block, table_ref[...], preferred_element_type=F32)
        re = product[:, :SGW]
        im = product[:, SGW:]
        pc = pc_ref[pl.ds(part * highs + high, 1), :]
        ps = ps_ref[pl.ds(part * highs + high, 1), :]
        acc_re = acc_re + (re * pc + im * ps)
        acc_im = acc_im + (im * pc - re * ps)
    re_ref[...] = acc_re
    im_ref[...] = acc_im

    @pl.when(part == PARTS1 - 1)
    def _():
        re = re_ref[...].T.astype(BF)
        im = im_ref[...].T.astype(BF)
        out_ref[:, :SLICE, :] = re.reshape(FACETS, SLICE, FROWS)
        out_ref[:, SLICE:, :] = im.reshape(FACETS, SLICE, FROWS)
        write_out([(out_ref, out_hbm, sem)])


def section(column_start, offsets, model):
    return pl.pallas_call(
        section_kernel,
        grid=(PARTS1,),
        out_shape=jax.ShapeDtypeStruct((FACETS, 2 * SLICE, FROWS), BF),
        in_specs=[SMEM_SPEC, SMEM_SPEC, pl.BlockSpec((FROWS, FW // PARTS1), lambda i: (0, i))],
        out_specs=HBM_SPEC,
        scratch_shapes=[
            pltpu.VMEM((STEP1, 2 * SGW), BF),
            pltpu.VMEM((HIGH1, SGW), F32),
            pltpu.VMEM((HIGH1, SGW), F32),
            pltpu.VMEM((FROWS, SGW), F32),
            pltpu.VMEM((FROWS, SGW), F32),
            pltpu.VMEM((FACETS, 2 * SLICE, FROWS), BF),
            pltpu.SemaphoreType.DMA,
        ],
        compiler_params=PARAMS,
        name="section",
    )(column_start, offsets, off_chip(model))


def row_table_kernel(offsets_ref, rows_ref, table_ref, c_ref, s_ref, base_ref, turn_ref):
    c, s = phase(iota((FROWS, SGW), 1), iota((FROWS, SGW), 0))
    base_ref[0] = c
    base_ref[1] = s
    row = iota((FACETS, SGW), 0)
    start = jnp.zeros((FACETS, SGW), I32)
    for f in range(FACETS):
        start = jnp.where(row == f, offsets_ref[0, f], start)
    c, s = phase(iota((FACETS, SGW), 1), start)
    turn_ref[0] = c
    turn_ref[1] = s
    row = iota((NROWSG, FROWS), 0)
    freq = jnp.zeros((NROWSG, FROWS), I32)
    for r in range(NROWSG):
        freq = jnp.where(row == r, rows_ref[0, r], freq)

    def one(f, carry):
        cf = turn_ref[0, pl.ds(f, 1), :]
        sf = turn_ref[1, pl.ds(f, 1), :]
        c = (base_ref[0] * cf - base_ref[1] * sf).astype(BF)
        s = (base_ref[1] * cf + base_ref[0] * sf).astype(BF)
        top = pl.ds(pl.multiple_of(f * 2 * FROWS, 2 * FROWS), FROWS)
        low = pl.ds(pl.multiple_of(f * 2 * FROWS + FROWS, FROWS), FROWS)
        table_ref[top, :SGW] = c
        table_ref[top, SGW:] = -s
        table_ref[low, :SGW] = s
        table_ref[low, SGW:] = c
        c, s = phase(freq, offsets_ref[0, f] + iota((NROWSG, FROWS), 1))
        c_ref[f] = c
        s_ref[f] = s
        return carry

    lax.fori_loop(0, FACETS, one, 0)


def row_tables(offsets, rows):
    return pl.pallas_call(
        row_table_kernel,
        out_shape=(
            pltpu.VMEM((FACETS * 2 * FROWS, 2 * SGW), BF),
            pltpu.VMEM((FACETS, NROWSG, FROWS), F32),
            pltpu.VMEM((FACETS, NROWSG, FROWS), F32),
        ),
        in_specs=[SMEM_SPEC, SMEM_SPEC],
        out_specs=(VMEM_SPEC, VMEM_SPEC, VMEM_SPEC),
        scratch_shapes=[
            pltpu.VMEM((2, FROWS, SGW), F32),
            pltpu.VMEM((2, FACETS, SGW), F32),
        ],
        compiler_params=PARAMS,
        name="row_tables",
    )(offsets, rows)


def grid_kernel(in_ref, c_ref, s_ref, table_ref, out_hbm, turned_ref, out_ref, sem):
    for f in range(FACETS):
        re = in_ref[f, :SLICE, :].astype(F32)
        im = in_ref[f, SLICE:, :].astype(F32)
        left = f * 2 * FROWS
        for r in range(NROWSG):
            c = c_ref[f, r : r + 1, :]
            s = s_ref[f, r : r + 1, :]
            lines = slice(r * SLICE, (r + 1) * SLICE)
            turned_ref[lines, left : left + FROWS] = (re * c + im * s).astype(BF)
            turned_ref[lines, left + FROWS : left + 2 * FROWS] = (im * c - re * s).astype(BF)
    product = jnp.dot(turned_ref[...], table_ref[...], preferred_element_type=F32)
    total = (NORM * product).astype(BF)
    out_ref[:, :SLICE, :] = total[:, :SGW].reshape(NROWSG, SLICE, SGW)
    out_ref[:, SLICE:, :] = total[:, SGW:].reshape(NROWSG, SLICE, SGW)
    write_out([(out_ref, out_hbm, sem)])


def grids(sections, tables):
    table, c, s = tables
    return pl.pallas_call(
        grid_kernel,
        out_shape=jax.ShapeDtypeStruct((NROWSG, 2 * SLICE, SGW), BF),
        in_specs=[VMEM_SPEC] * 4,
        out_specs=HBM_SPEC,
        scratch_shapes=[
            pltpu.VMEM((NROWSG * SLICE, FACETS * 2 * FROWS), BF),
            pltpu.VMEM((NROWSG, 2 * SLICE, SGW), BF),
            pltpu.SemaphoreType.DMA,
        ],
        compiler_params=PARAMS,
        name="grids",
    )(on_chip(sections), on_chip(c), on_chip(s), on_chip(table))


def adjoint_kernel(in_ref, c_ref, s_ref, table_ref, out_hbm, lines_ref, out_ref, sems):
    lines_ref[:, :SGW] = in_ref[:, :SLICE, :].reshape(NROWSG * SLICE, SGW)
    lines_ref[:, SGW:] = in_ref[:, SLICE:, :].reshape(NROWSG * SLICE, SGW)

    def one(f, carry):
        table = table_ref[pl.ds(pl.multiple_of(f * 2 * FROWS, 2 * FROWS), 2 * FROWS), :]
        product = lax.dot_general(
            lines_ref[...], table, (((1,), (1,)), ((), ())), preferred_element_type=F32
        )
        acc_re = jnp.zeros((SLICE, FROWS), F32)
        acc_im = jnp.zeros((SLICE, FROWS), F32)
        for r in range(NROWSG):
            re = product[r * SLICE : (r + 1) * SLICE, :FROWS]
            im = product[r * SLICE : (r + 1) * SLICE, FROWS:]
            c = c_ref[f, r : r + 1, :]
            s = s_ref[f, r : r + 1, :]
            acc_re = acc_re + (re * c - im * s)
            acc_im = acc_im + (im * c + re * s)
        out_ref[f] = jnp.concatenate([acc_re, acc_im], axis=1).astype(BF)
        return carry

    lax.fori_loop(0, FACETS, one, 0, unroll=UNROLL4)
    write_out([(out_ref, out_hbm.at[:, copy], sems.at[copy]) for copy in range(NCOL)])


def adjoint(gridded, tables):
    table, c, s = tables
    return pl.pallas_call(
        adjoint_kernel,
        out_shape=jax.ShapeDtypeStruct((FACETS, NCOL, SLICE, 2 * FROWS), BF),
        in_specs=[VMEM_SPEC] * 4,
        out_specs=HBM_SPEC,
        scratch_shapes=[
            pltpu.VMEM((NROWSG * SLICE, 2 * SGW), BF),
            pltpu.VMEM((FACETS, SLICE, 2 * FROWS), BF),
            pltpu.SemaphoreType.DMA((NCOL,)),
        ],
        compiler_params=PARAMS,
        name="adjoint",
    )(on_chip(gridded), on_chip(c), on_chip(s), on_chip(table))


def kernel_columns(position):
    cells = iota((SGW, position.shape[1]), 0) * OS + OS // 2
    offset = cells - position
    distance = offset.astype(F32) * (1.0 / OS)
    inside = jnp.abs(offset) <= KSUP * OS
    return jnp.where(inside, jnp.exp(-0.5 * distance * distance), 0.0).astype(BF)


def vis_table_kernel(uv_ref, ku_ref, kv_ref):
    def one(part, carry):
        cut = pl.ds(pl.multiple_of(part * 256, 256), 256)
        ku_ref[:, cut] = kernel_columns(uv_ref[0:1, cut])
        kv_ref[:, cut] = kernel_columns(uv_ref[1:2, cut])
        return carry

    lax.fori_loop(0, VCAP // 256, one, 0)


def vis_tables(uv):
    shape = pltpu.VMEM((SGW, VCAP), BF)
    return pl.pallas_call(
        vis_table_kernel,
        out_shape=(shape, shape),
        in_specs=[VMEM_SPEC],
        out_specs=(VMEM_SPEC, VMEM_SPEC),
        compiler_params=PARAMS,
        name="vis_tables",
    )(uv)


def visibility_kernel(counts_ref, obs_ref, weight_ref, in_ref, ku_ref, kv_ref, gridded_hbm, res_ref, acc_ref, gridded_ref, sem):
    count = counts_ref[0, lax.axis_index("facet")]
    grid = [in_ref[:, half * SLICE : (half + 1) * SLICE, :].reshape(SGW, SGW) for half in range(2)]
    for part in range(VCAP // VBLOCK):
        cut = slice(part * VBLOCK, (part + 1) * VBLOCK)
        live = part * VBLOCK + iota((1, VBLOCK), 1) < count
        weight = weight_ref[:, cut].astype(F32)
        for half in range(2):
            sampled = jnp.dot(grid[half], ku_ref[:, cut], preferred_element_type=F32)
            predicted = jnp.sum(sampled * kv_ref[:, cut].astype(F32), axis=0, keepdims=True)
            observed = obs_ref[half : half + 1, cut].astype(F32)
            residual = jnp.where(live, weight * (observed - predicted), 0.0)
            res_ref[half : half + 1, cut] = residual
            weighted = (residual * kv_ref[:, cut].astype(F32)).astype(BF)
            total = lax.dot_general(
                weighted, ku_ref[:, cut], (((1,), (1,)), ((), ())), preferred_element_type=F32
            )
            if part:
                total = total + acc_ref[half]
            if part + 1 < VCAP // VBLOCK:
                acc_ref[half] = total
            else:
                lines = total.astype(BF).reshape(FACETS, SLICE, SGW)
                gridded_ref[:, half * SLICE : (half + 1) * SLICE, :] = lines
    write_out([(gridded_ref, gridded_hbm, sem)])


def visibilities(counts, obs, weight, grid, tables):
    return pl.pallas_call(
        visibility_kernel,
        out_shape=(
            jax.ShapeDtypeStruct((FACETS, 2 * SLICE, SGW), BF),
            jax.ShapeDtypeStruct((2, VCAP), F32),
        ),
        in_specs=[SMEM_SPEC] + [VMEM_SPEC] * 5,
        out_specs=(HBM_SPEC, VMEM_SPEC),
        scratch_shapes=[
            pltpu.VMEM((2, SGW, SGW), F32),
            pltpu.VMEM((FACETS, 2 * SLICE, SGW), BF),
            pltpu.SemaphoreType.DMA,
        ],
        compiler_params=PARAMS,
        name="visibilities",
    )(counts, obs, weight, on_chip(grid), *map(on_chip, tables))


def dirichlet(distance, pixel_start):
    distance = ((distance & (NIMG - 1)) ^ (NIMG // 2)) - NIMG // 2
    top = cos_sin((distance * (NIMG // (NIMG // FW * 2))) & (NIMG - 1))[1]
    bottom = cos_sin(distance, 17)[1]
    ratio = jnp.where(distance == 0, float(FW), top / jnp.where(distance == 0, 1.0, bottom))
    c, s = cos_sin((distance * (2 * pixel_start + FW - 1)) & (2 * NIMG - 1), 17)
    return c * ratio, s * ratio


def gram_kernel(step_ref, starts_ref, column_ref, offsets_ref, adj_ref, first_ref, out_hbm, flip_ref, v_ref, out_ref, sem):
    wide = 2 * SGW
    pixel_start = offsets_ref[1, lax.axis_index("facet")]
    own = column_ref[0]
    row = iota((NCOL, wide), 0)
    starts = jnp.zeros((NCOL, wide), I32)
    for c in range(NCOL):
        starts = jnp.where(row == c, starts_ref[c], starts)
    lane = iota((NCOL, wide), 1)
    v_ref[0], v_ref[1] = dirichlet(starts - own + (lane - (SGW - 1)), pixel_start)
    v_ref[2], v_ref[3] = dirichlet(starts + own + (2 * (SGW - 1) - lane), pixel_start)
    anti = (iota((SGW, SGW), 0) + iota((SGW, SGW), 1)) == SGW - 1
    flip_ref[...] = jnp.where(anti, 1.0, 0.0).astype(BF)
    totals = [None] * 4
    for c in range(NCOL):
        lines = adj_ref[:, c].reshape(SGW, 2 * FROWS)
        turned = jnp.dot(flip_ref[...], lines, preferred_element_type=F32).astype(BF)
        for k in range(4):
            spread = jnp.broadcast_to(v_ref[k, c : c + 1, :], (SGW, wide))
            band = pltpu.roll(spread, SGW + 1, 1, stride=1, stride_axis=0)[:, :SGW].astype(BF)
            term = jnp.dot(band, lines if k < 2 else turned, preferred_element_type=F32)
            totals[k] = term if c == 0 else totals[k] + term
    scale = step_ref[0] * (0.5 * NORM)
    p1, p2, p3, p4 = totals
    re = p1[:, :FROWS] - p2[:, FROWS:] + p3[:, :FROWS] - p4[:, FROWS:]
    im = p2[:, :FROWS] + p1[:, FROWS:] - p4[:, :FROWS] - p3[:, FROWS:]
    first = first_ref[...].astype(F32)
    out_ref[:, :SLICE, :] = (first[:, :SLICE] + (scale * re).reshape(FACETS, SLICE, FROWS)).astype(BF)
    out_ref[:, SLICE:, :] = (first[:, SLICE:] + (scale * im).reshape(FACETS, SLICE, FROWS)).astype(BF)
    write_out([(out_ref, out_hbm, sem)])


def gram(steps, column_starts, column_start, offsets, adj, first):
    return pl.pallas_call(
        gram_kernel,
        out_shape=jax.ShapeDtypeStruct((FACETS, 2 * SLICE, FROWS), BF),
        in_specs=[SMEM_SPEC] * 4 + [VMEM_SPEC] * 2,
        out_specs=HBM_SPEC,
        scratch_shapes=[
            pltpu.VMEM((SGW, SGW), BF),
            pltpu.VMEM((4, NCOL, 2 * SGW), F32),
            pltpu.VMEM((FACETS, 2 * SLICE, FROWS), BF),
            pltpu.SemaphoreType.DMA,
        ],
        compiler_params=PARAMS,
        name="gram",
    )(steps, column_starts, column_start, offsets, on_chip(adj.reshape(FACETS, NCOL, SLICE, 2 * FROWS)), first)


def update_kernel(step_ref, adj0_ref, adj1_ref, table_ref, pc_ref, ps_ref, model_ref, out_ref, both_ref, even_ref, odd_ref):
    part = pl.program_id(0)

    def turn(pair, target_ref):
        re = both_ref[:FROWS, :]
        im = both_ref[FROWS:, :]
        for p in range(PAIR5):
            pc = pc_ref[pl.ds(pair * PAIR5 + p, 1), :]
            ps = ps_ref[pl.ds(pair * PAIR5 + p, 1), :]
            lines = slice(p * FROWS, (p + 1) * FROWS)
            target_ref[lines, :COLUMNS] = (re * pc - im * ps).astype(BF)
            target_ref[lines, COLUMNS:] = (im * pc + re * ps).astype(BF)

    def add(place, source_ref):
        gradient = jnp.dot(source_ref[...], table_ref[...], preferred_element_type=F32)
        for p in range(PAIR5):
            left = (place * PAIR5 + p) * STEP5
            lines = gradient[p * FROWS : (p + 1) * FROWS]
            out_ref[:, left : left + STEP5] = model_ref[:, left : left + STEP5] + lines

    @pl.when(part == 0)
    def _():
        first = step_ref[0] * NORM
        second = step_ref[1] * NORM
        for j in range(FACETS):
            lines0 = adj0_ref[j * NCOL : (j + 1) * NCOL].reshape(NCOL * SLICE, 2 * FROWS).astype(F32)
            lines1 = adj1_ref[j * NCOL : (j + 1) * NCOL].reshape(NCOL * SLICE, 2 * FROWS).astype(F32)
            both = first * lines0 + second * lines1
            both_ref[:, j * NCOL * SLICE : (j + 1) * NCOL * SLICE] = both.T
        turn(0, even_ref)

    turn(2 * part + 1, odd_ref)
    add(0, even_ref)
    turn(jnp.minimum(2 * part + 2, HIGH5 // PAIR5 - 2), even_ref)
    add(1, odd_ref)


def update(steps, adj0, adj1, tables, model):
    wide = pl.BlockSpec((FROWS, 2 * PAIR5 * STEP5), lambda i: (0, i))
    return pl.pallas_call(
        update_kernel,
        grid=(HIGH5 // PAIR5 // 2,),
        out_shape=jax.ShapeDtypeStruct((FROWS, FW), F32),
        in_specs=[SMEM_SPEC] + [VMEM_SPEC] * 5 + [wide],
        out_specs=wide,
        scratch_shapes=[
            pltpu.VMEM((2 * FROWS, COLUMNS), F32),
            pltpu.VMEM((PAIR5 * FROWS, 2 * COLUMNS), BF),
            pltpu.VMEM((PAIR5 * FROWS, 2 * COLUMNS), BF),
        ],
        compiler_params=WIDE_PARAMS,
        name="update",
    )(steps, on_chip(adj0), on_chip(adj1), *map(on_chip, tables), off_chip(model))


def update_table_kernel(starts_ref, offsets_ref, table_ref, pc_ref, ps_ref, base_ref, turn_ref):
    group = NCOL * SLICE
    line = iota((group, STEP5), 0)
    freq = line & (SLICE - 1)
    for c in range(NCOL):
        freq = freq + jnp.where((line >> 4) == c, starts_ref[c], 0)
    base_ref[0], base_ref[1] = phase(freq, iota((group, STEP5), 1))
    turn_ref[0], turn_ref[1] = phase(SLICE * iota((FACETS, STEP5), 0), iota((FACETS, STEP5), 1))

    def one(j, carry):
        c = turn_ref[0, pl.ds(j, 1), :]
        s = turn_ref[1, pl.ds(j, 1), :]
        cut = pl.ds(pl.multiple_of(j * group, group), group)
        table_ref[cut, :] = (base_ref[0] * c - base_ref[1] * s).astype(BF)
        cut = pl.ds(pl.multiple_of(COLUMNS + j * group, group), group)
        table_ref[cut, :] = (-(base_ref[1] * c + base_ref[0] * s)).astype(BF)
        return carry

    lax.fori_loop(0, FACETS, one, 0)
    lane = iota((HIGH5, COLUMNS), 1)
    freq = SLICE * (lane >> 7) + (lane & (SLICE - 1))
    for c in range(NCOL):
        freq = freq + jnp.where(((lane >> 4) & (NCOL - 1)) == c, starts_ref[c], 0)
    pixel_start = offsets_ref[1, lax.axis_index("facet")]
    pc_ref[...], ps_ref[...] = phase(freq, pixel_start + STEP5 * iota((HIGH5, COLUMNS), 0))


def update_tables(column_starts, offsets):
    return pl.pallas_call(
        update_table_kernel,
        out_shape=(
            pltpu.VMEM((2 * COLUMNS, STEP5), BF),
            pltpu.VMEM((HIGH5, COLUMNS), F32),
            pltpu.VMEM((HIGH5, COLUMNS), F32),
        ),
        in_specs=[SMEM_SPEC, SMEM_SPEC],
        out_specs=(VMEM_SPEC, VMEM_SPEC, VMEM_SPEC),
        scratch_shapes=[
            pltpu.VMEM((2, NCOL * SLICE, STEP5), F32),
            pltpu.VMEM((2, FACETS, STEP5), F32),
        ],
        compiler_params=PARAMS,
        name="update_tables",
    )(column_starts, offsets)


def exchange(value):
    return lax.all_to_all(value, "facet", split_axis=0, concat_axis=0, tiled=True)


def to_facets(value):
    copies = value.reshape(FACETS * NCOL, *value.shape[2:])
    return lax.all_to_all(copies, ("facet", "sub"), split_axis=0, concat_axis=0, tiled=True)


def local(
    model_image,
    step_sizes,
    facet_offsets,
    col_offsets,
    row_offsets,
    counts,
    vis_uv,
    vis_obs,
    vis_weight,
):
    lines = lax.optimization_barrier(jnp.broadcast_to(col_offsets[:, None], (8, 128)))
    column_starts = lax.optimization_barrier(lax.all_gather(lines, "sub", axis=0, tiled=True))[::8, 0]
    uv = vis_uv.reshape(2, VCAP)
    obs = vis_obs.reshape(2, VCAP)
    weight = vis_weight.reshape(1, VCAP)
    model = model_image[0]
    first = section(col_offsets, facet_offsets, model)
    rows = row_tables(facet_offsets, row_offsets)
    kernels = vis_tables(uv)
    grid = exchange(grids(exchange(first), rows))
    gridded, residual = visibilities(counts, obs, weight, grid, kernels)
    adj0 = to_facets(adjoint(exchange(gridded), rows))
    tables = update_tables(column_starts, facet_offsets)
    second = gram(step_sizes, column_starts, col_offsets, facet_offsets, adj0, first)
    grid = exchange(grids(exchange(second), rows))
    gridded, residual = visibilities(counts, obs, weight, grid, kernels)
    adj1 = to_facets(adjoint(exchange(gridded), rows))
    model = update(step_sizes, adj0, adj1, tables, model)
    return model[None], residual.reshape(2, 1, 1, VCAP)


def solution(mesh):
    in_specs = (
        P("facet", None, None),
        P(),
        P(),
        P("sub"),
        P("sub", None),
        P("sub", None),
        P(None, "sub", "facet", None),
        P(None, "sub", "facet", None),
        P("sub", "facet", None),
    )
    out_specs = (P("facet", None, None), P(None, "sub", "facet", None))
    return jax.shard_map(local, mesh=mesh, in_specs=in_specs, out_specs=out_specs, check_vma=False)
```

```python
import math

import jax
import jax.numpy as jnp
from jax import lax
from jax.experimental import pallas as pl
from jax.experimental.pallas import tpu as pltpu
from jax.sharding import PartitionSpec as P

NIMG = 65536
FW = 8192
FROWS = 128
SGW = 256
VCAP = 4096
OS = 8
KSUP = 4
FACETS = 16
NCOL = 8
NROWSG = 16
SLICE = SGW // FACETS
COLUMNS = NCOL * SGW

STEP1 = 256
HIGH1 = FW // STEP1
PARTS1 = 4
STEP5 = 512
HIGH5 = FW // STEP5
PAIR5 = 2
VBLOCK = 1024
CHUNK = 4
UNROLL4 = 8

BF = jnp.bfloat16
F32 = jnp.float32
I32 = jnp.int32
NORM = 1.0 / math.sqrt(FACETS * FROWS * FW)
PARAMS = pltpu.CompilerParams(vmem_limit_bytes=16 << 20)
WIDE_PARAMS = pltpu.CompilerParams(vmem_limit_bytes=24 << 20)
SMEM_SPEC = pl.BlockSpec(memory_space=pltpu.SMEM)
VMEM_SPEC = pl.BlockSpec(memory_space=pltpu.VMEM)
HBM_SPEC = pl.BlockSpec(memory_space=pltpu.HBM)


def cos_sin(index, bits=16):
    quadrant = (index + (1 << (bits - 3))) >> (bits - 2)
    angle = (index - (quadrant << (bits - 2))).astype(F32) * (2.0 * math.pi / (1 << bits))
    square = angle * angle
    sine = angle * (1.0 + square * (-1.0 / 6 + square * (1.0 / 120 + square * (-1.0 / 5040 + square / 362880))))
    cosine = 1.0 + square * (-0.5 + square * (1.0 / 24 + square * (-1.0 / 720 + square / 40320)))
    swapped = (quadrant & 1) != 0
    c = jnp.where(swapped, sine, cosine)
    s = jnp.where(swapped, cosine, sine)
    c = jnp.where(((quadrant + 1) & 2) != 0, -c, c)
    s = jnp.where((quadrant & 2) != 0, -s, s)
    return c, s


def phase(frequency, pixel):
    return cos_sin((frequency * pixel) & (NIMG - 1))


def on_chip(value):
    return pltpu.with_memory_space_constraint(value, pltpu.VMEM)


def off_chip(value):
    return pltpu.with_memory_space_constraint(value, pltpu.HBM)


def write_out(pairs):
    copies = [pltpu.make_async_copy(source, target, sem) for source, target, sem in pairs]
    for copy in copies:
        copy.start()
    for copy in copies:
        copy.wait()


def iota(shape, dim):
    return lax.broadcasted_iota(I32, shape, dim)


def column_of(ref, count, lanes):
    row = iota((count, lanes), 0)
    value = jnp.zeros((count, lanes), I32)
    for i in range(count):
        value = jnp.where(row == i, ref[i], value)
    return value


def section_kernel(column_ref, offsets_ref, model_hbm, out_hbm, model_ref, table_ref, pc_ref, ps_ref, out_ref, sems, sem):
    wide = FW // PARTS1
    fetches = []
    for part in range(PARTS1):
        cut = pl.ds(part * wide, wide)
        fetches.append(pltpu.make_async_copy(model_hbm.at[:, cut], model_ref.at[:, cut], sems.at[part]))
        fetches[-1].start()
    column_start = column_ref[0]
    pixel_start = offsets_ref[1, lax.axis_index("facet")]
    freq = column_start + iota((STEP1, SGW), 1)
    c, s = phase(freq, iota((STEP1, SGW), 0))
    table_ref[:, :SGW] = c.astype(BF)
    table_ref[:, SGW:] = (-s).astype(BF)
    freq = column_start + iota((HIGH1, SGW), 1)
    pc_ref[...], ps_ref[...] = phase(freq, pixel_start + STEP1 * iota((HIGH1, SGW), 0))
    acc_re = jnp.zeros((FROWS, SGW), F32)
    acc_im = jnp.zeros((FROWS, SGW), F32)
    for high in range(HIGH1):
        if high % (HIGH1 // PARTS1) == 0:
            fetches[high // (HIGH1 // PARTS1)].wait()
        block = model_ref[:, high * STEP1 : (high + 1) * STEP1].astype(BF)
        product = jnp.dot(block, table_ref[...], preferred_element_type=F32)
        re = product[:, :SGW]
        im = product[:, SGW:]
        pc = pc_ref[high : high + 1, :]
        ps = ps_ref[high : high + 1, :]
        acc_re = acc_re + (re * pc + im * ps)
        acc_im = acc_im + (im * pc - re * ps)
    out_ref[:, :SLICE, :] = acc_re.T.astype(BF).reshape(FACETS, SLICE, FROWS)
    out_ref[:, SLICE:, :] = acc_im.T.astype(BF).reshape(FACETS, SLICE, FROWS)
    write_out([(out_ref, out_hbm, sem)])


def section(column_start, offsets, model):
    return pl.pallas_call(
        section_kernel,
        out_shape=jax.ShapeDtypeStruct((FACETS, 2 * SLICE, FROWS), BF),
        in_specs=[SMEM_SPEC, SMEM_SPEC, HBM_SPEC],
        out_specs=HBM_SPEC,
        scratch_shapes=[
            pltpu.VMEM((FROWS, FW), F32),
            pltpu.VMEM((STEP1, 2 * SGW), BF),
            pltpu.VMEM((HIGH1, SGW), F32),
            pltpu.VMEM((HIGH1, SGW), F32),
            pltpu.VMEM((FACETS, 2 * SLICE, FROWS), BF),
            pltpu.SemaphoreType.DMA((PARTS1,)),
            pltpu.SemaphoreType.DMA,
        ],
        compiler_params=PARAMS,
        name="section",
    )(column_start, offsets, off_chip(model))


def kernel_columns(position):
    cells = iota((SGW, position.shape[1]), 0) * OS + OS // 2
    offset = cells - position
    distance = offset.astype(F32) * (1.0 / OS)
    inside = jnp.abs(offset) <= KSUP * OS
    return jnp.where(inside, jnp.exp(-0.5 * distance * distance), 0.0).astype(BF)


def table_kernel(offsets_ref, rows_ref, uv_ref, table_ref, c_ref, s_ref, ku_ref, kv_ref, base_ref, turn_ref):
    base_ref[0], base_ref[1] = phase(iota((FROWS, SGW), 1), iota((FROWS, SGW), 0))
    row = iota((FACETS, SGW), 0)
    start = jnp.zeros((FACETS, SGW), I32)
    for f in range(FACETS):
        start = jnp.where(row == f, offsets_ref[0, f], start)
    turn_ref[0], turn_ref[1] = phase(iota((FACETS, SGW), 1), start)
    row = iota((NROWSG, FROWS), 0)
    freq = jnp.zeros((NROWSG, FROWS), I32)
    for r in range(NROWSG):
        freq = jnp.where(row == r, rows_ref[0, r], freq)

    def one(f, carry):
        cf = turn_ref[0, pl.ds(f, 1), :]
        sf = turn_ref[1, pl.ds(f, 1), :]
        lines = pl.ds(pl.multiple_of(f * FROWS, FROWS), FROWS)
        table_ref[0, lines, :] = (base_ref[0] * cf - base_ref[1] * sf).astype(BF)
        table_ref[1, lines, :] = (base_ref[1] * cf + base_ref[0] * sf).astype(BF)
        c_ref[f], s_ref[f] = phase(freq, offsets_ref[0, f] + iota((NROWSG, FROWS), 1))
        cut = pl.ds(pl.multiple_of(f * SGW, SGW), SGW)
        ku_ref[:, cut] = kernel_columns(uv_ref[0:1, cut])
        kv_ref[:, cut] = kernel_columns(uv_ref[1:2, cut])
        return carry

    lax.fori_loop(0, FACETS, one, 0)


def cycle_tables(offsets, rows, uv):
    return pl.pallas_call(
        table_kernel,
        out_shape=(
            pltpu.VMEM((2, FACETS * FROWS, SGW), BF),
            pltpu.VMEM((FACETS, NROWSG, FROWS), F32),
            pltpu.VMEM((FACETS, NROWSG, FROWS), F32),
            pltpu.VMEM((SGW, VCAP), BF),
            pltpu.VMEM((SGW, VCAP), BF),
        ),
        in_specs=[SMEM_SPEC, SMEM_SPEC, VMEM_SPEC],
        out_specs=(VMEM_SPEC,) * 5,
        scratch_shapes=[
            pltpu.VMEM((2, FROWS, SGW), F32),
            pltpu.VMEM((2, FACETS, SGW), F32),
        ],
        compiler_params=PARAMS,
        name="cycle_tables",
    )(offsets, rows, uv)


def grid_kernel(in_ref, c_ref, s_ref, table_ref, out_hbm, turned_ref, out_ref, sem):
    half = NROWSG * SLICE
    for f in range(FACETS):
        re = in_ref[f, :SLICE, :].astype(F32)
        im = in_ref[f, SLICE:, :].astype(F32)
        cut = slice(f * FROWS, (f + 1) * FROWS)
        for r in range(NROWSG):
            c = c_ref[f, r : r + 1, :]
            s = s_ref[f, r : r + 1, :]
            turned_ref[r * SLICE : (r + 1) * SLICE, cut] = (re * c + im * s).astype(BF)
            turned_ref[half + r * SLICE : half + (r + 1) * SLICE, cut] = (im * c - re * s).astype(BF)
    by_c = jnp.dot(turned_ref[...], table_ref[0], preferred_element_type=F32)
    by_s = jnp.dot(turned_ref[...], table_ref[1], preferred_element_type=F32)
    re = (NORM * (by_c[:half] + by_s[half:])).astype(BF)
    im = (NORM * (by_c[half:] - by_s[:half])).astype(BF)
    out_ref[:, :SLICE, :] = re.reshape(NROWSG, SLICE, SGW)
    out_ref[:, SLICE:, :] = im.reshape(NROWSG, SLICE, SGW)
    write_out([(out_ref, out_hbm, sem)])


def grids(sections, tables):
    table, c, s = tables
    return pl.pallas_call(
        grid_kernel,
        out_shape=jax.ShapeDtypeStruct((NROWSG, 2 * SLICE, SGW), BF),
        in_specs=[VMEM_SPEC] * 4,
        out_specs=HBM_SPEC,
        scratch_shapes=[
            pltpu.VMEM((2 * NROWSG * SLICE, FACETS * FROWS), BF),
            pltpu.VMEM((NROWSG, 2 * SLICE, SGW), BF),
            pltpu.SemaphoreType.DMA,
        ],
        compiler_params=PARAMS,
        name="grids",
    )(on_chip(sections), on_chip(c), on_chip(s), on_chip(table))


def adjoint_kernel(in_ref, c_ref, s_ref, table_ref, out_hbm, lines_ref, out_ref, sems):
    half = NROWSG * SLICE
    lines_ref[:half] = in_ref[:, :SLICE, :].reshape(half, SGW)
    lines_ref[half:] = in_ref[:, SLICE:, :].reshape(half, SGW)

    def one(pair, carry):
        cut = pl.ds(pl.multiple_of(pair * 2 * FROWS, 2 * FROWS), 2 * FROWS)
        dims = (((1,), (1,)), ((), ()))
        by_c = lax.dot_general(lines_ref[...], table_ref[0, cut, :], dims, preferred_element_type=F32)
        by_s = lax.dot_general(lines_ref[...], table_ref[1, cut, :], dims, preferred_element_type=F32)
        for k in range(2):
            f = 2 * pair + k
            lanes = slice(k * FROWS, (k + 1) * FROWS)
            acc_re = jnp.zeros((SLICE, FROWS), F32)
            acc_im = jnp.zeros((SLICE, FROWS), F32)
            for r in range(NROWSG):
                top = slice(r * SLICE, (r + 1) * SLICE)
                low = slice(half + r * SLICE, half + (r + 1) * SLICE)
                re = by_c[top, lanes] - by_s[low, lanes]
                im = by_c[low, lanes] + by_s[top, lanes]
                c = c_ref[f, r : r + 1, :]
                s = s_ref[f, r : r + 1, :]
                acc_re = acc_re + (re * c - im * s)
                acc_im = acc_im + (im * c + re * s)
            out_ref[f] = jnp.concatenate([acc_re, acc_im], axis=1).astype(BF)
        return carry

    lax.fori_loop(0, FACETS // 2, one, 0, unroll=UNROLL4)
    write_out([(out_ref, out_hbm.at[:, copy], sems.at[copy]) for copy in range(NCOL)])


def adjoint(gridded, tables):
    table, c, s = tables
    return pl.pallas_call(
        adjoint_kernel,
        out_shape=jax.ShapeDtypeStruct((FACETS, NCOL, SLICE, 2 * FROWS), BF),
        in_specs=[VMEM_SPEC] * 4,
        out_specs=HBM_SPEC,
        scratch_shapes=[
            pltpu.VMEM((2 * NROWSG * SLICE, SGW), BF),
            pltpu.VMEM((FACETS, SLICE, 2 * FROWS), BF),
            pltpu.SemaphoreType.DMA((NCOL,)),
        ],
        compiler_params=PARAMS,
        name="adjoint",
    )(on_chip(gridded), on_chip(c), on_chip(s), on_chip(table))


def visibility_kernel(counts_ref, obs_ref, weight_ref, in_ref, ku_ref, kv_ref, gridded_hbm, res_ref, acc_ref, gridded_ref, sem):
    count = counts_ref[0, lax.axis_index("facet")]
    grid = [in_ref[:, half * SLICE : (half + 1) * SLICE, :].reshape(SGW, SGW) for half in range(2)]
    for part in range(VCAP // VBLOCK):
        cut = slice(part * VBLOCK, (part + 1) * VBLOCK)
        live = part * VBLOCK + iota((1, VBLOCK), 1) < count
        weight = weight_ref[:, cut].astype(F32)
        for half in range(2):
            sampled = jnp.dot(grid[half], ku_ref[:, cut], preferred_element_type=F32)
            predicted = jnp.sum(sampled * kv_ref[:, cut].astype(F32), axis=0, keepdims=True)
            observed = obs_ref[half : half + 1, cut].astype(F32)
            residual = jnp.where(live, weight * (observed - predicted), 0.0)
            res_ref[half : half + 1, cut] = residual
            weighted = (residual * kv_ref[:, cut].astype(F32)).astype(BF)
            total = lax.dot_general(
                weighted, ku_ref[:, cut], (((1,), (1,)), ((), ())), preferred_element_type=F32
            )
            if part:
                total = total + acc_ref[half]
            if part + 1 < VCAP // VBLOCK:
                acc_ref[half] = total
            else:
                lines = total.astype(BF).reshape(FACETS, SLICE, SGW)
                gridded_ref[:, half * SLICE : (half + 1) * SLICE, :] = lines
    write_out([(gridded_ref, gridded_hbm, sem)])


def visibilities(counts, obs, weight, grid, tables):
    return pl.pallas_call(
        visibility_kernel,
        out_shape=(
            jax.ShapeDtypeStruct((FACETS, 2 * SLICE, SGW), BF),
            jax.ShapeDtypeStruct((2, VCAP), F32),
        ),
        in_specs=[SMEM_SPEC] + [VMEM_SPEC] * 5,
        out_specs=(HBM_SPEC, VMEM_SPEC),
        scratch_shapes=[
            pltpu.VMEM((2, SGW, SGW), F32),
            pltpu.VMEM((FACETS, 2 * SLICE, SGW), BF),
            pltpu.SemaphoreType.DMA,
        ],
        compiler_params=PARAMS,
        name="visibilities",
    )(counts, obs, weight, on_chip(grid), *map(on_chip, tables))


def dirichlet(distance, pixel_start):
    distance = ((distance & (NIMG - 1)) ^ (NIMG // 2)) - NIMG // 2
    top = cos_sin((distance * (NIMG // (NIMG // FW * 2))) & (NIMG - 1))[1]
    bottom = cos_sin(distance, 17)[1]
    ratio = jnp.where(distance == 0, float(FW), top / jnp.where(distance == 0, 1.0, bottom))
    c, s = cos_sin((distance * (2 * pixel_start + FW - 1)) & (2 * NIMG - 1), 17)
    return c * ratio, s * ratio


def gram_kernel(step_ref, starts_ref, column_ref, offsets_ref, adj_ref, first_ref, out_hbm, flip_ref, v_ref, out_ref, sem):
    wide = 2 * SGW
    pixel_start = offsets_ref[1, lax.axis_index("facet")]
    own = column_ref[0]
    row = iota((NCOL, wide), 0)
    starts = jnp.zeros((NCOL, wide), I32)
    for c in range(NCOL):
        starts = jnp.where(row == c, starts_ref[c], starts)
    lane = iota((NCOL, wide), 1)
    v_ref[0], v_ref[1] = dirichlet(starts - own + (lane - (SGW - 1)), pixel_start)
    v_ref[2], v_ref[3] = dirichlet(starts + own + (2 * (SGW - 1) - lane), pixel_start)
    anti = (iota((SGW, SGW), 0) + iota((SGW, SGW), 1)) == SGW - 1
    flip_ref[...] = jnp.where(anti, 1.0, 0.0).astype(BF)
    totals = [None] * 4
    for c in range(NCOL):
        lines = adj_ref[:, c].reshape(SGW, 2 * FROWS)
        turned = jnp.dot(flip_ref[...], lines, preferred_element_type=F32).astype(BF)
        for k in range(4):
            spread = jnp.broadcast_to(v_ref[k, c : c + 1, :], (SGW, wide))
            band = pltpu.roll(spread, SGW + 1, 1, stride=1, stride_axis=0)[:, :SGW].astype(BF)
            term = jnp.dot(band, lines if k < 2 else turned, preferred_element_type=F32)
            totals[k] = term if c == 0 else totals[k] + term
    scale = step_ref[0] * (0.5 * NORM)
    p1, p2, p3, p4 = totals
    re = p1[:, :FROWS] - p2[:, FROWS:] + p3[:, :FROWS] - p4[:, FROWS:]
    im = p2[:, :FROWS] + p1[:, FROWS:] - p4[:, :FROWS] - p3[:, FROWS:]
    first = first_ref[...].astype(F32)
    out_ref[:, :SLICE, :] = (first[:, :SLICE] + (scale * re).reshape(FACETS, SLICE, FROWS)).astype(BF)
    out_ref[:, SLICE:, :] = (first[:, SLICE:] + (scale * im).reshape(FACETS, SLICE, FROWS)).astype(BF)
    write_out([(out_ref, out_hbm, sem)])


def gram(steps, column_starts, column_start, offsets, adj, first):
    return pl.pallas_call(
        gram_kernel,
        out_shape=jax.ShapeDtypeStruct((FACETS, 2 * SLICE, FROWS), BF),
        in_specs=[SMEM_SPEC] * 4 + [VMEM_SPEC] * 2,
        out_specs=HBM_SPEC,
        scratch_shapes=[
            pltpu.VMEM((SGW, SGW), BF),
            pltpu.VMEM((4, NCOL, 2 * SGW), F32),
            pltpu.VMEM((FACETS, 2 * SLICE, FROWS), BF),
            pltpu.SemaphoreType.DMA,
        ],
        compiler_params=PARAMS,
        name="gram",
    )(steps, column_starts, column_start, offsets, on_chip(adj.reshape(FACETS, NCOL, SLICE, 2 * FROWS)), first)


def update_kernel(step_ref, adj0_ref, adj1_ref, table_hbm, pc_ref, ps_ref, model_ref, out_ref, table_ref, both_ref, even_ref, odd_ref, sem):
    part = pl.program_id(0)
    fetch = pltpu.make_async_copy(table_hbm, table_ref, sem)

    def turn(pair, target_ref):
        re = both_ref[:FROWS, :]
        im = both_ref[FROWS:, :]
        for p in range(PAIR5):
            pc = pc_ref[pl.ds(pair * PAIR5 + p, 1), :]
            ps = ps_ref[pl.ds(pair * PAIR5 + p, 1), :]
            lines = slice(p * FROWS, (p + 1) * FROWS)
            target_ref[lines, :COLUMNS] = (re * pc - im * ps).astype(BF)
            target_ref[lines, COLUMNS:] = (im * pc + re * ps).astype(BF)

    def add(place, source_ref):
        gradient = jnp.dot(source_ref[...], table_ref[...], preferred_element_type=F32)
        for p in range(PAIR5):
            left = (place * PAIR5 + p) * STEP5
            lines = gradient[p * FROWS : (p + 1) * FROWS]
            out_ref[:, left : left + STEP5] = model_ref[:, left : left + STEP5] + lines

    @pl.when(part == 0)
    def _():
        fetch.start()
        first = step_ref[0] * NORM
        second = step_ref[1] * NORM
        for j in range(FACETS):
            lines0 = adj0_ref[j * NCOL : (j + 1) * NCOL].reshape(NCOL * SLICE, 2 * FROWS).astype(F32)
            lines1 = adj1_ref[j * NCOL : (j + 1) * NCOL].reshape(NCOL * SLICE, 2 * FROWS).astype(F32)
            both = first * lines0 + second * lines1
            both_ref[:, j * NCOL * SLICE : (j + 1) * NCOL * SLICE] = both.T
        turn(0, even_ref)
        fetch.wait()

    turn(2 * part + 1, odd_ref)
    add(0, even_ref)
    turn(jnp.minimum(2 * part + 2, HIGH5 // PAIR5 - 2), even_ref)
    add(1, odd_ref)


def update(steps, adj0, adj1, tables, model):
    table, pc, ps = tables
    wide = pl.BlockSpec((FROWS, 2 * PAIR5 * STEP5), lambda i: (0, i))
    return pl.pallas_call(
        update_kernel,
        grid=(HIGH5 // PAIR5 // 2,),
        out_shape=jax.ShapeDtypeStruct((FROWS, FW), F32),
        in_specs=[SMEM_SPEC, VMEM_SPEC, VMEM_SPEC, HBM_SPEC, VMEM_SPEC, VMEM_SPEC, wide],
        out_specs=wide,
        scratch_shapes=[
            pltpu.VMEM((2 * COLUMNS, STEP5), BF),
            pltpu.VMEM((2 * FROWS, COLUMNS), F32),
            pltpu.VMEM((PAIR5 * FROWS, 2 * COLUMNS), BF),
            pltpu.VMEM((PAIR5 * FROWS, 2 * COLUMNS), BF),
            pltpu.SemaphoreType.DMA,
        ],
        compiler_params=WIDE_PARAMS,
        name="update",
    )(steps, on_chip(adj0), on_chip(adj1), off_chip(table), on_chip(pc), on_chip(ps), off_chip(model))


def update_table_kernel(starts_ref, offsets_ref, table_hbm, pc_ref, ps_ref, table_ref, base_ref, turn_ref, sem):
    group = NCOL * SLICE
    line = iota((group, STEP5), 0)
    freq = line & (SLICE - 1)
    for c in range(NCOL):
        freq = freq + jnp.where((line >> 4) == c, starts_ref[c], 0)
    base_ref[0], base_ref[1] = phase(freq, iota((group, STEP5), 1))
    turn_ref[0], turn_ref[1] = phase(SLICE * iota((FACETS, STEP5), 0), iota((FACETS, STEP5), 1))

    def one(j, carry):
        c = turn_ref[0, pl.ds(j, 1), :]
        s = turn_ref[1, pl.ds(j, 1), :]
        cut = pl.ds(pl.multiple_of(j * group, group), group)
        table_ref[cut, :] = (base_ref[0] * c - base_ref[1] * s).astype(BF)
        cut = pl.ds(pl.multiple_of(COLUMNS + j * group, group), group)
        table_ref[cut, :] = (-(base_ref[1] * c + base_ref[0] * s)).astype(BF)
        return carry

    lax.fori_loop(0, FACETS, one, 0)
    lane = iota((HIGH5, COLUMNS), 1)
    freq = SLICE * (lane >> 7) + (lane & (SLICE - 1))
    for c in range(NCOL):
        freq = freq + jnp.where(((lane >> 4) & (NCOL - 1)) == c, starts_ref[c], 0)
    pixel_start = offsets_ref[1, lax.axis_index("facet")]
    pc_ref[...], ps_ref[...] = phase(freq, pixel_start + STEP5 * iota((HIGH5, COLUMNS), 0))
    write_out([(table_ref, table_hbm, sem)])


def update_tables(column_starts, offsets):
    return pl.pallas_call(
        update_table_kernel,
        out_shape=(
            pltpu.HBM((2 * COLUMNS, STEP5), BF),
            pltpu.VMEM((HIGH5, COLUMNS), F32),
            pltpu.VMEM((HIGH5, COLUMNS), F32),
        ),
        in_specs=[SMEM_SPEC, SMEM_SPEC],
        out_specs=(HBM_SPEC, VMEM_SPEC, VMEM_SPEC),
        scratch_shapes=[
            pltpu.VMEM((2 * COLUMNS, STEP5), BF),
            pltpu.VMEM((2, NCOL * SLICE, STEP5), F32),
            pltpu.VMEM((2, FACETS, STEP5), F32),
            pltpu.SemaphoreType.DMA,
        ],
        compiler_params=PARAMS,
        name="update_tables",
    )(column_starts, offsets)


def exchange(value):
    return lax.all_to_all(value, "facet", split_axis=0, concat_axis=0, tiled=True)


def to_facets(value):
    copies = value.reshape(FACETS * NCOL, *value.shape[2:])
    return lax.all_to_all(copies, ("facet", "sub"), split_axis=0, concat_axis=0, tiled=True)


def local(
    model_image,
    step_sizes,
    facet_offsets,
    col_offsets,
    row_offsets,
    counts,
    vis_uv,
    vis_obs,
    vis_weight,
):
    lines = lax.optimization_barrier(jnp.broadcast_to(col_offsets[:, None].astype(F32), (256, 128)))
    column_starts = lax.optimization_barrier(lax.all_gather(lines, "sub", axis=0, tiled=True))[::256, 0].astype(I32)
    uv = vis_uv.reshape(2, VCAP)
    obs = vis_obs.reshape(2, VCAP)
    weight = vis_weight.reshape(1, VCAP)
    model = model_image[0]
    first = section(col_offsets, facet_offsets, model)
    tables = cycle_tables(facet_offsets, row_offsets, uv)
    rows, kernels = tables[:3], tables[3:]
    grid = exchange(grids(exchange(first), rows))
    gridded, residual = visibilities(counts, obs, weight, grid, kernels)
    gridded, column_starts = lax.optimization_barrier((gridded, column_starts))
    adj0 = to_facets(adjoint(exchange(gridded), rows))
    tables = update_tables(column_starts, facet_offsets)
    second = gram(step_sizes, column_starts, col_offsets, facet_offsets, adj0, first)
    grid = exchange(grids(exchange(second), rows))
    gridded, residual = visibilities(counts, obs, weight, grid, kernels)
    adj1 = to_facets(adjoint(exchange(gridded), rows))
    model = update(step_sizes, adj0, adj1, tables, model)
    return model[None], residual.reshape(2, 1, 1, VCAP)


def solution(mesh):
    in_specs = (
        P("facet", None, None),
        P(),
        P(),
        P("sub"),
        P("sub", None),
        P("sub", None),
        P(None, "sub", "facet", None),
        P(None, "sub", "facet", None),
        P("sub", "facet", None),
    )
    out_specs = (P("facet", None, None), P(None, "sub", "facet", None))
    return jax.shard_map(local, mesh=mesh, in_specs=in_specs, out_specs=out_specs, check_vma=False)
```

```python
import math

import jax
import jax.numpy as jnp
from jax import lax
from jax.experimental import pallas as pl
from jax.experimental.pallas import tpu as pltpu
from jax.sharding import PartitionSpec as P

NIMG = 65536
FW = 8192
FROWS = 128
SGW = 256
VCAP = 4096
OS = 8
KSUP = 4
FACETS = 16
NCOL = 8
NROWSG = 16
SLICE = SGW // FACETS
COLUMNS = NCOL * SGW

STEP1 = 256
HIGH1 = FW // STEP1
PARTS1 = 4
STEP5 = 512
HIGH5 = FW // STEP5
PAIR5 = 2
VBLOCK = 1024
CHUNK = 4
UNROLL4 = 8

BF = jnp.bfloat16
F32 = jnp.float32
I32 = jnp.int32
NORM = 1.0 / math.sqrt(FACETS * FROWS * FW)
PARAMS = pltpu.CompilerParams(vmem_limit_bytes=16 << 20)
WIDE_PARAMS = pltpu.CompilerParams(vmem_limit_bytes=24 << 20)
SMEM_SPEC = pl.BlockSpec(memory_space=pltpu.SMEM)
VMEM_SPEC = pl.BlockSpec(memory_space=pltpu.VMEM)
HBM_SPEC = pl.BlockSpec(memory_space=pltpu.HBM)


def cos_sin(index, bits=16):
    quadrant = (index + (1 << (bits - 3))) >> (bits - 2)
    angle = (index - (quadrant << (bits - 2))).astype(F32) * (2.0 * math.pi / (1 << bits))
    square = angle * angle
    sine = angle * (1.0 + square * (-1.0 / 6 + square * (1.0 / 120 + square * (-1.0 / 5040 + square / 362880))))
    cosine = 1.0 + square * (-0.5 + square * (1.0 / 24 + square * (-1.0 / 720 + square / 40320)))
    swapped = (quadrant & 1) != 0
    c = jnp.where(swapped, sine, cosine)
    s = jnp.where(swapped, cosine, sine)
    c = jnp.where(((quadrant + 1) & 2) != 0, -c, c)
    s = jnp.where((quadrant & 2) != 0, -s, s)
    return c, s


def phase(frequency, pixel):
    return cos_sin((frequency * pixel) & (NIMG - 1))


def on_chip(value):
    return pltpu.with_memory_space_constraint(value, pltpu.VMEM)


def off_chip(value):
    return pltpu.with_memory_space_constraint(value, pltpu.HBM)


def write_out(pairs):
    copies = [pltpu.make_async_copy(source, target, sem) for source, target, sem in pairs]
    for copy in copies:
        copy.start()
    for copy in copies:
        copy.wait()


def iota(shape, dim):
    return lax.broadcasted_iota(I32, shape, dim)


def column_of(ref, count, lanes):
    row = iota((count, lanes), 0)
    value = jnp.zeros((count, lanes), I32)
    for i in range(count):
        value = jnp.where(row == i, ref[i], value)
    return value


def section_kernel(column_ref, offsets_ref, model_hbm, out_hbm, model_ref, table_ref, pc_ref, ps_ref, out_ref, sems, sem):
    wide = FW // PARTS1
    fetches = []
    for part in range(PARTS1):
        cut = pl.ds(part * wide, wide)
        fetches.append(pltpu.make_async_copy(model_hbm.at[:, cut], model_ref.at[:, cut], sems.at[part]))
        fetches[-1].start()
    column_start = column_ref[0]
    pixel_start = offsets_ref[1, lax.axis_index("facet")]
    freq = column_start + iota((STEP1, SGW), 1)
    c, s = phase(freq, iota((STEP1, SGW), 0))
    table_ref[:, :SGW] = c.astype(BF)
    table_ref[:, SGW:] = (-s).astype(BF)
    freq = column_start + iota((HIGH1, SGW), 1)
    pc_ref[...], ps_ref[...] = phase(freq, pixel_start + STEP1 * iota((HIGH1, SGW), 0))
    acc_re = jnp.zeros((FROWS, SGW), F32)
    acc_im = jnp.zeros((FROWS, SGW), F32)
    for high in range(HIGH1):
        if high % (HIGH1 // PARTS1) == 0:
            fetches[high // (HIGH1 // PARTS1)].wait()
        block = model_ref[:, high * STEP1 : (high + 1) * STEP1].astype(BF)
        product = jnp.dot(block, table_ref[...], preferred_element_type=F32)
        re = product[:, :SGW]
        im = product[:, SGW:]
        pc = pc_ref[high : high + 1, :]
        ps = ps_ref[high : high + 1, :]
        acc_re = acc_re + (re * pc + im * ps)
        acc_im = acc_im + (im * pc - re * ps)
    out_ref[:, :SLICE, :] = acc_re.T.astype(BF).reshape(FACETS, SLICE, FROWS)
    out_ref[:, SLICE:, :] = acc_im.T.astype(BF).reshape(FACETS, SLICE, FROWS)
    write_out([(out_ref, out_hbm, sem)])


def section(column_start, offsets, model):
    return pl.pallas_call(
        section_kernel,
        out_shape=jax.ShapeDtypeStruct((FACETS, 2 * SLICE, FROWS), BF),
        in_specs=[SMEM_SPEC, SMEM_SPEC, HBM_SPEC],
        out_specs=HBM_SPEC,
        scratch_shapes=[
            pltpu.VMEM((FROWS, FW), F32),
            pltpu.VMEM((STEP1, 2 * SGW), BF),
            pltpu.VMEM((HIGH1, SGW), F32),
            pltpu.VMEM((HIGH1, SGW), F32),
            pltpu.VMEM((FACETS, 2 * SLICE, FROWS), BF),
            pltpu.SemaphoreType.DMA((PARTS1,)),
            pltpu.SemaphoreType.DMA,
        ],
        compiler_params=PARAMS,
        name="section",
    )(column_start, offsets, off_chip(model))


def kernel_columns(position):
    cells = iota((SGW, position.shape[1]), 0) * OS + OS // 2
    offset = cells - position
    distance = offset.astype(F32) * (1.0 / OS)
    inside = jnp.abs(offset) <= KSUP * OS
    return jnp.where(inside, jnp.exp(-0.5 * distance * distance), 0.0).astype(BF)


def table_kernel(offsets_ref, rows_ref, uv_ref, table_ref, c_ref, s_ref, ku_ref, kv_ref, base_ref, turn_ref):
    base_ref[0], base_ref[1] = phase(iota((FROWS, SGW), 1), iota((FROWS, SGW), 0))
    row = iota((FACETS, SGW), 0)
    start = jnp.zeros((FACETS, SGW), I32)
    for f in range(FACETS):
        start = jnp.where(row == f, offsets_ref[0, f], start)
    turn_ref[0], turn_ref[1] = phase(iota((FACETS, SGW), 1), start)
    row = iota((NROWSG, FROWS), 0)
    freq = jnp.zeros((NROWSG, FROWS), I32)
    for r in range(NROWSG):
        freq = jnp.where(row == r, rows_ref[0, r], freq)

    def one(f, carry):
        cf = turn_ref[0, pl.ds(f, 1), :]
        sf = turn_ref[1, pl.ds(f, 1), :]
        lines = pl.ds(pl.multiple_of(f * FROWS, FROWS), FROWS)
        table_ref[0, lines, :] = (base_ref[0] * cf - base_ref[1] * sf).astype(BF)
        table_ref[1, lines, :] = (base_ref[1] * cf + base_ref[0] * sf).astype(BF)
        c_ref[f], s_ref[f] = phase(freq, offsets_ref[0, f] + iota((NROWSG, FROWS), 1))
        cut = pl.ds(pl.multiple_of(f * SGW, SGW), SGW)
        ku_ref[:, cut] = kernel_columns(uv_ref[0:1, cut])
        kv_ref[:, cut] = kernel_columns(uv_ref[1:2, cut])
        return carry

    lax.fori_loop(0, FACETS, one, 0)


def cycle_tables(offsets, rows, uv):
    return pl.pallas_call(
        table_kernel,
        out_shape=(
            pltpu.VMEM((2, FACETS * FROWS, SGW), BF),
            pltpu.VMEM((FACETS, NROWSG, FROWS), F32),
            pltpu.VMEM((FACETS, NROWSG, FROWS), F32),
            pltpu.VMEM((SGW, VCAP), BF),
            pltpu.VMEM((SGW, VCAP), BF),
        ),
        in_specs=[SMEM_SPEC, SMEM_SPEC, VMEM_SPEC],
        out_specs=(VMEM_SPEC,) * 5,
        scratch_shapes=[
            pltpu.VMEM((2, FROWS, SGW), F32),
            pltpu.VMEM((2, FACETS, SGW), F32),
        ],
        compiler_params=PARAMS,
        name="cycle_tables",
    )(offsets, rows, uv)


def grid_kernel(in_ref, c_ref, s_ref, table_ref, out_hbm, turned_ref, out_ref, sem):
    half = NROWSG * SLICE
    for f in range(FACETS):
        re = in_ref[f, :SLICE, :].astype(F32)
        im = in_ref[f, SLICE:, :].astype(F32)
        cut = slice(f * FROWS, (f + 1) * FROWS)
        for r in range(NROWSG):
            c = c_ref[f, r : r + 1, :]
            s = s_ref[f, r : r + 1, :]
            turned_ref[r * SLICE : (r + 1) * SLICE, cut] = (re * c + im * s).astype(BF)
            turned_ref[half + r * SLICE : half + (r + 1) * SLICE, cut] = (im * c - re * s).astype(BF)
    by_c = jnp.dot(turned_ref[...], table_ref[0], preferred_element_type=F32)
    by_s = jnp.dot(turned_ref[...], table_ref[1], preferred_element_type=F32)
    re = (NORM * (by_c[:half] + by_s[half:])).astype(BF)
    im = (NORM * (by_c[half:] - by_s[:half])).astype(BF)
    out_ref[:, :SLICE, :] = re.reshape(NROWSG, SLICE, SGW)
    out_ref[:, SLICE:, :] = im.reshape(NROWSG, SLICE, SGW)
    write_out([(out_ref, out_hbm, sem)])


def grids(sections, tables):
    table, c, s = tables
    return pl.pallas_call(
        grid_kernel,
        out_shape=jax.ShapeDtypeStruct((NROWSG, 2 * SLICE, SGW), BF),
        in_specs=[VMEM_SPEC] * 4,
        out_specs=HBM_SPEC,
        scratch_shapes=[
            pltpu.VMEM((2 * NROWSG * SLICE, FACETS * FROWS), BF),
            pltpu.VMEM((NROWSG, 2 * SLICE, SGW), BF),
            pltpu.SemaphoreType.DMA,
        ],
        compiler_params=PARAMS,
        name="grids",
    )(on_chip(sections), on_chip(c), on_chip(s), on_chip(table))


def adjoint_kernel(in_ref, c_ref, s_ref, table_ref, out_hbm, lines_ref, out_ref, sems):
    half = NROWSG * SLICE
    lines_ref[:half] = in_ref[:, :SLICE, :].reshape(half, SGW)
    lines_ref[half:] = in_ref[:, SLICE:, :].reshape(half, SGW)

    def one(pair, carry):
        cut = pl.ds(pl.multiple_of(pair * 2 * FROWS, 2 * FROWS), 2 * FROWS)
        dims = (((1,), (1,)), ((), ()))
        by_c = lax.dot_general(lines_ref[...], table_ref[0, cut, :], dims, preferred_element_type=F32)
        by_s = lax.dot_general(lines_ref[...], table_ref[1, cut, :], dims, preferred_element_type=F32)
        for k in range(2):
            f = 2 * pair + k
            lanes = slice(k * FROWS, (k + 1) * FROWS)
            acc_re = jnp.zeros((SLICE, FROWS), F32)
            acc_im = jnp.zeros((SLICE, FROWS), F32)
            for r in range(NROWSG):
                top = slice(r * SLICE, (r + 1) * SLICE)
                low = slice(half + r * SLICE, half + (r + 1) * SLICE)
                re = by_c[top, lanes] - by_s[low, lanes]
                im = by_c[low, lanes] + by_s[top, lanes]
                c = c_ref[f, r : r + 1, :]
                s = s_ref[f, r : r + 1, :]
                acc_re = acc_re + (re * c - im * s)
                acc_im = acc_im + (im * c + re * s)
            out_ref[f] = jnp.concatenate([acc_re, acc_im], axis=1).astype(BF)
        return carry

    lax.fori_loop(0, FACETS // 2, one, 0, unroll=UNROLL4)
    write_out([(out_ref, out_hbm.at[:, copy], sems.at[copy]) for copy in range(NCOL)])


def adjoint(gridded, tables):
    table, c, s = tables
    return pl.pallas_call(
        adjoint_kernel,
        out_shape=jax.ShapeDtypeStruct((FACETS, NCOL, SLICE, 2 * FROWS), BF),
        in_specs=[VMEM_SPEC] * 4,
        out_specs=HBM_SPEC,
        scratch_shapes=[
            pltpu.VMEM((2 * NROWSG * SLICE, SGW), BF),
            pltpu.VMEM((FACETS, SLICE, 2 * FROWS), BF),
            pltpu.SemaphoreType.DMA((NCOL,)),
        ],
        compiler_params=PARAMS,
        name="adjoint",
    )(on_chip(gridded), on_chip(c), on_chip(s), on_chip(table))


def visibility_kernel(counts_ref, obs_ref, weight_ref, in_ref, ku_ref, kv_ref, gridded_hbm, res_ref, acc_ref, gridded_ref, sem):
    count = counts_ref[0, lax.axis_index("facet")]
    grid = [in_ref[:, half * SLICE : (half + 1) * SLICE, :].reshape(SGW, SGW) for half in range(2)]
    for part in range(VCAP // VBLOCK):
        cut = slice(part * VBLOCK, (part + 1) * VBLOCK)
        live = part * VBLOCK + iota((1, VBLOCK), 1) < count
        weight = weight_ref[:, cut].astype(F32)
        for half in range(2):
            sampled = jnp.dot(grid[half], ku_ref[:, cut], preferred_element_type=F32)
            predicted = jnp.sum(sampled * kv_ref[:, cut].astype(F32), axis=0, keepdims=True)
            observed = obs_ref[half : half + 1, cut].astype(F32)
            residual = jnp.where(live, weight * (observed - predicted), 0.0)
            res_ref[half : half + 1, cut] = residual
            weighted = (residual * kv_ref[:, cut].astype(F32)).astype(BF)
            total = lax.dot_general(
                weighted, ku_ref[:, cut], (((1,), (1,)), ((), ())), preferred_element_type=F32
            )
            if part:
                total = total + acc_ref[half]
            if part + 1 < VCAP // VBLOCK:
                acc_ref[half] = total
            else:
                lines = total.astype(BF).reshape(FACETS, SLICE, SGW)
                gridded_ref[:, half * SLICE : (half + 1) * SLICE, :] = lines
    write_out([(gridded_ref, gridded_hbm, sem)])


def visibilities(counts, obs, weight, grid, tables):
    return pl.pallas_call(
        visibility_kernel,
        out_shape=(
            jax.ShapeDtypeStruct((FACETS, 2 * SLICE, SGW), BF),
            jax.ShapeDtypeStruct((2, VCAP), F32),
        ),
        in_specs=[SMEM_SPEC] + [VMEM_SPEC] * 5,
        out_specs=(HBM_SPEC, VMEM_SPEC),
        scratch_shapes=[
            pltpu.VMEM((2, SGW, SGW), F32),
            pltpu.VMEM((FACETS, 2 * SLICE, SGW), BF),
            pltpu.SemaphoreType.DMA,
        ],
        compiler_params=PARAMS,
        name="visibilities",
    )(counts, obs, weight, on_chip(grid), *map(on_chip, tables))


def dirichlet(distance, pixel_start):
    distance = ((distance & (NIMG - 1)) ^ (NIMG // 2)) - NIMG // 2
    top = cos_sin((distance * (NIMG // (NIMG // FW * 2))) & (NIMG - 1))[1]
    bottom = cos_sin(distance, 17)[1]
    ratio = jnp.where(distance == 0, float(FW), top / jnp.where(distance == 0, 1.0, bottom))
    c, s = cos_sin((distance * (2 * pixel_start + FW - 1)) & (2 * NIMG - 1), 17)
    return c * ratio, s * ratio


def gram_kernel(step_ref, starts_ref, column_ref, offsets_ref, adj_ref, first_ref, out_hbm, flip_ref, v_ref, out_ref, sem):
    wide = 2 * SGW
    pixel_start = offsets_ref[1, lax.axis_index("facet")]
    own = column_ref[0]
    row = iota((NCOL, wide), 0)
    starts = jnp.zeros((NCOL, wide), I32)
    for c in range(NCOL):
        starts = jnp.where(row == c, starts_ref[c], starts)
    lane = iota((NCOL, wide), 1)
    v_ref[0], v_ref[1] = dirichlet(starts - own + (lane - (SGW - 1)), pixel_start)
    v_ref[2], v_ref[3] = dirichlet(starts + own + (2 * (SGW - 1) - lane), pixel_start)
    anti = (iota((SGW, SGW), 0) + iota((SGW, SGW), 1)) == SGW - 1
    flip_ref[...] = jnp.where(anti, 1.0, 0.0).astype(BF)
    totals = [None] * 4
    for c in range(NCOL):
        lines = adj_ref[:, c].reshape(SGW, 2 * FROWS)
        turned = jnp.dot(flip_ref[...], lines, preferred_element_type=F32).astype(BF)
        for k in range(4):
            spread = jnp.broadcast_to(v_ref[k, c : c + 1, :], (SGW, wide))
            band = pltpu.roll(spread, SGW + 1, 1, stride=1, stride_axis=0)[:, :SGW].astype(BF)
            term = jnp.dot(band, lines if k < 2 else turned, preferred_element_type=F32)
            totals[k] = term if c == 0 else totals[k] + term
    scale = step_ref[0] * (0.5 * NORM)
    p1, p2, p3, p4 = totals
    re = p1[:, :FROWS] - p2[:, FROWS:] + p3[:, :FROWS] - p4[:, FROWS:]
    im = p2[:, :FROWS] + p1[:, FROWS:] - p4[:, :FROWS] - p3[:, FROWS:]
    first = first_ref[...].astype(F32)
    out_ref[:, :SLICE, :] = (first[:, :SLICE] + (scale * re).reshape(FACETS, SLICE, FROWS)).astype(BF)
    out_ref[:, SLICE:, :] = (first[:, SLICE:] + (scale * im).reshape(FACETS, SLICE, FROWS)).astype(BF)
    write_out([(out_ref, out_hbm, sem)])


def gram(steps, column_starts, column_start, offsets, adj, first):
    return pl.pallas_call(
        gram_kernel,
        out_shape=jax.ShapeDtypeStruct((FACETS, 2 * SLICE, FROWS), BF),
        in_specs=[SMEM_SPEC] * 4 + [VMEM_SPEC] * 2,
        out_specs=HBM_SPEC,
        scratch_shapes=[
            pltpu.VMEM((SGW, SGW), BF),
            pltpu.VMEM((4, NCOL, 2 * SGW), F32),
            pltpu.VMEM((FACETS, 2 * SLICE, FROWS), BF),
            pltpu.SemaphoreType.DMA,
        ],
        compiler_params=PARAMS,
        name="gram",
    )(steps, column_starts, column_start, offsets, on_chip(adj.reshape(FACETS, NCOL, SLICE, 2 * FROWS)), first)


def update_kernel(step_ref, adj0_ref, adj1_ref, table_hbm, pc_ref, ps_ref, model_ref, out_ref, table_ref, both_ref, even_ref, odd_ref, sem):
    part = pl.program_id(0)
    fetch = pltpu.make_async_copy(table_hbm, table_ref, sem)

    def turn(pair, target_ref):
        re = both_ref[:FROWS, :]
        im = both_ref[FROWS:, :]
        for p in range(PAIR5):
            pc = pc_ref[pl.ds(pair * PAIR5 + p, 1), :]
            ps = ps_ref[pl.ds(pair * PAIR5 + p, 1), :]
            lines = slice(p * FROWS, (p + 1) * FROWS)
            target_ref[lines, :COLUMNS] = (re * pc - im * ps).astype(BF)
            target_ref[lines, COLUMNS:] = (im * pc + re * ps).astype(BF)

    def add(place, source_ref):
        gradient = jnp.dot(source_ref[...], table_ref[...], preferred_element_type=F32)
        for p in range(PAIR5):
            left = (place * PAIR5 + p) * STEP5
            lines = gradient[p * FROWS : (p + 1) * FROWS]
            out_ref[:, left : left + STEP5] = model_ref[:, left : left + STEP5] + lines

    @pl.when(part == 0)
    def _():
        fetch.start()
        first = step_ref[0] * NORM
        second = step_ref[1] * NORM
        for j in range(FACETS):
            lines0 = adj0_ref[j * NCOL : (j + 1) * NCOL].reshape(NCOL * SLICE, 2 * FROWS).astype(F32)
            lines1 = adj1_ref[j * NCOL : (j + 1) * NCOL].reshape(NCOL * SLICE, 2 * FROWS).astype(F32)
            both = first * lines0 + second * lines1
            both_ref[:, j * NCOL * SLICE : (j + 1) * NCOL * SLICE] = both.T
        turn(0, even_ref)
        fetch.wait()

    turn(2 * part + 1, odd_ref)
    add(0, even_ref)
    turn(jnp.minimum(2 * part + 2, HIGH5 // PAIR5 - 2), even_ref)
    add(1, odd_ref)


def update(steps, adj0, adj1, tables, model):
    table, pc, ps = tables
    wide = pl.BlockSpec((FROWS, 2 * PAIR5 * STEP5), lambda i: (0, i))
    return pl.pallas_call(
        update_kernel,
        grid=(HIGH5 // PAIR5 // 2,),
        out_shape=jax.ShapeDtypeStruct((FROWS, FW), F32),
        in_specs=[SMEM_SPEC, VMEM_SPEC, VMEM_SPEC, HBM_SPEC, VMEM_SPEC, VMEM_SPEC, wide],
        out_specs=wide,
        scratch_shapes=[
            pltpu.VMEM((2 * COLUMNS, STEP5), BF),
            pltpu.VMEM((2 * FROWS, COLUMNS), F32),
            pltpu.VMEM((PAIR5 * FROWS, 2 * COLUMNS), BF),
            pltpu.VMEM((PAIR5 * FROWS, 2 * COLUMNS), BF),
            pltpu.SemaphoreType.DMA,
        ],
        compiler_params=WIDE_PARAMS,
        name="update",
    )(steps, on_chip(adj0), on_chip(adj1), off_chip(table), on_chip(pc), on_chip(ps), off_chip(model))


def update_table_kernel(starts_ref, offsets_ref, table_hbm, pc_ref, ps_ref, table_ref, base_ref, turn_ref, sem):
    group = NCOL * SLICE
    line = iota((group, STEP5), 0)
    freq = line & (SLICE - 1)
    for c in range(NCOL):
        freq = freq + jnp.where((line >> 4) == c, starts_ref[c], 0)
    base_ref[0], base_ref[1] = phase(freq, iota((group, STEP5), 1))
    turn_ref[0], turn_ref[1] = phase(SLICE * iota((FACETS, STEP5), 0), iota((FACETS, STEP5), 1))

    def one(j, carry):
        c = turn_ref[0, pl.ds(j, 1), :]
        s = turn_ref[1, pl.ds(j, 1), :]
        cut = pl.ds(pl.multiple_of(j * group, group), group)
        table_ref[cut, :] = (base_ref[0] * c - base_ref[1] * s).astype(BF)
        cut = pl.ds(pl.multiple_of(COLUMNS + j * group, group), group)
        table_ref[cut, :] = (-(base_ref[1] * c + base_ref[0] * s)).astype(BF)
        return carry

    lax.fori_loop(0, FACETS, one, 0)
    lane = iota((HIGH5, COLUMNS), 1)
    freq = SLICE * (lane >> 7) + (lane & (SLICE - 1))
    for c in range(NCOL):
        freq = freq + jnp.where(((lane >> 4) & (NCOL - 1)) == c, starts_ref[c], 0)
    pixel_start = offsets_ref[1, lax.axis_index("facet")]
    pc_ref[...], ps_ref[...] = phase(freq, pixel_start + STEP5 * iota((HIGH5, COLUMNS), 0))
    write_out([(table_ref, table_hbm, sem)])


def update_tables(column_starts, offsets):
    return pl.pallas_call(
        update_table_kernel,
        out_shape=(
            pltpu.HBM((2 * COLUMNS, STEP5), BF),
            pltpu.VMEM((HIGH5, COLUMNS), F32),
            pltpu.VMEM((HIGH5, COLUMNS), F32),
        ),
        in_specs=[SMEM_SPEC, SMEM_SPEC],
        out_specs=(HBM_SPEC, VMEM_SPEC, VMEM_SPEC),
        scratch_shapes=[
            pltpu.VMEM((2 * COLUMNS, STEP5), BF),
            pltpu.VMEM((2, NCOL * SLICE, STEP5), F32),
            pltpu.VMEM((2, FACETS, STEP5), F32),
            pltpu.SemaphoreType.DMA,
        ],
        compiler_params=PARAMS,
        name="update_tables",
    )(column_starts, offsets)


def exchange(value):
    return lax.all_to_all(value, "facet", split_axis=0, concat_axis=0, tiled=True)


def to_facets(value):
    copies = value.reshape(FACETS * NCOL, *value.shape[2:])
    return lax.all_to_all(copies, ("facet", "sub"), split_axis=0, concat_axis=0, tiled=True)


def local(
    model_image,
    step_sizes,
    facet_offsets,
    col_offsets,
    row_offsets,
    counts,
    vis_uv,
    vis_obs,
    vis_weight,
):
    lines = lax.optimization_barrier(jnp.broadcast_to(col_offsets[:, None], (8, 128)))
    column_starts = lax.optimization_barrier(lax.all_gather(lines, "sub", axis=0, tiled=True))[::8, 0]
    uv = vis_uv.reshape(2, VCAP)
    obs = vis_obs.reshape(2, VCAP)
    weight = vis_weight.reshape(1, VCAP)
    model = model_image[0]
    first = section(col_offsets, facet_offsets, model)
    tables = cycle_tables(facet_offsets, row_offsets, uv)
    rows, kernels = tables[:3], tables[3:]
    grid = exchange(grids(exchange(first), rows))
    gridded, residual = visibilities(counts, obs, weight, grid, kernels)
    adj0 = to_facets(adjoint(exchange(gridded), rows))
    tables = update_tables(column_starts, facet_offsets)
    second = gram(step_sizes, column_starts, col_offsets, facet_offsets, adj0, first)
    grid = exchange(grids(exchange(second), rows))
    gridded, residual = visibilities(counts, obs, weight, grid, kernels)
    adj1 = to_facets(adjoint(exchange(gridded), rows))
    model = update(step_sizes, adj0, adj1, tables, model)
    return model[None], residual.reshape(2, 1, 1, VCAP)


def solution(mesh):
    in_specs = (
        P("facet", None, None),
        P(),
        P(),
        P("sub"),
        P("sub", None),
        P("sub", None),
        P(None, "sub", "facet", None),
        P(None, "sub", "facet", None),
        P("sub", "facet", None),
    )
    out_specs = (P("facet", None, None), P(None, "sub", "facet", None))
    return jax.shard_map(local, mesh=mesh, in_specs=in_specs, out_specs=out_specs, check_vma=False)
```

```python
import math

import jax
import jax.numpy as jnp
from jax import lax
from jax.experimental import pallas as pl
from jax.experimental.pallas import tpu as pltpu
from jax.sharding import PartitionSpec as P

NIMG = 65536
FW = 8192
FROWS = 128
SGW = 256
VCAP = 4096
OS = 8
KSUP = 4
FACETS = 16
NCOL = 8
NROWSG = 16
SLICE = SGW // FACETS
COLUMNS = NCOL * SGW

STEP1 = 256
HIGH1 = FW // STEP1
PARTS1 = 4
STEP5 = 512
HIGH5 = FW // STEP5
PAIR5 = 4
HALF = FROWS // 2
PARTS7 = 2
VBLOCK = 1024
CHUNK = 4
UNROLL4 = 8

BF = jnp.bfloat16
F32 = jnp.float32
I32 = jnp.int32
NORM = 1.0 / math.sqrt(FACETS * FROWS * FW)
PARAMS = pltpu.CompilerParams(vmem_limit_bytes=16 << 20)
WIDE_PARAMS = pltpu.CompilerParams(vmem_limit_bytes=24 << 20)
SMEM_SPEC = pl.BlockSpec(memory_space=pltpu.SMEM)
VMEM_SPEC = pl.BlockSpec(memory_space=pltpu.VMEM)
HBM_SPEC = pl.BlockSpec(memory_space=pltpu.HBM)


def cos_sin(index, bits=16):
    quadrant = (index + (1 << (bits - 3))) >> (bits - 2)
    angle = (index - (quadrant << (bits - 2))).astype(F32) * (2.0 * math.pi / (1 << bits))
    square = angle * angle
    sine = angle * (1.0 + square * (-1.0 / 6 + square * (1.0 / 120 + square * (-1.0 / 5040 + square / 362880))))
    cosine = 1.0 + square * (-0.5 + square * (1.0 / 24 + square * (-1.0 / 720 + square / 40320)))
    swapped = (quadrant & 1) != 0
    c = jnp.where(swapped, sine, cosine)
    s = jnp.where(swapped, cosine, sine)
    c = jnp.where(((quadrant + 1) & 2) != 0, -c, c)
    s = jnp.where((quadrant & 2) != 0, -s, s)
    return c, s


def phase(frequency, pixel):
    return cos_sin((frequency * pixel) & (NIMG - 1))


def on_chip(value):
    return pltpu.with_memory_space_constraint(value, pltpu.VMEM)


def off_chip(value):
    return pltpu.with_memory_space_constraint(value, pltpu.HBM)


def write_out(pairs):
    copies = [pltpu.make_async_copy(source, target, sem) for source, target, sem in pairs]
    for copy in copies:
        copy.start()
    for copy in copies:
        copy.wait()


def iota(shape, dim):
    return lax.broadcasted_iota(I32, shape, dim)


def column_of(ref, count, lanes):
    row = iota((count, lanes), 0)
    value = jnp.zeros((count, lanes), I32)
    for i in range(count):
        value = jnp.where(row == i, ref[i], value)
    return value


def section_kernel(column_ref, offsets_ref, model_hbm, out_hbm, model_ref, table_ref, pc_ref, ps_ref, out_ref, sems, sem):
    wide = FW // PARTS1
    fetches = []
    for part in range(PARTS1):
        cut = pl.ds(part * wide, wide)
        fetches.append(pltpu.make_async_copy(model_hbm.at[:, cut], model_ref.at[:, cut], sems.at[part]))
        fetches[-1].start()
    column_start = column_ref[0]
    pixel_start = offsets_ref[1, lax.axis_index("facet")]
    freq = column_start + iota((STEP1, SGW), 1)
    c, s = phase(freq, iota((STEP1, SGW), 0))
    table_ref[:, :SGW] = c.astype(BF)
    table_ref[:, SGW:] = (-s).astype(BF)
    freq = column_start + iota((HIGH1, SGW), 1)
    pc_ref[...], ps_ref[...] = phase(freq, pixel_start + STEP1 * iota((HIGH1, SGW), 0))
    acc_re = jnp.zeros((FROWS, SGW), F32)
    acc_im = jnp.zeros((FROWS, SGW), F32)
    for high in range(HIGH1):
        if high % (HIGH1 // PARTS1) == 0:
            fetches[high // (HIGH1 // PARTS1)].wait()
        block = model_ref[:, high * STEP1 : (high + 1) * STEP1].astype(BF)
        product = jnp.dot(block, table_ref[...], preferred_element_type=F32)
        re = product[:, :SGW]
        im = product[:, SGW:]
        pc = pc_ref[high : high + 1, :]
        ps = ps_ref[high : high + 1, :]
        acc_re = acc_re + (re * pc + im * ps)
        acc_im = acc_im + (im * pc - re * ps)
    out_ref[:, :SLICE, :] = acc_re.T.astype(BF).reshape(FACETS, SLICE, FROWS)
    out_ref[:, SLICE:, :] = acc_im.T.astype(BF).reshape(FACETS, SLICE, FROWS)
    write_out([(out_ref, out_hbm, sem)])


def section(column_start, offsets, model):
    return pl.pallas_call(
        section_kernel,
        out_shape=jax.ShapeDtypeStruct((FACETS, 2 * SLICE, FROWS), BF),
        in_specs=[SMEM_SPEC, SMEM_SPEC, HBM_SPEC],
        out_specs=HBM_SPEC,
        scratch_shapes=[
            pltpu.VMEM((FROWS, FW), F32),
            pltpu.VMEM((STEP1, 2 * SGW), BF),
            pltpu.VMEM((HIGH1, SGW), F32),
            pltpu.VMEM((HIGH1, SGW), F32),
            pltpu.VMEM((FACETS, 2 * SLICE, FROWS), BF),
            pltpu.SemaphoreType.DMA((PARTS1,)),
            pltpu.SemaphoreType.DMA,
        ],
        compiler_params=PARAMS,
        name="section",
    )(column_start, offsets, off_chip(model))


def kernel_columns(position):
    cells = iota((SGW, position.shape[1]), 0) * OS + OS // 2
    offset = cells - position
    distance = offset.astype(F32) * (1.0 / OS)
    inside = jnp.abs(offset) <= KSUP * OS
    return jnp.where(inside, jnp.exp(-0.5 * distance * distance), 0.0).astype(BF)


def table_kernel(offsets_ref, rows_ref, uv_ref, table_ref, c_ref, s_ref, ku_ref, kv_ref, base_ref, turn_ref):
    base_ref[0], base_ref[1] = phase(iota((FROWS, SGW), 1), iota((FROWS, SGW), 0))
    row = iota((FACETS, SGW), 0)
    start = jnp.zeros((FACETS, SGW), I32)
    for f in range(FACETS):
        start = jnp.where(row == f, offsets_ref[0, f], start)
    turn_ref[0], turn_ref[1] = phase(iota((FACETS, SGW), 1), start)
    row = iota((NROWSG, FROWS), 0)
    freq = jnp.zeros((NROWSG, FROWS), I32)
    for r in range(NROWSG):
        freq = jnp.where(row == r, rows_ref[0, r], freq)

    def one(f, carry):
        cf = turn_ref[0, pl.ds(f, 1), :]
        sf = turn_ref[1, pl.ds(f, 1), :]
        lines = pl.ds(pl.multiple_of(f * FROWS, FROWS), FROWS)
        table_ref[0, lines, :] = (base_ref[0] * cf - base_ref[1] * sf).astype(BF)
        table_ref[1, lines, :] = (base_ref[1] * cf + base_ref[0] * sf).astype(BF)
        c_ref[f], s_ref[f] = phase(freq, offsets_ref[0, f] + iota((NROWSG, FROWS), 1))
        cut = pl.ds(pl.multiple_of(f * SGW, SGW), SGW)
        ku_ref[:, cut] = kernel_columns(uv_ref[0:1, cut])
        kv_ref[:, cut] = kernel_columns(uv_ref[1:2, cut])
        return carry

    lax.fori_loop(0, FACETS, one, 0)


def cycle_tables(offsets, rows, uv):
    return pl.pallas_call(
        table_kernel,
        out_shape=(
            pltpu.VMEM((2, FACETS * FROWS, SGW), BF),
            pltpu.VMEM((FACETS, NROWSG, FROWS), F32),
            pltpu.VMEM((FACETS, NROWSG, FROWS), F32),
            pltpu.VMEM((SGW, VCAP), BF),
            pltpu.VMEM((SGW, VCAP), BF),
        ),
        in_specs=[SMEM_SPEC, SMEM_SPEC, VMEM_SPEC],
        out_specs=(VMEM_SPEC,) * 5,
        scratch_shapes=[
            pltpu.VMEM((2, FROWS, SGW), F32),
            pltpu.VMEM((2, FACETS, SGW), F32),
        ],
        compiler_params=PARAMS,
        name="cycle_tables",
    )(offsets, rows, uv)


def grid_kernel(in_ref, c_ref, s_ref, table_ref, out_hbm, turned_ref, out_ref, sem):
    half = NROWSG * SLICE
    for f in range(FACETS):
        re = in_ref[f, :SLICE, :].astype(F32)
        im = in_ref[f, SLICE:, :].astype(F32)
        cut = slice(f * FROWS, (f + 1) * FROWS)
        for r in range(NROWSG):
            c = c_ref[f, r : r + 1, :]
            s = s_ref[f, r : r + 1, :]
            turned_ref[r * SLICE : (r + 1) * SLICE, cut] = (re * c + im * s).astype(BF)
            turned_ref[half + r * SLICE : half + (r + 1) * SLICE, cut] = (im * c - re * s).astype(BF)
    by_c = jnp.dot(turned_ref[...], table_ref[0], preferred_element_type=F32)
    by_s = jnp.dot(turned_ref[...], table_ref[1], preferred_element_type=F32)
    re = (NORM * (by_c[:half] + by_s[half:])).astype(BF)
    im = (NORM * (by_c[half:] - by_s[:half])).astype(BF)
    out_ref[:, :SLICE, :] = re.reshape(NROWSG, SLICE, SGW)
    out_ref[:, SLICE:, :] = im.reshape(NROWSG, SLICE, SGW)
    write_out([(out_ref, out_hbm, sem)])


def grids(sections, tables):
    table, c, s = tables
    return pl.pallas_call(
        grid_kernel,
        out_shape=jax.ShapeDtypeStruct((NROWSG, 2 * SLICE, SGW), BF),
        in_specs=[VMEM_SPEC] * 4,
        out_specs=HBM_SPEC,
        scratch_shapes=[
            pltpu.VMEM((2 * NROWSG * SLICE, FACETS * FROWS), BF),
            pltpu.VMEM((NROWSG, 2 * SLICE, SGW), BF),
            pltpu.SemaphoreType.DMA,
        ],
        compiler_params=PARAMS,
        name="grids",
    )(on_chip(sections), on_chip(c), on_chip(s), on_chip(table))


def adjoint_kernel(in_ref, c_ref, s_ref, table_ref, out_hbm, lines_ref, out_ref, sems):
    half = NROWSG * SLICE
    lines_ref[:half] = in_ref[:, :SLICE, :].reshape(half, SGW)
    lines_ref[half:] = in_ref[:, SLICE:, :].reshape(half, SGW)

    def one(pair, carry):
        cut = pl.ds(pl.multiple_of(pair * 2 * FROWS, 2 * FROWS), 2 * FROWS)
        dims = (((1,), (1,)), ((), ()))
        by_c = lax.dot_general(lines_ref[...], table_ref[0, cut, :], dims, preferred_element_type=F32)
        by_s = lax.dot_general(lines_ref[...], table_ref[1, cut, :], dims, preferred_element_type=F32)
        for k in range(2):
            f = 2 * pair + k
            lanes = slice(k * FROWS, (k + 1) * FROWS)
            acc_re = jnp.zeros((SLICE, FROWS), F32)
            acc_im = jnp.zeros((SLICE, FROWS), F32)
            for r in range(NROWSG):
                top = slice(r * SLICE, (r + 1) * SLICE)
                low = slice(half + r * SLICE, half + (r + 1) * SLICE)
                re = by_c[top, lanes] - by_s[low, lanes]
                im = by_c[low, lanes] + by_s[top, lanes]
                c = c_ref[f, r : r + 1, :]
                s = s_ref[f, r : r + 1, :]
                acc_re = acc_re + (re * c - im * s)
                acc_im = acc_im + (im * c + re * s)
            lower = iota((SLICE, FROWS), 1) < HALF
            out_ref[0, f] = jnp.where(lower, acc_re, pltpu.roll(acc_im, HALF, 1)).astype(BF)
            out_ref[1, f] = jnp.where(lower, pltpu.roll(acc_re, HALF, 1), acc_im).astype(BF)
        return carry

    lax.fori_loop(0, FACETS // 2, one, 0, unroll=UNROLL4)
    write_out([(out_ref.at[copy % 2], out_hbm.at[:, copy], sems.at[copy]) for copy in range(NCOL)])


def adjoint(gridded, tables):
    table, c, s = tables
    return pl.pallas_call(
        adjoint_kernel,
        out_shape=jax.ShapeDtypeStruct((FACETS, NCOL, SLICE, FROWS), BF),
        in_specs=[VMEM_SPEC] * 4,
        out_specs=HBM_SPEC,
        scratch_shapes=[
            pltpu.VMEM((2 * NROWSG * SLICE, SGW), BF),
            pltpu.VMEM((2, FACETS, SLICE, FROWS), BF),
            pltpu.SemaphoreType.DMA((NCOL,)),
        ],
        compiler_params=PARAMS,
        name="adjoint",
    )(on_chip(gridded), on_chip(c), on_chip(s), on_chip(table))


def visibility_kernel(counts_ref, obs_ref, weight_ref, in_ref, ku_ref, kv_ref, gridded_hbm, res_ref, acc_ref, gridded_ref, sem):
    count = counts_ref[0, lax.axis_index("facet")]
    grid = [in_ref[:, half * SLICE : (half + 1) * SLICE, :].reshape(SGW, SGW) for half in range(2)]
    for part in range(VCAP // VBLOCK):
        cut = slice(part * VBLOCK, (part + 1) * VBLOCK)
        live = part * VBLOCK + iota((1, VBLOCK), 1) < count
        weight = weight_ref[:, cut].astype(F32)
        for half in range(2):
            sampled = jnp.dot(grid[half], ku_ref[:, cut], preferred_element_type=F32)
            predicted = jnp.sum(sampled * kv_ref[:, cut].astype(F32), axis=0, keepdims=True)
            observed = obs_ref[half : half + 1, cut].astype(F32)
            residual = jnp.where(live, weight * (observed - predicted), 0.0)
            res_ref[half : half + 1, cut] = residual
            weighted = (residual * kv_ref[:, cut].astype(F32)).astype(BF)
            total = lax.dot_general(
                weighted, ku_ref[:, cut], (((1,), (1,)), ((), ())), preferred_element_type=F32
            )
            if part:
                total = total + acc_ref[half]
            if part + 1 < VCAP // VBLOCK:
                acc_ref[half] = total
            else:
                lines = total.astype(BF).reshape(FACETS, SLICE, SGW)
                gridded_ref[:, half * SLICE : (half + 1) * SLICE, :] = lines
    write_out([(gridded_ref, gridded_hbm, sem)])


def visibilities(counts, obs, weight, grid, tables):
    return pl.pallas_call(
        visibility_kernel,
        out_shape=(
            jax.ShapeDtypeStruct((FACETS, 2 * SLICE, SGW), BF),
            jax.ShapeDtypeStruct((2, VCAP), F32),
        ),
        in_specs=[SMEM_SPEC] + [VMEM_SPEC] * 5,
        out_specs=(HBM_SPEC, VMEM_SPEC),
        scratch_shapes=[
            pltpu.VMEM((2, SGW, SGW), F32),
            pltpu.VMEM((FACETS, 2 * SLICE, SGW), BF),
            pltpu.SemaphoreType.DMA,
        ],
        compiler_params=PARAMS,
        name="visibilities",
    )(counts, obs, weight, on_chip(grid), *map(on_chip, tables))


def dirichlet(distance, pixel_start):
    distance = ((distance & (NIMG - 1)) ^ (NIMG // 2)) - NIMG // 2
    top = cos_sin((distance * (NIMG // (NIMG // FW * 2))) & (NIMG - 1))[1]
    bottom = cos_sin(distance, 17)[1]
    ratio = jnp.where(distance == 0, float(FW), top / jnp.where(distance == 0, 1.0, bottom))
    c, s = cos_sin((distance * (2 * pixel_start + FW - 1)) & (2 * NIMG - 1), 17)
    return c * ratio, s * ratio


def gram_kernel(step_ref, starts_ref, column_ref, offsets_ref, mine_ref, theirs_ref, first_ref, out_hbm, flip_ref, v_ref, out_ref, sem):
    wide = 2 * SGW
    pixel_start = offsets_ref[1, lax.axis_index("facet")]
    own = column_ref[0]
    row = iota((NCOL, wide), 0)
    starts = jnp.zeros((NCOL, wide), I32)
    for c in range(NCOL):
        starts = jnp.where(row == c, starts_ref[c], starts)
    lane = iota((NCOL, wide), 1)
    v_ref[0], v_ref[1] = dirichlet(starts - own + (lane - (SGW - 1)), pixel_start)
    v_ref[2], v_ref[3] = dirichlet(starts + own + (2 * (SGW - 1) - lane), pixel_start)
    anti = (iota((SGW, SGW), 0) + iota((SGW, SGW), 1)) == SGW - 1
    flip_ref[...] = jnp.where(anti, 1.0, 0.0).astype(BF)
    totals = [None] * 4
    for c in range(NCOL):
        lines = [half_ref[:, c].reshape(SGW, FROWS) for half_ref in (mine_ref, theirs_ref)]
        lines = jnp.concatenate(lines, axis=1)
        turned = jnp.dot(flip_ref[...], lines, preferred_element_type=F32).astype(BF)
        for k in range(4):
            spread = jnp.broadcast_to(v_ref[k, c : c + 1, :], (SGW, wide))
            band = pltpu.roll(spread, SGW + 1, 1, stride=1, stride_axis=0)[:, :SGW].astype(BF)
            term = jnp.dot(band, lines if k < 2 else turned, preferred_element_type=F32)
            totals[k] = term if c == 0 else totals[k] + term
    scale = step_ref[0] * (0.5 * NORM)
    p1, p2, p3, p4 = totals
    upper = (lax.axis_index("sub") & 1) == 1
    left = iota((SGW, FROWS), 1) < HALF

    def joined(straight, crossed):
        mine, theirs = [
            straight[:, k * FROWS : (k + 1) * FROWS] + pltpu.roll(crossed[:, k * FROWS : (k + 1) * FROWS], HALF, 1)
            for k in range(2)
        ]
        low = jnp.where(upper, theirs, mine)
        high = jnp.where(upper, mine, theirs)
        return jnp.where(left, low, pltpu.roll(high, HALF, 1))

    re = joined(p1 + p3, -(p2 + p4))
    im = joined(p2 - p4, p1 - p3)
    first = first_ref[...].astype(F32)
    out_ref[:, :SLICE, :] = (first[:, :SLICE] + (scale * re).reshape(FACETS, SLICE, FROWS)).astype(BF)
    out_ref[:, SLICE:, :] = (first[:, SLICE:] + (scale * im).reshape(FACETS, SLICE, FROWS)).astype(BF)
    write_out([(out_ref, out_hbm, sem)])


def gram(steps, column_starts, column_start, offsets, mine, theirs, first):
    shape = (FACETS, NCOL, SLICE, FROWS)
    return pl.pallas_call(
        gram_kernel,
        out_shape=jax.ShapeDtypeStruct((FACETS, 2 * SLICE, FROWS), BF),
        in_specs=[SMEM_SPEC] * 4 + [VMEM_SPEC] * 3,
        out_specs=HBM_SPEC,
        scratch_shapes=[
            pltpu.VMEM((SGW, SGW), BF),
            pltpu.VMEM((4, NCOL, 2 * SGW), F32),
            pltpu.VMEM((FACETS, 2 * SLICE, FROWS), BF),
            pltpu.SemaphoreType.DMA,
        ],
        compiler_params=PARAMS,
        name="gram",
    )(steps, column_starts, column_start, offsets, on_chip(mine.reshape(shape)), on_chip(theirs.reshape(shape)), first)


def update_kernel(step_ref, adj0_ref, adj1_ref, table_hbm, pc_ref, ps_ref, out_ref, table_ref, both_ref, even_ref, odd_ref, sem):
    part = pl.program_id(0)
    fetch = pltpu.make_async_copy(table_hbm, table_ref, sem)

    def turn(group, target_ref):
        re = both_ref[:HALF, :]
        im = both_ref[HALF:, :]
        for p in range(PAIR5):
            pc = pc_ref[pl.ds(group * PAIR5 + p, 1), :]
            ps = ps_ref[pl.ds(group * PAIR5 + p, 1), :]
            lines = slice(p * HALF, (p + 1) * HALF)
            target_ref[lines, :COLUMNS] = (re * pc - im * ps).astype(BF)
            target_ref[lines, COLUMNS:] = (im * pc + re * ps).astype(BF)

    def put(place, source_ref):
        gradient = jnp.dot(source_ref[...], table_ref[...], preferred_element_type=F32).astype(BF)
        for p in range(PAIR5):
            left = (place * PAIR5 + p) * STEP5
            out_ref[:, left : left + STEP5] = gradient[p * HALF : (p + 1) * HALF]

    @pl.when(part == 0)
    def _():
        fetch.start()
        first = step_ref[0] * NORM
        second = step_ref[1] * NORM
        group = NCOL * SLICE
        for j in range(FACETS):
            lines0 = adj0_ref[j * NCOL : (j + 1) * NCOL].reshape(group, FROWS).astype(F32)
            lines1 = adj1_ref[j * NCOL : (j + 1) * NCOL].reshape(group, FROWS).astype(F32)
            both_ref[:, j * group : (j + 1) * group] = (first * lines0 + second * lines1).T
        turn(0, even_ref)
        fetch.wait()

    turn(2 * part + 1, odd_ref)
    put(0, even_ref)
    turn(jnp.minimum(2 * part + 2, HIGH5 // PAIR5 - 2), even_ref)
    put(1, odd_ref)


def update(steps, adj0, adj1, tables):
    table, pc, ps = tables
    return pl.pallas_call(
        update_kernel,
        grid=(HIGH5 // PAIR5 // 2,),
        out_shape=jax.ShapeDtypeStruct((HALF, FW), BF),
        in_specs=[SMEM_SPEC, VMEM_SPEC, VMEM_SPEC, HBM_SPEC, VMEM_SPEC, VMEM_SPEC],
        out_specs=pl.BlockSpec((HALF, 2 * PAIR5 * STEP5), lambda i: (0, i)),
        scratch_shapes=[
            pltpu.VMEM((2 * COLUMNS, STEP5), BF),
            pltpu.VMEM((FROWS, COLUMNS), F32),
            pltpu.VMEM((PAIR5 * HALF, 2 * COLUMNS), BF),
            pltpu.VMEM((PAIR5 * HALF, 2 * COLUMNS), BF),
            pltpu.SemaphoreType.DMA,
        ],
        compiler_params=WIDE_PARAMS,
        name="update",
    )(steps, on_chip(adj0), on_chip(adj1), off_chip(table), on_chip(pc), on_chip(ps))


def step_kernel(mine_ref, theirs_ref, model_ref, out_ref):
    upper = (lax.axis_index("sub") & 1) == 1
    mine = mine_ref[...].astype(F32)
    theirs = theirs_ref[...].astype(F32)
    out_ref[:HALF] = model_ref[:HALF] + jnp.where(upper, theirs, mine)
    out_ref[HALF:] = model_ref[HALF:] + jnp.where(upper, mine, theirs)


def take_step(mine, theirs, model):
    part = pl.BlockSpec((HALF, FW // PARTS7), lambda i: (0, i))
    wide = pl.BlockSpec((FROWS, FW // PARTS7), lambda i: (0, i))
    return pl.pallas_call(
        step_kernel,
        grid=(PARTS7,),
        out_shape=jax.ShapeDtypeStruct((FROWS, FW), F32),
        in_specs=[part, part, wide],
        out_specs=wide,
        compiler_params=PARAMS,
        name="take_step",
    )(mine, theirs, off_chip(model))


def update_table_kernel(starts_ref, offsets_ref, table_hbm, pc_ref, ps_ref, table_ref, base_ref, turn_ref, sem):
    group = NCOL * SLICE
    line = iota((group, STEP5), 0)
    freq = line & (SLICE - 1)
    for c in range(NCOL):
        freq = freq + jnp.where((line >> 4) == c, starts_ref[c], 0)
    base_ref[0], base_ref[1] = phase(freq, iota((group, STEP5), 1))
    turn_ref[0], turn_ref[1] = phase(SLICE * iota((FACETS, STEP5), 0), iota((FACETS, STEP5), 1))

    def one(j, carry):
        c = turn_ref[0, pl.ds(j, 1), :]
        s = turn_ref[1, pl.ds(j, 1), :]
        cut = pl.ds(pl.multiple_of(j * group, group), group)
        table_ref[cut, :] = (base_ref[0] * c - base_ref[1] * s).astype(BF)
        cut = pl.ds(pl.multiple_of(COLUMNS + j * group, group), group)
        table_ref[cut, :] = (-(base_ref[1] * c + base_ref[0] * s)).astype(BF)
        return carry

    lax.fori_loop(0, FACETS, one, 0)
    lane = iota((HIGH5, COLUMNS), 1)
    freq = SLICE * (lane >> 7) + (lane & (SLICE - 1))
    for c in range(NCOL):
        freq = freq + jnp.where(((lane >> 4) & (NCOL - 1)) == c, starts_ref[c], 0)
    pixel_start = offsets_ref[1, lax.axis_index("facet")]
    pc_ref[...], ps_ref[...] = phase(freq, pixel_start + STEP5 * iota((HIGH5, COLUMNS), 0))
    write_out([(table_ref, table_hbm, sem)])


def update_tables(column_starts, offsets):
    return pl.pallas_call(
        update_table_kernel,
        out_shape=(
            pltpu.HBM((2 * COLUMNS, STEP5), BF),
            pltpu.VMEM((HIGH5, COLUMNS), F32),
            pltpu.VMEM((HIGH5, COLUMNS), F32),
        ),
        in_specs=[SMEM_SPEC, SMEM_SPEC],
        out_specs=(HBM_SPEC, VMEM_SPEC, VMEM_SPEC),
        scratch_shapes=[
            pltpu.VMEM((2 * COLUMNS, STEP5), BF),
            pltpu.VMEM((2, NCOL * SLICE, STEP5), F32),
            pltpu.VMEM((2, FACETS, STEP5), F32),
            pltpu.SemaphoreType.DMA,
        ],
        compiler_params=PARAMS,
        name="update_tables",
    )(column_starts, offsets)


def exchange(value):
    return lax.all_to_all(value, "facet", split_axis=0, concat_axis=0, tiled=True)


def other_core(value):
    return lax.ppermute(value, "sub", [(i, i ^ 1) for i in range(NCOL)])


def to_facets(value):
    copies = value.reshape(FACETS * NCOL, *value.shape[2:])
    return lax.all_to_all(copies, ("facet", "sub"), split_axis=0, concat_axis=0, tiled=True)


def local(
    model_image,
    step_sizes,
    facet_offsets,
    col_offsets,
    row_offsets,
    counts,
    vis_uv,
    vis_obs,
    vis_weight,
):
    lines = lax.optimization_barrier(jnp.broadcast_to(col_offsets[:, None], (8, 128)))
    column_starts = lax.optimization_barrier(lax.all_gather(lines, "sub", axis=0, tiled=True))[::8, 0]
    uv = vis_uv.reshape(2, VCAP)
    obs = vis_obs.reshape(2, VCAP)
    weight = vis_weight.reshape(1, VCAP)
    model = model_image[0]
    first = section(col_offsets, facet_offsets, model)
    tables = cycle_tables(facet_offsets, row_offsets, uv)
    rows, kernels = tables[:3], tables[3:]
    grid = exchange(grids(exchange(first), rows))
    gridded, residual = visibilities(counts, obs, weight, grid, kernels)
    adj0 = to_facets(adjoint(exchange(gridded), rows))
    adj0, column_starts = lax.optimization_barrier((adj0, column_starts))
    second = gram(step_sizes, column_starts, col_offsets, facet_offsets, adj0, other_core(adj0), first)
    grid = exchange(grids(exchange(second), rows))
    gridded, residual = visibilities(counts, obs, weight, grid, kernels)
    adj1 = to_facets(adjoint(exchange(gridded), rows))
    tables = update_tables(column_starts, facet_offsets)
    step = update(step_sizes, adj0, adj1, tables)
    model = take_step(step, other_core(step), model)
    return model[None], residual.reshape(2, 1, 1, VCAP)


def solution(mesh):
    in_specs = (
        P("facet", None, None),
        P(),
        P(),
        P("sub"),
        P("sub", None),
        P("sub", None),
        P(None, "sub", "facet", None),
        P(None, "sub", "facet", None),
        P("sub", "facet", None),
    )
    out_specs = (P("facet", None, None), P(None, "sub", "facet", None))
    return jax.shard_map(local, mesh=mesh, in_specs=in_specs, out_specs=out_specs, check_vma=False)
```

```python
import math

import jax
import jax.numpy as jnp
from jax import lax
from jax.experimental import pallas as pl
from jax.experimental.pallas import tpu as pltpu
from jax.sharding import PartitionSpec as P

NIMG = 65536
FW = 8192
FROWS = 128
SGW = 256
VCAP = 4096
OS = 8
KSUP = 4
FACETS = 16
NCOL = 8
NROWSG = 16
SLICE = SGW // FACETS
COLUMNS = NCOL * SGW

STEP1 = 256
HIGH1 = FW // STEP1
PARTS1 = 4
GROUP1 = 4
ROWS1 = 32
STEP5 = 512
HIGH5 = FW // STEP5
PAIR5 = 4
HALF = FROWS // 2
PARTS7 = 2
VBLOCK = 1024
CHUNK = 4
UNROLL4 = 8

BF = jnp.bfloat16
F32 = jnp.float32
I32 = jnp.int32
NORM = 1.0 / math.sqrt(FACETS * FROWS * FW)
PARAMS = pltpu.CompilerParams(vmem_limit_bytes=16 << 20)
WIDE_PARAMS = pltpu.CompilerParams(vmem_limit_bytes=24 << 20)
SMEM_SPEC = pl.BlockSpec(memory_space=pltpu.SMEM)
VMEM_SPEC = pl.BlockSpec(memory_space=pltpu.VMEM)
HBM_SPEC = pl.BlockSpec(memory_space=pltpu.HBM)


def cos_sin(index, bits=16):
    quadrant = (index + (1 << (bits - 3))) >> (bits - 2)
    angle = (index - (quadrant << (bits - 2))).astype(F32) * (2.0 * math.pi / (1 << bits))
    square = angle * angle
    sine = angle * (1.0 + square * (-1.0 / 6 + square * (1.0 / 120 + square * (-1.0 / 5040 + square / 362880))))
    cosine = 1.0 + square * (-0.5 + square * (1.0 / 24 + square * (-1.0 / 720 + square / 40320)))
    swapped = (quadrant & 1) != 0
    c = jnp.where(swapped, sine, cosine)
    s = jnp.where(swapped, cosine, sine)
    c = jnp.where(((quadrant + 1) & 2) != 0, -c, c)
    s = jnp.where((quadrant & 2) != 0, -s, s)
    return c, s


def phase(frequency, pixel):
    return cos_sin((frequency * pixel) & (NIMG - 1))


def on_chip(value):
    return pltpu.with_memory_space_constraint(value, pltpu.VMEM)


def off_chip(value):
    return pltpu.with_memory_space_constraint(value, pltpu.HBM)


def write_out(pairs):
    copies = [pltpu.make_async_copy(source, target, sem) for source, target, sem in pairs]
    for copy in copies:
        copy.start()
    for copy in copies:
        copy.wait()


def iota(shape, dim):
    return lax.broadcasted_iota(I32, shape, dim)


def column_of(ref, count, lanes):
    row = iota((count, lanes), 0)
    value = jnp.zeros((count, lanes), I32)
    for i in range(count):
        value = jnp.where(row == i, ref[i], value)
    return value


def section_kernel(column_ref, offsets_ref, model_hbm, out_hbm, model_ref, table_ref, pc_ref, ps_ref, block_ref, acc_ref, out_ref, sems, sem):
    wide = FW // PARTS1
    fetches = []
    for part in range(PARTS1):
        cut = pl.ds(part * wide, wide)
        fetches.append(pltpu.make_async_copy(model_hbm.at[:, cut], model_ref.at[:, cut], sems.at[part]))
        fetches[-1].start()
    column_start = column_ref[0]
    pixel_start = offsets_ref[1, lax.axis_index("facet")]
    freq = column_start + iota((STEP1, SGW), 1)
    c, s = phase(freq, iota((STEP1, SGW), 0))
    table_ref[:, :SGW] = c.astype(BF)
    table_ref[:, SGW:] = (-s).astype(BF)
    freq = column_start + iota((HIGH1, SGW), 1)
    pc_ref[...], ps_ref[...] = phase(freq, pixel_start + STEP1 * iota((HIGH1, SGW), 0))
    for first in range(0, HIGH1, GROUP1):
        if first % (HIGH1 // PARTS1) == 0:
            fetches[first // (HIGH1 // PARTS1)].wait()
        for k in range(GROUP1):
            cut = slice((first + k) * STEP1, (first + k + 1) * STEP1)
            block_ref[k * FROWS : (k + 1) * FROWS] = model_ref[:, cut].astype(BF)
        product = jnp.dot(block_ref[...], table_ref[...], preferred_element_type=F32)
        for row in range(0, FROWS, ROWS1):
            lines = slice(row, row + ROWS1)
            acc_re = acc_ref[0, lines, :] if first else 0.0
            acc_im = acc_ref[1, lines, :] if first else 0.0
            for k in range(GROUP1):
                re = product[k * FROWS + row : k * FROWS + row + ROWS1, :SGW]
                im = product[k * FROWS + row : k * FROWS + row + ROWS1, SGW:]
                pc = pc_ref[first + k : first + k + 1, :]
                ps = ps_ref[first + k : first + k + 1, :]
                acc_re = acc_re + (re * pc + im * ps)
                acc_im = acc_im + (im * pc - re * ps)
            acc_ref[0, lines, :] = acc_re
            acc_ref[1, lines, :] = acc_im
    out_ref[:, :SLICE, :] = acc_ref[0].T.astype(BF).reshape(FACETS, SLICE, FROWS)
    out_ref[:, SLICE:, :] = acc_ref[1].T.astype(BF).reshape(FACETS, SLICE, FROWS)
    write_out([(out_ref, out_hbm, sem)])


def section(column_start, offsets, model):
    return pl.pallas_call(
        section_kernel,
        out_shape=jax.ShapeDtypeStruct((FACETS, 2 * SLICE, FROWS), BF),
        in_specs=[SMEM_SPEC, SMEM_SPEC, HBM_SPEC],
        out_specs=HBM_SPEC,
        scratch_shapes=[
            pltpu.VMEM((FROWS, FW), F32),
            pltpu.VMEM((STEP1, 2 * SGW), BF),
            pltpu.VMEM((HIGH1, SGW), F32),
            pltpu.VMEM((HIGH1, SGW), F32),
            pltpu.VMEM((GROUP1 * FROWS, STEP1), BF),
            pltpu.VMEM((2, FROWS, SGW), F32),
            pltpu.VMEM((FACETS, 2 * SLICE, FROWS), BF),
            pltpu.SemaphoreType.DMA((PARTS1,)),
            pltpu.SemaphoreType.DMA,
        ],
        compiler_params=PARAMS,
        name="section",
    )(column_start, offsets, off_chip(model))


def kernel_columns(position):
    cells = iota((SGW, position.shape[1]), 0) * OS + OS // 2
    offset = cells - position
    distance = offset.astype(F32) * (1.0 / OS)
    inside = jnp.abs(offset) <= KSUP * OS
    return jnp.where(inside, jnp.exp(-0.5 * distance * distance), 0.0).astype(BF)


def row_table_kernel(offsets_ref, rows_ref, table_ref, c_ref, s_ref, base_ref, turn_ref):
    base_ref[0], base_ref[1] = phase(iota((FROWS, SGW), 1), iota((FROWS, SGW), 0))
    row = iota((FACETS, SGW), 0)
    start = jnp.zeros((FACETS, SGW), I32)
    for f in range(FACETS):
        start = jnp.where(row == f, offsets_ref[0, f], start)
    turn_ref[0], turn_ref[1] = phase(iota((FACETS, SGW), 1), start)
    row = iota((NROWSG, FROWS), 0)
    freq = jnp.zeros((NROWSG, FROWS), I32)
    for r in range(NROWSG):
        freq = jnp.where(row == r, rows_ref[0, r], freq)

    def one(f, carry):
        cf = turn_ref[0, pl.ds(f, 1), :]
        sf = turn_ref[1, pl.ds(f, 1), :]
        lines = pl.ds(pl.multiple_of(f * FROWS, FROWS), FROWS)
        table_ref[0, lines, :] = (base_ref[0] * cf - base_ref[1] * sf).astype(BF)
        table_ref[1, lines, :] = (base_ref[1] * cf + base_ref[0] * sf).astype(BF)
        c_ref[f], s_ref[f] = phase(freq, offsets_ref[0, f] + iota((NROWSG, FROWS), 1))
        return carry

    lax.fori_loop(0, FACETS, one, 0)


def row_tables(offsets, rows):
    return pl.pallas_call(
        row_table_kernel,
        out_shape=(
            pltpu.VMEM((2, FACETS * FROWS, SGW), BF),
            pltpu.VMEM((FACETS, NROWSG, FROWS), F32),
            pltpu.VMEM((FACETS, NROWSG, FROWS), F32),
        ),
        in_specs=[SMEM_SPEC, SMEM_SPEC],
        out_specs=(VMEM_SPEC,) * 3,
        scratch_shapes=[
            pltpu.VMEM((2, FROWS, SGW), F32),
            pltpu.VMEM((2, FACETS, SGW), F32),
        ],
        compiler_params=PARAMS,
        name="row_tables",
    )(offsets, rows)


def grid_kernel(in_ref, c_ref, s_ref, table_ref, out_hbm, turned_ref, out_ref, sem):
    half = NROWSG * SLICE
    for f in range(FACETS):
        re = in_ref[f, :SLICE, :].astype(F32)
        im = in_ref[f, SLICE:, :].astype(F32)
        cut = slice(f * FROWS, (f + 1) * FROWS)
        for r in range(NROWSG):
            c = c_ref[f, r : r + 1, :]
            s = s_ref[f, r : r + 1, :]
            turned_ref[r * SLICE : (r + 1) * SLICE, cut] = (re * c + im * s).astype(BF)
            turned_ref[half + r * SLICE : half + (r + 1) * SLICE, cut] = (im * c - re * s).astype(BF)
    by_c = jnp.dot(turned_ref[...], table_ref[0], preferred_element_type=F32)
    by_s = jnp.dot(turned_ref[...], table_ref[1], preferred_element_type=F32)
    re = (NORM * (by_c[:half] + by_s[half:])).astype(BF)
    im = (NORM * (by_c[half:] - by_s[:half])).astype(BF)
    out_ref[:, :SLICE, :] = re.reshape(NROWSG, SLICE, SGW)
    out_ref[:, SLICE:, :] = im.reshape(NROWSG, SLICE, SGW)
    write_out([(out_ref, out_hbm, sem)])


def grids(sections, tables):
    table, c, s = tables
    return pl.pallas_call(
        grid_kernel,
        out_shape=jax.ShapeDtypeStruct((NROWSG, 2 * SLICE, SGW), BF),
        in_specs=[VMEM_SPEC] * 4,
        out_specs=HBM_SPEC,
        scratch_shapes=[
            pltpu.VMEM((2 * NROWSG * SLICE, FACETS * FROWS), BF),
            pltpu.VMEM((NROWSG, 2 * SLICE, SGW), BF),
            pltpu.SemaphoreType.DMA,
        ],
        compiler_params=PARAMS,
        name="grids",
    )(on_chip(sections), on_chip(c), on_chip(s), on_chip(table))


def adjoint_kernel(in_ref, c_ref, s_ref, table_ref, out_hbm, lines_ref, out_ref, sems):
    half = NROWSG * SLICE
    lines_ref[:half] = in_ref[:, :SLICE, :].reshape(half, SGW)
    lines_ref[half:] = in_ref[:, SLICE:, :].reshape(half, SGW)

    def one(pair, carry):
        cut = pl.ds(pl.multiple_of(pair * 2 * FROWS, 2 * FROWS), 2 * FROWS)
        dims = (((1,), (1,)), ((), ()))
        by_c = lax.dot_general(lines_ref[...], table_ref[0, cut, :], dims, preferred_element_type=F32)
        by_s = lax.dot_general(lines_ref[...], table_ref[1, cut, :], dims, preferred_element_type=F32)
        for k in range(2):
            f = 2 * pair + k
            lanes = slice(k * FROWS, (k + 1) * FROWS)
            acc_re = jnp.zeros((SLICE, FROWS), F32)
            acc_im = jnp.zeros((SLICE, FROWS), F32)
            for r in range(NROWSG):
                top = slice(r * SLICE, (r + 1) * SLICE)
                low = slice(half + r * SLICE, half + (r + 1) * SLICE)
                re = by_c[top, lanes] - by_s[low, lanes]
                im = by_c[low, lanes] + by_s[top, lanes]
                c = c_ref[f, r : r + 1, :]
                s = s_ref[f, r : r + 1, :]
                acc_re = acc_re + (re * c - im * s)
                acc_im = acc_im + (im * c + re * s)
            lower = iota((SLICE, FROWS), 1) < HALF
            out_ref[0, f] = jnp.where(lower, acc_re, pltpu.roll(acc_im, HALF, 1)).astype(BF)
            out_ref[1, f] = jnp.where(lower, pltpu.roll(acc_re, HALF, 1), acc_im).astype(BF)
        return carry

    lax.fori_loop(0, FACETS // 2, one, 0, unroll=UNROLL4)
    write_out([(out_ref.at[copy % 2], out_hbm.at[:, copy], sems.at[copy]) for copy in range(NCOL)])


def adjoint(gridded, tables):
    table, c, s = tables
    return pl.pallas_call(
        adjoint_kernel,
        out_shape=jax.ShapeDtypeStruct((FACETS, NCOL, SLICE, FROWS), BF),
        in_specs=[VMEM_SPEC] * 4,
        out_specs=HBM_SPEC,
        scratch_shapes=[
            pltpu.VMEM((2 * NROWSG * SLICE, SGW), BF),
            pltpu.VMEM((2, FACETS, SLICE, FROWS), BF),
            pltpu.SemaphoreType.DMA((NCOL,)),
        ],
        compiler_params=PARAMS,
        name="adjoint",
    )(on_chip(gridded), on_chip(c), on_chip(s), on_chip(table))


def visibility_pass(counts_ref, obs_ref, weight_ref, in_ref, kernels, gridded_hbm, res_ref, acc_ref, gridded_ref, sem):
    count = counts_ref[0, lax.axis_index("facet")]
    grid = [in_ref[:, half * SLICE : (half + 1) * SLICE, :].reshape(SGW, SGW) for half in range(2)]
    for part in range(VCAP // VBLOCK):
        cut = slice(part * VBLOCK, (part + 1) * VBLOCK)
        ku, kv = kernels(cut)
        live = part * VBLOCK + iota((1, VBLOCK), 1) < count
        weight = weight_ref[:, cut].astype(F32)
        for half in range(2):
            sampled = jnp.dot(grid[half], ku, preferred_element_type=F32)
            predicted = jnp.sum(sampled * kv.astype(F32), axis=0, keepdims=True)
            observed = obs_ref[half : half + 1, cut].astype(F32)
            residual = jnp.where(live, weight * (observed - predicted), 0.0)
            if res_ref is not None:
                res_ref[half : half + 1, cut] = residual
            weighted = (residual * kv.astype(F32)).astype(BF)
            total = lax.dot_general(
                weighted, ku, (((1,), (1,)), ((), ())), preferred_element_type=F32
            )
            if part:
                total = total + acc_ref[half]
            if part + 1 < VCAP // VBLOCK:
                acc_ref[half] = total
            else:
                lines = total.astype(BF).reshape(FACETS, SLICE, SGW)
                gridded_ref[:, half * SLICE : (half + 1) * SLICE, :] = lines
    write_out([(gridded_ref, gridded_hbm, sem)])


def first_kernel(counts_ref, obs_ref, weight_ref, in_ref, uv_ref, gridded_hbm, ku_ref, kv_ref, acc_ref, gridded_ref, sem):
    def kernels(cut):
        ku_ref[:, cut] = kernel_columns(uv_ref[0:1, cut])
        kv_ref[:, cut] = kernel_columns(uv_ref[1:2, cut])
        return ku_ref[:, cut], kv_ref[:, cut]

    visibility_pass(counts_ref, obs_ref, weight_ref, in_ref, kernels, gridded_hbm, None, acc_ref, gridded_ref, sem)


def last_kernel(counts_ref, obs_ref, weight_ref, in_ref, ku_ref, kv_ref, gridded_hbm, res_ref, acc_ref, gridded_ref, sem):
    def kernels(cut):
        return ku_ref[:, cut], kv_ref[:, cut]

    visibility_pass(counts_ref, obs_ref, weight_ref, in_ref, kernels, gridded_hbm, res_ref, acc_ref, gridded_ref, sem)


VIS_SCRATCH = [
    pltpu.VMEM((2, SGW, SGW), F32),
    pltpu.VMEM((FACETS, 2 * SLICE, SGW), BF),
    pltpu.SemaphoreType.DMA,
]


def first_visibilities(counts, obs, weight, grid, uv):
    return pl.pallas_call(
        first_kernel,
        out_shape=(
            jax.ShapeDtypeStruct((FACETS, 2 * SLICE, SGW), BF),
            pltpu.VMEM((SGW, VCAP), BF),
            pltpu.VMEM((SGW, VCAP), BF),
        ),
        in_specs=[SMEM_SPEC] + [VMEM_SPEC] * 4,
        out_specs=(HBM_SPEC, VMEM_SPEC, VMEM_SPEC),
        scratch_shapes=VIS_SCRATCH,
        compiler_params=PARAMS,
        name="first_visibilities",
    )(counts, obs, weight, on_chip(grid), uv)


def last_visibilities(counts, obs, weight, grid, ku, kv):
    return pl.pallas_call(
        last_kernel,
        out_shape=(
            jax.ShapeDtypeStruct((FACETS, 2 * SLICE, SGW), BF),
            jax.ShapeDtypeStruct((2, VCAP), F32),
        ),
        in_specs=[SMEM_SPEC] + [VMEM_SPEC] * 5,
        out_specs=(HBM_SPEC, VMEM_SPEC),
        scratch_shapes=VIS_SCRATCH,
        compiler_params=PARAMS,
        name="last_visibilities",
    )(counts, obs, weight, on_chip(grid), on_chip(ku), on_chip(kv))


def start_of(starts_ref, column):
    own = lax.axis_index("sub")
    return starts_ref[2 * (((own >> 1) - (column >> 1)) & (NCOL // 2 - 1)) + ((own ^ column) & 1)]


def dirichlet(distance, pixel_start):
    distance = ((distance & (NIMG - 1)) ^ (NIMG // 2)) - NIMG // 2
    top = cos_sin((distance * (NIMG // (NIMG // FW * 2))) & (NIMG - 1))[1]
    bottom = cos_sin(distance, 17)[1]
    ratio = jnp.where(distance == 0, float(FW), top / jnp.where(distance == 0, 1.0, bottom))
    c, s = cos_sin((distance * (2 * pixel_start + FW - 1)) & (2 * NIMG - 1), 17)
    return c * ratio, s * ratio


def gram_kernel(step_ref, starts_ref, column_ref, offsets_ref, mine_ref, theirs_ref, first_ref, out_hbm, flip_ref, v_ref, out_ref, sem):
    wide = 2 * SGW
    pixel_start = offsets_ref[1, lax.axis_index("facet")]
    own = column_ref[0]
    row = iota((NCOL, wide), 0)
    starts = jnp.zeros((NCOL, wide), I32)
    for c in range(NCOL):
        starts = jnp.where(row == c, start_of(starts_ref, c), starts)
    lane = iota((NCOL, wide), 1)
    v_ref[0], v_ref[1] = dirichlet(starts - own + (lane - (SGW - 1)), pixel_start)
    v_ref[2], v_ref[3] = dirichlet(starts + own + (2 * (SGW - 1) - lane), pixel_start)
    anti = (iota((SGW, SGW), 0) + iota((SGW, SGW), 1)) == SGW - 1
    flip_ref[...] = jnp.where(anti, 1.0, 0.0).astype(BF)
    totals = [None] * 4
    for c in range(NCOL):
        lines = [half_ref[:, c].reshape(SGW, FROWS) for half_ref in (mine_ref, theirs_ref)]
        lines = jnp.concatenate(lines, axis=1)
        turned = jnp.dot(flip_ref[...], lines, preferred_element_type=F32).astype(BF)
        for k in range(4):
            spread = jnp.broadcast_to(v_ref[k, c : c + 1, :], (SGW, wide))
            band = pltpu.roll(spread, SGW + 1, 1, stride=1, stride_axis=0)[:, :SGW].astype(BF)
            term = jnp.dot(band, lines if k < 2 else turned, preferred_element_type=F32)
            totals[k] = term if c == 0 else totals[k] + term
    scale = step_ref[0] * (0.5 * NORM)
    p1, p2, p3, p4 = totals
    upper = (lax.axis_index("sub") & 1) == 1
    left = iota((SGW, FROWS), 1) < HALF

    def joined(straight, crossed):
        mine, theirs = [
            straight[:, k * FROWS : (k + 1) * FROWS] + pltpu.roll(crossed[:, k * FROWS : (k + 1) * FROWS], HALF, 1)
            for k in range(2)
        ]
        low = jnp.where(upper, theirs, mine)
        high = jnp.where(upper, mine, theirs)
        return jnp.where(left, low, pltpu.roll(high, HALF, 1))

    re = joined(p1 + p3, -(p2 + p4))
    im = joined(p2 - p4, p1 - p3)
    first = first_ref[...].astype(F32)
    out_ref[:, :SLICE, :] = (first[:, :SLICE] + (scale * re).reshape(FACETS, SLICE, FROWS)).astype(BF)
    out_ref[:, SLICE:, :] = (first[:, SLICE:] + (scale * im).reshape(FACETS, SLICE, FROWS)).astype(BF)
    write_out([(out_ref, out_hbm, sem)])


def gram(steps, column_starts, column_start, offsets, mine, theirs, first):
    shape = (FACETS, NCOL, SLICE, FROWS)
    return pl.pallas_call(
        gram_kernel,
        out_shape=jax.ShapeDtypeStruct((FACETS, 2 * SLICE, FROWS), BF),
        in_specs=[SMEM_SPEC] * 4 + [VMEM_SPEC] * 3,
        out_specs=HBM_SPEC,
        scratch_shapes=[
            pltpu.VMEM((SGW, SGW), BF),
            pltpu.VMEM((4, NCOL, 2 * SGW), F32),
            pltpu.VMEM((FACETS, 2 * SLICE, FROWS), BF),
            pltpu.SemaphoreType.DMA,
        ],
        compiler_params=PARAMS,
        name="gram",
    )(steps, column_starts, column_start, offsets, on_chip(mine.reshape(shape)), on_chip(theirs.reshape(shape)), first)


def update_kernel(step_ref, adj0_ref, adj1_ref, table_hbm, pc_ref, ps_ref, out_ref, table_ref, both_ref, even_ref, odd_ref, sem):
    part = pl.program_id(0)
    fetch = pltpu.make_async_copy(table_hbm, table_ref, sem)

    def turn(group, target_ref):
        re = both_ref[:HALF, :]
        im = both_ref[HALF:, :]
        for p in range(PAIR5):
            pc = pc_ref[pl.ds(group * PAIR5 + p, 1), :]
            ps = ps_ref[pl.ds(group * PAIR5 + p, 1), :]
            lines = slice(p * HALF, (p + 1) * HALF)
            target_ref[lines, :COLUMNS] = (re * pc - im * ps).astype(BF)
            target_ref[lines, COLUMNS:] = (im * pc + re * ps).astype(BF)

    def put(place, source_ref):
        gradient = jnp.dot(source_ref[...], table_ref[...], preferred_element_type=F32).astype(BF)
        for p in range(PAIR5):
            left = (place * PAIR5 + p) * STEP5
            out_ref[:, left : left + STEP5] = gradient[p * HALF : (p + 1) * HALF]

    @pl.when(part == 0)
    def _():
        fetch.start()
        first = step_ref[0] * NORM
        second = step_ref[1] * NORM
        group = NCOL * SLICE
        for j in range(FACETS):
            lines0 = adj0_ref[j * NCOL : (j + 1) * NCOL].reshape(group, FROWS).astype(F32)
            lines1 = adj1_ref[j * NCOL : (j + 1) * NCOL].reshape(group, FROWS).astype(F32)
            both_ref[:, j * group : (j + 1) * group] = (first * lines0 + second * lines1).T
        turn(0, even_ref)
        fetch.wait()

    turn(2 * part + 1, odd_ref)
    put(0, even_ref)
    turn(jnp.minimum(2 * part + 2, HIGH5 // PAIR5 - 2), even_ref)
    put(1, odd_ref)


def update(steps, adj0, adj1, tables):
    table, pc, ps = tables
    return pl.pallas_call(
        update_kernel,
        grid=(HIGH5 // PAIR5 // 2,),
        out_shape=jax.ShapeDtypeStruct((HALF, FW), BF),
        in_specs=[SMEM_SPEC, VMEM_SPEC, VMEM_SPEC, HBM_SPEC, VMEM_SPEC, VMEM_SPEC],
        out_specs=pl.BlockSpec((HALF, 2 * PAIR5 * STEP5), lambda i: (0, i)),
        scratch_shapes=[
            pltpu.VMEM((2 * COLUMNS, STEP5), BF),
            pltpu.VMEM((FROWS, COLUMNS), F32),
            pltpu.VMEM((PAIR5 * HALF, 2 * COLUMNS), BF),
            pltpu.VMEM((PAIR5 * HALF, 2 * COLUMNS), BF),
            pltpu.SemaphoreType.DMA,
        ],
        compiler_params=WIDE_PARAMS,
        name="update",
    )(steps, on_chip(adj0), on_chip(adj1), off_chip(table), on_chip(pc), on_chip(ps))


def step_kernel(mine_ref, theirs_ref, model_ref, out_ref):
    upper = (lax.axis_index("sub") & 1) == 1
    mine = mine_ref[...].astype(F32)
    theirs = theirs_ref[...].astype(F32)
    out_ref[:HALF] = model_ref[:HALF] + jnp.where(upper, theirs, mine)
    out_ref[HALF:] = model_ref[HALF:] + jnp.where(upper, mine, theirs)


def take_step(mine, theirs, model):
    part = pl.BlockSpec((HALF, FW // PARTS7), lambda i: (0, i))
    wide = pl.BlockSpec((FROWS, FW // PARTS7), lambda i: (0, i))
    return pl.pallas_call(
        step_kernel,
        grid=(PARTS7,),
        out_shape=jax.ShapeDtypeStruct((FROWS, FW), F32),
        in_specs=[part, part, wide],
        out_specs=wide,
        compiler_params=PARAMS,
        name="take_step",
    )(mine, theirs, off_chip(model))


def update_table_kernel(starts_ref, offsets_ref, table_hbm, pc_ref, ps_ref, table_ref, base_ref, turn_ref, sem):
    group = NCOL * SLICE
    line = iota((group, STEP5), 0)
    freq = line & (SLICE - 1)
    for c in range(NCOL):
        freq = freq + jnp.where((line >> 4) == c, start_of(starts_ref, c), 0)
    base_ref[0], base_ref[1] = phase(freq, iota((group, STEP5), 1))
    turn_ref[0], turn_ref[1] = phase(SLICE * iota((FACETS, STEP5), 0), iota((FACETS, STEP5), 1))

    def one(j, carry):
        c = turn_ref[0, pl.ds(j, 1), :]
        s = turn_ref[1, pl.ds(j, 1), :]
        cut = pl.ds(pl.multiple_of(j * group, group), group)
        table_ref[cut, :] = (base_ref[0] * c - base_ref[1] * s).astype(BF)
        cut = pl.ds(pl.multiple_of(COLUMNS + j * group, group), group)
        table_ref[cut, :] = (-(base_ref[1] * c + base_ref[0] * s)).astype(BF)
        return carry

    lax.fori_loop(0, FACETS, one, 0)
    lane = iota((HIGH5, COLUMNS), 1)
    freq = SLICE * (lane >> 7) + (lane & (SLICE - 1))
    for c in range(NCOL):
        freq = freq + jnp.where(((lane >> 4) & (NCOL - 1)) == c, start_of(starts_ref, c), 0)
    pixel_start = offsets_ref[1, lax.axis_index("facet")]
    pc_ref[...], ps_ref[...] = phase(freq, pixel_start + STEP5 * iota((HIGH5, COLUMNS), 0))
    write_out([(table_ref, table_hbm, sem)])


def update_tables(column_starts, offsets):
    return pl.pallas_call(
        update_table_kernel,
        out_shape=(
            pltpu.HBM((2 * COLUMNS, STEP5), BF),
            pltpu.VMEM((HIGH5, COLUMNS), F32),
            pltpu.VMEM((HIGH5, COLUMNS), F32),
        ),
        in_specs=[SMEM_SPEC, SMEM_SPEC],
        out_specs=(HBM_SPEC, VMEM_SPEC, VMEM_SPEC),
        scratch_shapes=[
            pltpu.VMEM((2 * COLUMNS, STEP5), BF),
            pltpu.VMEM((2, NCOL * SLICE, STEP5), F32),
            pltpu.VMEM((2, FACETS, STEP5), F32),
            pltpu.SemaphoreType.DMA,
        ],
        compiler_params=PARAMS,
        name="update_tables",
    )(column_starts, offsets)


def exchange(value):
    return lax.all_to_all(value, "facet", split_axis=0, concat_axis=0, tiled=True)


def other_core(value):
    return lax.ppermute(value, "sub", [(i, i ^ 1) for i in range(NCOL)])


def all_starts(own):
    lines = lax.optimization_barrier(jnp.broadcast_to(own[:, None], (8, 128)))
    pair = jnp.concatenate([lines, other_core(lines)], axis=0)
    chips = [pair]
    for away in range(2, NCOL, 2):
        chips.append(lax.ppermute(pair, "sub", [(i, (i + away) % NCOL) for i in range(NCOL)]))
    return jnp.concatenate([chip[::8, 0] for chip in chips])


def to_facets(value):
    copies = value.reshape(FACETS * NCOL, *value.shape[2:])
    return lax.all_to_all(copies, ("facet", "sub"), split_axis=0, concat_axis=0, tiled=True)


def local(
    model_image,
    step_sizes,
    facet_offsets,
    col_offsets,
    row_offsets,
    counts,
    vis_uv,
    vis_obs,
    vis_weight,
):
    column_starts = all_starts(col_offsets)
    uv = vis_uv.reshape(2, VCAP)
    obs = vis_obs.reshape(2, VCAP)
    weight = vis_weight.reshape(1, VCAP)
    model = model_image[0]
    first = section(col_offsets, facet_offsets, model)
    rows = row_tables(facet_offsets, row_offsets)
    grid = exchange(grids(exchange(first), rows))
    gridded, ku, kv = first_visibilities(counts, obs, weight, grid, uv)
    gridded, column_starts = lax.optimization_barrier((gridded, column_starts))
    adj0 = to_facets(adjoint(exchange(gridded), rows))
    second = gram(step_sizes, column_starts, col_offsets, facet_offsets, adj0, other_core(adj0), first)
    grid = exchange(grids(exchange(second), rows))
    gridded, residual = last_visibilities(counts, obs, weight, grid, ku, kv)
    adj1 = to_facets(adjoint(exchange(gridded), rows))
    tables = update_tables(column_starts, facet_offsets)
    step = update(step_sizes, adj0, adj1, tables)
    model = take_step(step, other_core(step), model)
    return model[None], residual.reshape(2, 1, 1, VCAP)


def solution(mesh):
    in_specs = (
        P("facet", None, None),
        P(),
        P(),
        P("sub"),
        P("sub", None),
        P("sub", None),
        P(None, "sub", "facet", None),
        P(None, "sub", "facet", None),
        P("sub", "facet", None),
    )
    out_specs = (P("facet", None, None), P(None, "sub", "facet", None))
    return jax.shard_map(local, mesh=mesh, in_specs=in_specs, out_specs=out_specs, check_vma=False)
```

```python
import math

import jax
import jax.numpy as jnp
from jax import lax
from jax.experimental import pallas as pl
from jax.experimental.pallas import tpu as pltpu
from jax.sharding import PartitionSpec as P

NIMG = 65536
FW = 8192
FROWS = 128
SGW = 256
VCAP = 4096
OS = 8
KSUP = 4
FACETS = 16
NCOL = 8
NROWSG = 16
SLICE = SGW // FACETS
COLUMNS = NCOL * SGW

STEP1 = 256
HIGH1 = FW // STEP1
PARTS1 = 4
GROUP1 = 4
ROWS1 = 32
STEP5 = 512
HIGH5 = FW // STEP5
PAIR5 = 4
HALF = FROWS // 2
PARTS7 = 4
VBLOCK = 1024
CHUNK = 4
UNROLL4 = 8

BF = jnp.bfloat16
F32 = jnp.float32
I32 = jnp.int32
NORM = 1.0 / math.sqrt(FACETS * FROWS * FW)
PARAMS = pltpu.CompilerParams(vmem_limit_bytes=16 << 20)
WIDE_PARAMS = pltpu.CompilerParams(vmem_limit_bytes=24 << 20)
SMEM_SPEC = pl.BlockSpec(memory_space=pltpu.SMEM)
VMEM_SPEC = pl.BlockSpec(memory_space=pltpu.VMEM)
HBM_SPEC = pl.BlockSpec(memory_space=pltpu.HBM)


def cos_sin(index, bits=16):
    quadrant = (index + (1 << (bits - 3))) >> (bits - 2)
    angle = (index - (quadrant << (bits - 2))).astype(F32) * (2.0 * math.pi / (1 << bits))
    square = angle * angle
    sine = angle * (1.0 + square * (-1.0 / 6 + square * (1.0 / 120 + square * (-1.0 / 5040 + square / 362880))))
    cosine = 1.0 + square * (-0.5 + square * (1.0 / 24 + square * (-1.0 / 720 + square / 40320)))
    swapped = (quadrant & 1) != 0
    c = jnp.where(swapped, sine, cosine)
    s = jnp.where(swapped, cosine, sine)
    c = jnp.where(((quadrant + 1) & 2) != 0, -c, c)
    s = jnp.where((quadrant & 2) != 0, -s, s)
    return c, s


def phase(frequency, pixel):
    return cos_sin((frequency * pixel) & (NIMG - 1))


def on_chip(value):
    return pltpu.with_memory_space_constraint(value, pltpu.VMEM)


def off_chip(value):
    return pltpu.with_memory_space_constraint(value, pltpu.HBM)


def write_out(pairs):
    copies = [pltpu.make_async_copy(source, target, sem) for source, target, sem in pairs]
    for copy in copies:
        copy.start()
    for copy in copies:
        copy.wait()


def iota(shape, dim):
    return lax.broadcasted_iota(I32, shape, dim)


def column_of(ref, count, lanes):
    row = iota((count, lanes), 0)
    value = jnp.zeros((count, lanes), I32)
    for i in range(count):
        value = jnp.where(row == i, ref[i], value)
    return value


def section_kernel(column_ref, offsets_ref, model_hbm, out_hbm, model_ref, table_ref, pc_ref, ps_ref, block_ref, acc_ref, out_ref, sems, sem):
    wide = FW // PARTS1
    fetches = []
    for part in range(PARTS1):
        cut = pl.ds(part * wide, wide)
        fetches.append(pltpu.make_async_copy(model_hbm.at[:, cut], model_ref.at[:, cut], sems.at[part]))
        fetches[-1].start()
    column_start = column_ref[0]
    pixel_start = offsets_ref[1, lax.axis_index("facet")]
    freq = column_start + iota((STEP1, SGW), 1)
    c, s = phase(freq, iota((STEP1, SGW), 0))
    table_ref[:, :SGW] = c.astype(BF)
    table_ref[:, SGW:] = (-s).astype(BF)
    freq = column_start + iota((HIGH1, SGW), 1)
    pc_ref[...], ps_ref[...] = phase(freq, pixel_start + STEP1 * iota((HIGH1, SGW), 0))
    for first in range(0, HIGH1, GROUP1):
        if first % (HIGH1 // PARTS1) == 0:
            fetches[first // (HIGH1 // PARTS1)].wait()
        for k in range(GROUP1):
            cut = slice((first + k) * STEP1, (first + k + 1) * STEP1)
            block_ref[k * FROWS : (k + 1) * FROWS] = model_ref[:, cut].astype(BF)
        product = jnp.dot(block_ref[...], table_ref[...], preferred_element_type=F32)
        for row in range(0, FROWS, ROWS1):
            lines = slice(row, row + ROWS1)
            acc_re = acc_ref[0, lines, :] if first else 0.0
            acc_im = acc_ref[1, lines, :] if first else 0.0
            for k in range(GROUP1):
                re = product[k * FROWS + row : k * FROWS + row + ROWS1, :SGW]
                im = product[k * FROWS + row : k * FROWS + row + ROWS1, SGW:]
                pc = pc_ref[first + k : first + k + 1, :]
                ps = ps_ref[first + k : first + k + 1, :]
                acc_re = acc_re + (re * pc + im * ps)
                acc_im = acc_im + (im * pc - re * ps)
            acc_ref[0, lines, :] = acc_re
            acc_ref[1, lines, :] = acc_im
    out_ref[:, :SLICE, :] = acc_ref[0].T.astype(BF).reshape(FACETS, SLICE, FROWS)
    out_ref[:, SLICE:, :] = acc_ref[1].T.astype(BF).reshape(FACETS, SLICE, FROWS)
    write_out([(out_ref, out_hbm, sem)])


def section(column_start, offsets, model):
    return pl.pallas_call(
        section_kernel,
        out_shape=jax.ShapeDtypeStruct((FACETS, 2 * SLICE, FROWS), BF),
        in_specs=[SMEM_SPEC, SMEM_SPEC, HBM_SPEC],
        out_specs=HBM_SPEC,
        scratch_shapes=[
            pltpu.VMEM((FROWS, FW), F32),
            pltpu.VMEM((STEP1, 2 * SGW), BF),
            pltpu.VMEM((HIGH1, SGW), F32),
            pltpu.VMEM((HIGH1, SGW), F32),
            pltpu.VMEM((GROUP1 * FROWS, STEP1), BF),
            pltpu.VMEM((2, FROWS, SGW), F32),
            pltpu.VMEM((FACETS, 2 * SLICE, FROWS), BF),
            pltpu.SemaphoreType.DMA((PARTS1,)),
            pltpu.SemaphoreType.DMA,
        ],
        compiler_params=PARAMS,
        name="section",
    )(column_start, offsets, off_chip(model))


def kernel_columns(position):
    cells = (iota((SGW, position.shape[1]), 0) * OS + OS // 2).astype(F32)
    offset = cells - position.astype(F32)
    square = offset * offset
    value = jnp.exp2(square * (-0.5 / (OS * OS) / math.log(2.0)))
    return jnp.where(square <= float((KSUP * OS) ** 2), value, 0.0).astype(BF)


def row_table_kernel(offsets_ref, rows_ref, table_ref, c_ref, s_ref, base_ref, turn_ref):
    base_ref[0], base_ref[1] = phase(iota((FROWS, SGW), 1), iota((FROWS, SGW), 0))
    row = iota((FACETS, SGW), 0)
    start = jnp.zeros((FACETS, SGW), I32)
    for f in range(FACETS):
        start = jnp.where(row == f, offsets_ref[0, f], start)
    turn_ref[0], turn_ref[1] = phase(iota((FACETS, SGW), 1), start)
    row = iota((NROWSG, FROWS), 0)
    freq = jnp.zeros((NROWSG, FROWS), I32)
    for r in range(NROWSG):
        freq = jnp.where(row == r, rows_ref[0, r], freq)

    def one(f, carry):
        cf = turn_ref[0, pl.ds(f, 1), :]
        sf = turn_ref[1, pl.ds(f, 1), :]
        lines = pl.ds(pl.multiple_of(f * FROWS, FROWS), FROWS)
        table_ref[0, lines, :] = (base_ref[0] * cf - base_ref[1] * sf).astype(BF)
        table_ref[1, lines, :] = (base_ref[1] * cf + base_ref[0] * sf).astype(BF)
        c_ref[f], s_ref[f] = phase(freq, offsets_ref[0, f] + iota((NROWSG, FROWS), 1))
        return carry

    lax.fori_loop(0, FACETS, one, 0)


def row_tables(offsets, rows):
    return pl.pallas_call(
        row_table_kernel,
        out_shape=(
            pltpu.VMEM((2, FACETS * FROWS, SGW), BF),
            pltpu.VMEM((FACETS, NROWSG, FROWS), F32),
            pltpu.VMEM((FACETS, NROWSG, FROWS), F32),
        ),
        in_specs=[SMEM_SPEC, SMEM_SPEC],
        out_specs=(VMEM_SPEC,) * 3,
        scratch_shapes=[
            pltpu.VMEM((2, FROWS, SGW), F32),
            pltpu.VMEM((2, FACETS, SGW), F32),
        ],
        compiler_params=PARAMS,
        name="row_tables",
    )(offsets, rows)


def grid_kernel(in_ref, c_ref, s_ref, table_ref, out_hbm, turned_ref, out_ref, sem):
    half = NROWSG * SLICE
    for f in range(FACETS):
        re = in_ref[f, :SLICE, :].astype(F32)
        im = in_ref[f, SLICE:, :].astype(F32)
        cut = slice(f * FROWS, (f + 1) * FROWS)
        for r in range(NROWSG):
            c = c_ref[f, r : r + 1, :]
            s = s_ref[f, r : r + 1, :]
            turned_ref[r * SLICE : (r + 1) * SLICE, cut] = (re * c + im * s).astype(BF)
            turned_ref[half + r * SLICE : half + (r + 1) * SLICE, cut] = (im * c - re * s).astype(BF)
    by_c = jnp.dot(turned_ref[...], table_ref[0], preferred_element_type=F32)
    by_s = jnp.dot(turned_ref[...], table_ref[1], preferred_element_type=F32)
    re = (NORM * (by_c[:half] + by_s[half:])).astype(BF)
    im = (NORM * (by_c[half:] - by_s[:half])).astype(BF)
    out_ref[:, :SLICE, :] = re.reshape(NROWSG, SLICE, SGW)
    out_ref[:, SLICE:, :] = im.reshape(NROWSG, SLICE, SGW)
    write_out([(out_ref, out_hbm, sem)])


def grids(sections, tables):
    table, c, s = tables
    return pl.pallas_call(
        grid_kernel,
        out_shape=jax.ShapeDtypeStruct((NROWSG, 2 * SLICE, SGW), BF),
        in_specs=[VMEM_SPEC] * 4,
        out_specs=HBM_SPEC,
        scratch_shapes=[
            pltpu.VMEM((2 * NROWSG * SLICE, FACETS * FROWS), BF),
            pltpu.VMEM((NROWSG, 2 * SLICE, SGW), BF),
            pltpu.SemaphoreType.DMA,
        ],
        compiler_params=PARAMS,
        name="grids",
    )(on_chip(sections), on_chip(c), on_chip(s), on_chip(table))


def adjoint_kernel(in_ref, c_ref, s_ref, table_ref, out_hbm, lines_ref, out_ref, sems):
    half = NROWSG * SLICE
    lines_ref[:half] = in_ref[:, :SLICE, :].reshape(half, SGW)
    lines_ref[half:] = in_ref[:, SLICE:, :].reshape(half, SGW)

    def one(pair, carry):
        cut = pl.ds(pl.multiple_of(pair * 2 * FROWS, 2 * FROWS), 2 * FROWS)
        dims = (((1,), (1,)), ((), ()))
        by_c = lax.dot_general(lines_ref[...], table_ref[0, cut, :], dims, preferred_element_type=F32)
        by_s = lax.dot_general(lines_ref[...], table_ref[1, cut, :], dims, preferred_element_type=F32)
        for k in range(2):
            f = 2 * pair + k
            lanes = slice(k * FROWS, (k + 1) * FROWS)
            acc_re = jnp.zeros((SLICE, FROWS), F32)
            acc_im = jnp.zeros((SLICE, FROWS), F32)
            for r in range(NROWSG):
                top = slice(r * SLICE, (r + 1) * SLICE)
                low = slice(half + r * SLICE, half + (r + 1) * SLICE)
                re = by_c[top, lanes] - by_s[low, lanes]
                im = by_c[low, lanes] + by_s[top, lanes]
                c = c_ref[f, r : r + 1, :]
                s = s_ref[f, r : r + 1, :]
                acc_re = acc_re + (re * c - im * s)
                acc_im = acc_im + (im * c + re * s)
            lower = iota((SLICE, FROWS), 1) < HALF
            out_ref[0, f] = jnp.where(lower, acc_re, pltpu.roll(acc_im, HALF, 1)).astype(BF)
            out_ref[1, f] = jnp.where(lower, pltpu.roll(acc_re, HALF, 1), acc_im).astype(BF)
        return carry

    lax.fori_loop(0, FACETS // 2, one, 0, unroll=UNROLL4)
    write_out([(out_ref.at[copy % 2], out_hbm.at[:, copy], sems.at[copy]) for copy in range(NCOL)])


def adjoint(gridded, tables):
    table, c, s = tables
    return pl.pallas_call(
        adjoint_kernel,
        out_shape=jax.ShapeDtypeStruct((FACETS, NCOL, SLICE, FROWS), BF),
        in_specs=[VMEM_SPEC] * 4,
        out_specs=HBM_SPEC,
        scratch_shapes=[
            pltpu.VMEM((2 * NROWSG * SLICE, SGW), BF),
            pltpu.VMEM((2, FACETS, SLICE, FROWS), BF),
            pltpu.SemaphoreType.DMA((NCOL,)),
        ],
        compiler_params=PARAMS,
        name="adjoint",
    )(on_chip(gridded), on_chip(c), on_chip(s), on_chip(table))


def visibility_pass(counts_ref, obs_ref, weight_ref, in_ref, kernels, gridded_hbm, res_ref, acc_ref, gridded_ref, sem):
    count = counts_ref[0, lax.axis_index("facet")]
    grid = [in_ref[:, half * SLICE : (half + 1) * SLICE, :].reshape(SGW, SGW) for half in range(2)]
    for part in range(VCAP // VBLOCK):
        cut = slice(part * VBLOCK, (part + 1) * VBLOCK)
        ku, kv = kernels(cut)
        live = part * VBLOCK + iota((1, VBLOCK), 1) < count
        weight = weight_ref[:, cut].astype(F32)
        for half in range(2):
            sampled = jnp.dot(grid[half], ku, preferred_element_type=F32)
            predicted = jnp.sum(sampled * kv.astype(F32), axis=0, keepdims=True)
            observed = obs_ref[half : half + 1, cut].astype(F32)
            residual = jnp.where(live, weight * (observed - predicted), 0.0)
            if res_ref is not None:
                res_ref[half : half + 1, cut] = residual
            weighted = (residual * kv.astype(F32)).astype(BF)
            total = lax.dot_general(
                weighted, ku, (((1,), (1,)), ((), ())), preferred_element_type=F32
            )
            if part:
                total = total + acc_ref[half]
            if part + 1 < VCAP // VBLOCK:
                acc_ref[half] = total
            else:
                lines = total.astype(BF).reshape(FACETS, SLICE, SGW)
                gridded_ref[:, half * SLICE : (half + 1) * SLICE, :] = lines
    write_out([(gridded_ref, gridded_hbm, sem)])


def first_kernel(counts_ref, obs_ref, weight_ref, in_ref, uv_ref, gridded_hbm, ku_ref, kv_ref, acc_ref, gridded_ref, sem):
    def kernels(cut):
        ku_ref[:, cut] = kernel_columns(uv_ref[0:1, cut])
        kv_ref[:, cut] = kernel_columns(uv_ref[1:2, cut])
        return ku_ref[:, cut], kv_ref[:, cut]

    visibility_pass(counts_ref, obs_ref, weight_ref, in_ref, kernels, gridded_hbm, None, acc_ref, gridded_ref, sem)


def last_kernel(counts_ref, obs_ref, weight_ref, in_ref, ku_ref, kv_ref, gridded_hbm, res_ref, acc_ref, gridded_ref, sem):
    def kernels(cut):
        return ku_ref[:, cut], kv_ref[:, cut]

    visibility_pass(counts_ref, obs_ref, weight_ref, in_ref, kernels, gridded_hbm, res_ref, acc_ref, gridded_ref, sem)


VIS_SCRATCH = [
    pltpu.VMEM((2, SGW, SGW), F32),
    pltpu.VMEM((FACETS, 2 * SLICE, SGW), BF),
    pltpu.SemaphoreType.DMA,
]


def first_visibilities(counts, obs, weight, grid, uv):
    return pl.pallas_call(
        first_kernel,
        out_shape=(
            jax.ShapeDtypeStruct((FACETS, 2 * SLICE, SGW), BF),
            pltpu.VMEM((SGW, VCAP), BF),
            pltpu.VMEM((SGW, VCAP), BF),
        ),
        in_specs=[SMEM_SPEC] + [VMEM_SPEC] * 4,
        out_specs=(HBM_SPEC, VMEM_SPEC, VMEM_SPEC),
        scratch_shapes=VIS_SCRATCH,
        compiler_params=PARAMS,
        name="first_visibilities",
    )(counts, obs, weight, on_chip(grid), uv)


def last_visibilities(counts, obs, weight, grid, ku, kv):
    return pl.pallas_call(
        last_kernel,
        out_shape=(
            jax.ShapeDtypeStruct((FACETS, 2 * SLICE, SGW), BF),
            jax.ShapeDtypeStruct((2, VCAP), F32),
        ),
        in_specs=[SMEM_SPEC] + [VMEM_SPEC] * 5,
        out_specs=(HBM_SPEC, VMEM_SPEC),
        scratch_shapes=VIS_SCRATCH,
        compiler_params=PARAMS,
        name="last_visibilities",
    )(counts, obs, weight, on_chip(grid), on_chip(ku), on_chip(kv))


def start_of(starts_ref, column):
    own = lax.axis_index("sub")
    return starts_ref[2 * (((own >> 1) - (column >> 1)) & (NCOL // 2 - 1)) + ((own ^ column) & 1)]


def dirichlet(distance, pixel_start):
    distance = ((distance & (NIMG - 1)) ^ (NIMG // 2)) - NIMG // 2
    top = cos_sin((distance * (NIMG // (NIMG // FW * 2))) & (NIMG - 1))[1]
    bottom = cos_sin(distance, 17)[1]
    ratio = jnp.where(distance == 0, float(FW), top / jnp.where(distance == 0, 1.0, bottom))
    c, s = cos_sin((distance * (2 * pixel_start + FW - 1)) & (2 * NIMG - 1), 17)
    return c * ratio, s * ratio


def gram_kernel(step_ref, starts_ref, column_ref, offsets_ref, mine_ref, theirs_ref, first_ref, out_hbm, flip_ref, v_ref, out_ref, sem):
    wide = 2 * SGW
    pixel_start = offsets_ref[1, lax.axis_index("facet")]
    own = column_ref[0]
    row = iota((NCOL, wide), 0)
    starts = jnp.zeros((NCOL, wide), I32)
    for c in range(NCOL):
        starts = jnp.where(row == c, start_of(starts_ref, c), starts)
    lane = iota((NCOL, wide), 1)
    v_ref[0], v_ref[1] = dirichlet(starts - own + (lane - (SGW - 1)), pixel_start)
    v_ref[2], v_ref[3] = dirichlet(starts + own + (2 * (SGW - 1) - lane), pixel_start)
    anti = (iota((SGW, SGW), 0) + iota((SGW, SGW), 1)) == SGW - 1
    flip_ref[...] = jnp.where(anti, 1.0, 0.0).astype(BF)
    totals = [None] * 4
    for c in range(NCOL):
        lines = [half_ref[:, c].reshape(SGW, FROWS) for half_ref in (mine_ref, theirs_ref)]
        lines = jnp.concatenate(lines, axis=1)
        turned = jnp.dot(flip_ref[...], lines, preferred_element_type=F32).astype(BF)
        for k in range(4):
            spread = jnp.broadcast_to(v_ref[k, c : c + 1, :], (SGW, wide))
            band = pltpu.roll(spread, SGW + 1, 1, stride=1, stride_axis=0)[:, :SGW].astype(BF)
            term = jnp.dot(band, lines if k < 2 else turned, preferred_element_type=F32)
            totals[k] = term if c == 0 else totals[k] + term
    scale = step_ref[0] * (0.5 * NORM)
    p1, p2, p3, p4 = totals
    upper = (lax.axis_index("sub") & 1) == 1
    left = iota((SGW, FROWS), 1) < HALF

    def joined(straight, crossed):
        mine, theirs = [
            straight[:, k * FROWS : (k + 1) * FROWS] + pltpu.roll(crossed[:, k * FROWS : (k + 1) * FROWS], HALF, 1)
            for k in range(2)
        ]
        low = jnp.where(upper, theirs, mine)
        high = jnp.where(upper, mine, theirs)
        return jnp.where(left, low, pltpu.roll(high, HALF, 1))

    re = joined(p1 + p3, -(p2 + p4))
    im = joined(p2 - p4, p1 - p3)
    first = first_ref[...].astype(F32)
    out_ref[:, :SLICE, :] = (first[:, :SLICE] + (scale * re).reshape(FACETS, SLICE, FROWS)).astype(BF)
    out_ref[:, SLICE:, :] = (first[:, SLICE:] + (scale * im).reshape(FACETS, SLICE, FROWS)).astype(BF)
    write_out([(out_ref, out_hbm, sem)])


def gram(steps, column_starts, column_start, offsets, mine, theirs, first):
    shape = (FACETS, NCOL, SLICE, FROWS)
    return pl.pallas_call(
        gram_kernel,
        out_shape=jax.ShapeDtypeStruct((FACETS, 2 * SLICE, FROWS), BF),
        in_specs=[SMEM_SPEC] * 4 + [VMEM_SPEC] * 3,
        out_specs=HBM_SPEC,
        scratch_shapes=[
            pltpu.VMEM((SGW, SGW), BF),
            pltpu.VMEM((4, NCOL, 2 * SGW), F32),
            pltpu.VMEM((FACETS, 2 * SLICE, FROWS), BF),
            pltpu.SemaphoreType.DMA,
        ],
        compiler_params=PARAMS,
        name="gram",
    )(steps, column_starts, column_start, offsets, on_chip(mine.reshape(shape)), on_chip(theirs.reshape(shape)), first)


def update_kernel(step_ref, adj0_ref, adj1_ref, table_hbm, pc_ref, ps_ref, out_ref, table_ref, both_ref, even_ref, odd_ref, sem):
    part = pl.program_id(0)
    fetch = pltpu.make_async_copy(table_hbm, table_ref, sem)

    def turn(group, target_ref):
        re = both_ref[:HALF, :]
        im = both_ref[HALF:, :]
        for p in range(PAIR5):
            pc = pc_ref[pl.ds(group * PAIR5 + p, 1), :]
            ps = ps_ref[pl.ds(group * PAIR5 + p, 1), :]
            lines = slice(p * HALF, (p + 1) * HALF)
            target_ref[lines, :COLUMNS] = (re * pc - im * ps).astype(BF)
            target_ref[lines, COLUMNS:] = (im * pc + re * ps).astype(BF)

    def put(place, source_ref):
        gradient = jnp.dot(source_ref[...], table_ref[...], preferred_element_type=F32).astype(BF)
        for p in range(PAIR5):
            left = (place * PAIR5 + p) * STEP5
            out_ref[:, left : left + STEP5] = gradient[p * HALF : (p + 1) * HALF]

    @pl.when(part == 0)
    def _():
        fetch.start()
        first = step_ref[0] * NORM
        second = step_ref[1] * NORM
        group = NCOL * SLICE
        for j in range(FACETS):
            lines0 = adj0_ref[j * NCOL : (j + 1) * NCOL].reshape(group, FROWS).astype(F32)
            lines1 = adj1_ref[j * NCOL : (j + 1) * NCOL].reshape(group, FROWS).astype(F32)
            both_ref[:, j * group : (j + 1) * group] = (first * lines0 + second * lines1).T
        turn(0, even_ref)
        fetch.wait()

    turn(2 * part + 1, odd_ref)
    put(0, even_ref)
    turn(jnp.minimum(2 * part + 2, HIGH5 // PAIR5 - 2), even_ref)
    put(1, odd_ref)


def update(steps, adj0, adj1, tables):
    table, pc, ps = tables
    return pl.pallas_call(
        update_kernel,
        grid=(HIGH5 // PAIR5 // 2,),
        out_shape=jax.ShapeDtypeStruct((HALF, FW), BF),
        in_specs=[SMEM_SPEC, VMEM_SPEC, VMEM_SPEC, HBM_SPEC, VMEM_SPEC, VMEM_SPEC],
        out_specs=pl.BlockSpec((HALF, 2 * PAIR5 * STEP5), lambda i: (0, i)),
        scratch_shapes=[
            pltpu.VMEM((2 * COLUMNS, STEP5), BF),
            pltpu.VMEM((FROWS, COLUMNS), F32),
            pltpu.VMEM((PAIR5 * HALF, 2 * COLUMNS), BF),
            pltpu.VMEM((PAIR5 * HALF, 2 * COLUMNS), BF),
            pltpu.SemaphoreType.DMA,
        ],
        compiler_params=WIDE_PARAMS,
        name="update",
    )(steps, on_chip(adj0), on_chip(adj1), off_chip(table), on_chip(pc), on_chip(ps))


def step_kernel(mine_ref, theirs_ref, model_ref, out_hbm, out_ref, sems):
    upper = (lax.axis_index("sub") & 1) == 1
    wide = FW // PARTS7
    sent = []
    for part in range(PARTS7):
        cut = slice(part * wide, (part + 1) * wide)
        mine = mine_ref[:, cut].astype(F32)
        theirs = theirs_ref[:, cut].astype(F32)
        out_ref[:HALF, cut] = model_ref[:HALF, cut] + jnp.where(upper, theirs, mine)
        out_ref[HALF:, cut] = model_ref[HALF:, cut] + jnp.where(upper, mine, theirs)
        lanes = pl.ds(part * wide, wide)
        sent.append(pltpu.make_async_copy(out_ref.at[:, lanes], out_hbm.at[:, lanes], sems.at[part]))
        sent[-1].start()
    for copy in sent:
        copy.wait()


def take_step(mine, theirs, model):
    return pl.pallas_call(
        step_kernel,
        out_shape=jax.ShapeDtypeStruct((FROWS, FW), F32),
        in_specs=[VMEM_SPEC] * 3,
        out_specs=HBM_SPEC,
        scratch_shapes=[pltpu.VMEM((FROWS, FW), F32), pltpu.SemaphoreType.DMA((PARTS7,))],
        compiler_params=PARAMS,
        name="take_step",
    )(on_chip(mine), on_chip(theirs), on_chip(model))


def update_table_kernel(starts_ref, offsets_ref, table_hbm, pc_ref, ps_ref, table_ref, base_ref, turn_ref, sem):
    group = NCOL * SLICE
    line = iota((group, STEP5), 0)
    freq = line & (SLICE - 1)
    for c in range(NCOL):
        freq = freq + jnp.where((line >> 4) == c, start_of(starts_ref, c), 0)
    base_ref[0], base_ref[1] = phase(freq, iota((group, STEP5), 1))
    turn_ref[0], turn_ref[1] = phase(SLICE * iota((FACETS, STEP5), 0), iota((FACETS, STEP5), 1))

    def one(j, carry):
        c = turn_ref[0, pl.ds(j, 1), :]
        s = turn_ref[1, pl.ds(j, 1), :]
        cut = pl.ds(pl.multiple_of(j * group, group), group)
        table_ref[cut, :] = (base_ref[0] * c - base_ref[1] * s).astype(BF)
        cut = pl.ds(pl.multiple_of(COLUMNS + j * group, group), group)
        table_ref[cut, :] = (-(base_ref[1] * c + base_ref[0] * s)).astype(BF)
        return carry

    lax.fori_loop(0, FACETS, one, 0)
    lane = iota((HIGH5, COLUMNS), 1)
    freq = SLICE * (lane >> 7) + (lane & (SLICE - 1))
    for c in range(NCOL):
        freq = freq + jnp.where(((lane >> 4) & (NCOL - 1)) == c, start_of(starts_ref, c), 0)
    pixel_start = offsets_ref[1, lax.axis_index("facet")]
    pc_ref[...], ps_ref[...] = phase(freq, pixel_start + STEP5 * iota((HIGH5, COLUMNS), 0))
    write_out([(table_ref, table_hbm, sem)])


def update_tables(column_starts, offsets):
    return pl.pallas_call(
        update_table_kernel,
        out_shape=(
            pltpu.HBM((2 * COLUMNS, STEP5), BF),
            pltpu.VMEM((HIGH5, COLUMNS), F32),
            pltpu.VMEM((HIGH5, COLUMNS), F32),
        ),
        in_specs=[SMEM_SPEC, SMEM_SPEC],
        out_specs=(HBM_SPEC, VMEM_SPEC, VMEM_SPEC),
        scratch_shapes=[
            pltpu.VMEM((2 * COLUMNS, STEP5), BF),
            pltpu.VMEM((2, NCOL * SLICE, STEP5), F32),
            pltpu.VMEM((2, FACETS, STEP5), F32),
            pltpu.SemaphoreType.DMA,
        ],
        compiler_params=PARAMS,
        name="update_tables",
    )(column_starts, offsets)


def exchange(value):
    return lax.all_to_all(value, "facet", split_axis=0, concat_axis=0, tiled=True)


def other_core(value):
    return lax.ppermute(value, "sub", [(i, i ^ 1) for i in range(NCOL)])


def all_starts(own):
    lines = lax.optimization_barrier(jnp.broadcast_to(own[:, None], (8, 128)))
    pair = jnp.concatenate([lines, other_core(lines)], axis=0)
    chips = [pair]
    for away in range(2, NCOL, 2):
        chips.append(lax.ppermute(pair, "sub", [(i, (i + away) % NCOL) for i in range(NCOL)]))
    return jnp.concatenate([chip[::8, 0] for chip in chips])


def to_facets(value):
    copies = value.reshape(FACETS * NCOL, *value.shape[2:])
    return lax.all_to_all(copies, ("facet", "sub"), split_axis=0, concat_axis=0, tiled=True)


def local(
    model_image,
    step_sizes,
    facet_offsets,
    col_offsets,
    row_offsets,
    counts,
    vis_uv,
    vis_obs,
    vis_weight,
):
    column_starts = all_starts(col_offsets)
    uv = vis_uv.reshape(2, VCAP)
    obs = vis_obs.reshape(2, VCAP)
    weight = vis_weight.reshape(1, VCAP)
    model = model_image[0]
    first = section(col_offsets, facet_offsets, model)
    rows = row_tables(facet_offsets, row_offsets)
    grid = exchange(grids(exchange(first), rows))
    gridded, ku, kv = first_visibilities(counts, obs, weight, grid, uv)
    gridded, column_starts = lax.optimization_barrier((gridded, column_starts))
    adj0 = to_facets(adjoint(exchange(gridded), rows))
    second = gram(step_sizes, column_starts, col_offsets, facet_offsets, adj0, other_core(adj0), first)
    grid = exchange(grids(exchange(second), rows))
    gridded, residual = last_visibilities(counts, obs, weight, grid, ku, kv)
    adj1 = to_facets(adjoint(exchange(gridded), rows))
    tables = update_tables(column_starts, facet_offsets)
    step = update(step_sizes, adj0, adj1, tables)
    model = take_step(step, other_core(step), model)
    return model[None], residual.reshape(2, 1, 1, VCAP)


def solution(mesh):
    in_specs = (
        P("facet", None, None),
        P(),
        P(),
        P("sub"),
        P("sub", None),
        P("sub", None),
        P(None, "sub", "facet", None),
        P(None, "sub", "facet", None),
        P("sub", "facet", None),
    )
    out_specs = (P("facet", None, None), P(None, "sub", "facet", None))
    return jax.shard_map(local, mesh=mesh, in_specs=in_specs, out_specs=out_specs, check_vma=False)
```

```python
import math

import jax
import jax.numpy as jnp
from jax import lax
from jax.experimental import pallas as pl
from jax.experimental.pallas import tpu as pltpu
from jax.sharding import PartitionSpec as P

NIMG = 65536
FW = 8192
FROWS = 128
SGW = 256
VCAP = 4096
OS = 8
KSUP = 4
FACETS = 16
NCOL = 8
NROWSG = 16
SLICE = SGW // FACETS
COLUMNS = NCOL * SGW

STEP1 = 256
HIGH1 = FW // STEP1
PARTS1 = 4
GROUP1 = 4
ROWS1 = 32
STEP5 = 512
HIGH5 = FW // STEP5
PAIR5 = 4
HALF = FROWS // 2
PARTS7 = 4
VBLOCK = 1024
CHUNK = 4
UNROLL4 = 8

BF = jnp.bfloat16
F32 = jnp.float32
I32 = jnp.int32
NORM = 1.0 / math.sqrt(FACETS * FROWS * FW)
PARAMS = pltpu.CompilerParams(vmem_limit_bytes=16 << 20)
WIDE_PARAMS = pltpu.CompilerParams(vmem_limit_bytes=24 << 20)
SMEM_SPEC = pl.BlockSpec(memory_space=pltpu.SMEM)
VMEM_SPEC = pl.BlockSpec(memory_space=pltpu.VMEM)
HBM_SPEC = pl.BlockSpec(memory_space=pltpu.HBM)


def cos_sin(index, bits=16):
    quadrant = (index + (1 << (bits - 3))) >> (bits - 2)
    angle = (index - (quadrant << (bits - 2))).astype(F32) * (2.0 * math.pi / (1 << bits))
    square = angle * angle
    sine = angle * (1.0 + square * (-1.0 / 6 + square * (1.0 / 120 + square * (-1.0 / 5040 + square / 362880))))
    cosine = 1.0 + square * (-0.5 + square * (1.0 / 24 + square * (-1.0 / 720 + square / 40320)))
    swapped = (quadrant & 1) != 0
    c = jnp.where(swapped, sine, cosine)
    s = jnp.where(swapped, cosine, sine)
    c = jnp.where(((quadrant + 1) & 2) != 0, -c, c)
    s = jnp.where((quadrant & 2) != 0, -s, s)
    return c, s


def phase(frequency, pixel):
    return cos_sin((frequency * pixel) & (NIMG - 1))


def on_chip(value):
    return pltpu.with_memory_space_constraint(value, pltpu.VMEM)


def off_chip(value):
    return pltpu.with_memory_space_constraint(value, pltpu.HBM)


def write_out(pairs):
    copies = [pltpu.make_async_copy(source, target, sem) for source, target, sem in pairs]
    for copy in copies:
        copy.start()
    for copy in copies:
        copy.wait()


def iota(shape, dim):
    return lax.broadcasted_iota(I32, shape, dim)


def column_of(ref, count, lanes):
    row = iota((count, lanes), 0)
    value = jnp.zeros((count, lanes), I32)
    for i in range(count):
        value = jnp.where(row == i, ref[i], value)
    return value


def section_kernel(column_ref, offsets_ref, model_hbm, out_hbm, model_ref, table_ref, pc_ref, ps_ref, block_ref, acc_ref, out_ref, sems, sem):
    wide = FW // PARTS1
    fetches = []
    for part in range(PARTS1):
        cut = pl.ds(part * wide, wide)
        fetches.append(pltpu.make_async_copy(model_hbm.at[:, cut], model_ref.at[:, cut], sems.at[part]))
        fetches[-1].start()
    column_start = column_ref[0]
    pixel_start = offsets_ref[1, lax.axis_index("facet")]
    freq = column_start + iota((STEP1, SGW), 1)
    c, s = phase(freq, iota((STEP1, SGW), 0))
    table_ref[:, :SGW] = c.astype(BF)
    table_ref[:, SGW:] = (-s).astype(BF)
    freq = column_start + iota((HIGH1, SGW), 1)
    pc_ref[...], ps_ref[...] = phase(freq, pixel_start + STEP1 * iota((HIGH1, SGW), 0))
    for first in range(0, HIGH1, GROUP1):
        if first % (HIGH1 // PARTS1) == 0:
            fetches[first // (HIGH1 // PARTS1)].wait()
        for k in range(GROUP1):
            cut = slice((first + k) * STEP1, (first + k + 1) * STEP1)
            block_ref[k * FROWS : (k + 1) * FROWS] = model_ref[:, cut].astype(BF)
        product = jnp.dot(block_ref[...], table_ref[...], preferred_element_type=F32)
        for row in range(0, FROWS, ROWS1):
            lines = slice(row, row + ROWS1)
            acc_re = acc_ref[0, lines, :] if first else 0.0
            acc_im = acc_ref[1, lines, :] if first else 0.0
            for k in range(GROUP1):
                re = product[k * FROWS + row : k * FROWS + row + ROWS1, :SGW]
                im = product[k * FROWS + row : k * FROWS + row + ROWS1, SGW:]
                pc = pc_ref[first + k : first + k + 1, :]
                ps = ps_ref[first + k : first + k + 1, :]
                acc_re = acc_re + (re * pc + im * ps)
                acc_im = acc_im + (im * pc - re * ps)
            acc_ref[0, lines, :] = acc_re
            acc_ref[1, lines, :] = acc_im
    out_ref[:, :SLICE, :] = acc_ref[0].T.astype(BF).reshape(FACETS, SLICE, FROWS)
    out_ref[:, SLICE:, :] = acc_ref[1].T.astype(BF).reshape(FACETS, SLICE, FROWS)
    write_out([(out_ref, out_hbm, sem)])


def section(column_start, offsets, model):
    return pl.pallas_call(
        section_kernel,
        out_shape=jax.ShapeDtypeStruct((FACETS, 2 * SLICE, FROWS), BF),
        in_specs=[SMEM_SPEC, SMEM_SPEC, HBM_SPEC],
        out_specs=HBM_SPEC,
        scratch_shapes=[
            pltpu.VMEM((FROWS, FW), F32),
            pltpu.VMEM((STEP1, 2 * SGW), BF),
            pltpu.VMEM((HIGH1, SGW), F32),
            pltpu.VMEM((HIGH1, SGW), F32),
            pltpu.VMEM((GROUP1 * FROWS, STEP1), BF),
            pltpu.VMEM((2, FROWS, SGW), F32),
            pltpu.VMEM((FACETS, 2 * SLICE, FROWS), BF),
            pltpu.SemaphoreType.DMA((PARTS1,)),
            pltpu.SemaphoreType.DMA,
        ],
        compiler_params=PARAMS,
        name="section",
    )(column_start, off_chip(offsets), off_chip(model))


def kernel_columns(position):
    cells = (iota((SGW, position.shape[1]), 0) * OS + OS // 2).astype(F32)
    offset = cells - position.astype(F32)
    square = offset * offset
    value = jnp.exp2(square * (-0.5 / (OS * OS) / math.log(2.0)))
    return jnp.where(square <= float((KSUP * OS) ** 2), value, 0.0).astype(BF)


def row_table_kernel(offsets_ref, rows_ref, table_ref, c_ref, s_ref, base_ref, turn_ref):
    base_ref[0], base_ref[1] = phase(iota((FROWS, SGW), 1), iota((FROWS, SGW), 0))
    row = iota((FACETS, SGW), 0)
    start = jnp.zeros((FACETS, SGW), I32)
    for f in range(FACETS):
        start = jnp.where(row == f, offsets_ref[0, f], start)
    turn_ref[0], turn_ref[1] = phase(iota((FACETS, SGW), 1), start)
    row = iota((NROWSG, FROWS), 0)
    freq = jnp.zeros((NROWSG, FROWS), I32)
    for r in range(NROWSG):
        freq = jnp.where(row == r, rows_ref[0, r], freq)

    def one(f, carry):
        cf = turn_ref[0, pl.ds(f, 1), :]
        sf = turn_ref[1, pl.ds(f, 1), :]
        lines = pl.ds(pl.multiple_of(f * FROWS, FROWS), FROWS)
        table_ref[0, lines, :] = (base_ref[0] * cf - base_ref[1] * sf).astype(BF)
        table_ref[1, lines, :] = (base_ref[1] * cf + base_ref[0] * sf).astype(BF)
        c_ref[f], s_ref[f] = phase(freq, offsets_ref[0, f] + iota((NROWSG, FROWS), 1))
        return carry

    lax.fori_loop(0, FACETS, one, 0)


def row_tables(offsets, rows):
    return pl.pallas_call(
        row_table_kernel,
        out_shape=(
            pltpu.VMEM((2, FACETS * FROWS, SGW), BF),
            pltpu.VMEM((FACETS, NROWSG, FROWS), F32),
            pltpu.VMEM((FACETS, NROWSG, FROWS), F32),
        ),
        in_specs=[SMEM_SPEC, SMEM_SPEC],
        out_specs=(VMEM_SPEC,) * 3,
        scratch_shapes=[
            pltpu.VMEM((2, FROWS, SGW), F32),
            pltpu.VMEM((2, FACETS, SGW), F32),
        ],
        compiler_params=PARAMS,
        name="row_tables",
    )(offsets, rows)


def grid_kernel(in_ref, c_ref, s_ref, table_ref, out_hbm, turned_ref, out_ref, sem):
    half = NROWSG * SLICE
    for f in range(FACETS):
        re = in_ref[f, :SLICE, :].astype(F32)
        im = in_ref[f, SLICE:, :].astype(F32)
        cut = slice(f * FROWS, (f + 1) * FROWS)
        for r in range(NROWSG):
            c = c_ref[f, r : r + 1, :]
            s = s_ref[f, r : r + 1, :]
            turned_ref[r * SLICE : (r + 1) * SLICE, cut] = (re * c + im * s).astype(BF)
            turned_ref[half + r * SLICE : half + (r + 1) * SLICE, cut] = (im * c - re * s).astype(BF)
    by_c = jnp.dot(turned_ref[...], table_ref[0], preferred_element_type=F32)
    by_s = jnp.dot(turned_ref[...], table_ref[1], preferred_element_type=F32)
    re = (NORM * (by_c[:half] + by_s[half:])).astype(BF)
    im = (NORM * (by_c[half:] - by_s[:half])).astype(BF)
    out_ref[:, :SLICE, :] = re.reshape(NROWSG, SLICE, SGW)
    out_ref[:, SLICE:, :] = im.reshape(NROWSG, SLICE, SGW)
    write_out([(out_ref, out_hbm, sem)])


def grids(sections, tables):
    table, c, s = tables
    return pl.pallas_call(
        grid_kernel,
        out_shape=jax.ShapeDtypeStruct((NROWSG, 2 * SLICE, SGW), BF),
        in_specs=[VMEM_SPEC] * 4,
        out_specs=HBM_SPEC,
        scratch_shapes=[
            pltpu.VMEM((2 * NROWSG * SLICE, FACETS * FROWS), BF),
            pltpu.VMEM((NROWSG, 2 * SLICE, SGW), BF),
            pltpu.SemaphoreType.DMA,
        ],
        compiler_params=PARAMS,
        name="grids",
    )(on_chip(sections), on_chip(c), on_chip(s), on_chip(table))


def adjoint_kernel(in_ref, c_ref, s_ref, table_ref, out_hbm, lines_ref, out_ref, sems):
    half = NROWSG * SLICE
    lines_ref[:half] = in_ref[:, :SLICE, :].reshape(half, SGW)
    lines_ref[half:] = in_ref[:, SLICE:, :].reshape(half, SGW)

    def one(pair, carry):
        cut = pl.ds(pl.multiple_of(pair * 2 * FROWS, 2 * FROWS), 2 * FROWS)
        dims = (((1,), (1,)), ((), ()))
        by_c = lax.dot_general(lines_ref[...], table_ref[0, cut, :], dims, preferred_element_type=F32)
        by_s = lax.dot_general(lines_ref[...], table_ref[1, cut, :], dims, preferred_element_type=F32)
        for k in range(2):
            f = 2 * pair + k
            lanes = slice(k * FROWS, (k + 1) * FROWS)
            acc_re = jnp.zeros((SLICE, FROWS), F32)
            acc_im = jnp.zeros((SLICE, FROWS), F32)
            for r in range(NROWSG):
                top = slice(r * SLICE, (r + 1) * SLICE)
                low = slice(half + r * SLICE, half + (r + 1) * SLICE)
                re = by_c[top, lanes] - by_s[low, lanes]
                im = by_c[low, lanes] + by_s[top, lanes]
                c = c_ref[f, r : r + 1, :]
                s = s_ref[f, r : r + 1, :]
                acc_re = acc_re + (re * c - im * s)
                acc_im = acc_im + (im * c + re * s)
            lower = iota((SLICE, FROWS), 1) < HALF
            out_ref[0, f] = jnp.where(lower, acc_re, pltpu.roll(acc_im, HALF, 1)).astype(BF)
            out_ref[1, f] = jnp.where(lower, pltpu.roll(acc_re, HALF, 1), acc_im).astype(BF)
        return carry

    lax.fori_loop(0, FACETS // 2, one, 0, unroll=UNROLL4)
    write_out([(out_ref.at[copy % 2], out_hbm.at[:, copy], sems.at[copy]) for copy in range(NCOL)])


def adjoint(gridded, tables):
    table, c, s = tables
    return pl.pallas_call(
        adjoint_kernel,
        out_shape=jax.ShapeDtypeStruct((FACETS, NCOL, SLICE, FROWS), BF),
        in_specs=[VMEM_SPEC] * 4,
        out_specs=HBM_SPEC,
        scratch_shapes=[
            pltpu.VMEM((2 * NROWSG * SLICE, SGW), BF),
            pltpu.VMEM((2, FACETS, SLICE, FROWS), BF),
            pltpu.SemaphoreType.DMA((NCOL,)),
        ],
        compiler_params=PARAMS,
        name="adjoint",
    )(on_chip(gridded), on_chip(c), on_chip(s), on_chip(table))


def visibility_pass(counts_ref, obs_ref, weight_ref, in_ref, kernels, gridded_hbm, res_ref, acc_ref, gridded_ref, sem):
    count = counts_ref[0, lax.axis_index("facet")]
    grid = [in_ref[:, half * SLICE : (half + 1) * SLICE, :].reshape(SGW, SGW) for half in range(2)]
    for part in range(VCAP // VBLOCK):
        cut = slice(part * VBLOCK, (part + 1) * VBLOCK)
        ku, kv = kernels(cut)
        live = part * VBLOCK + iota((1, VBLOCK), 1) < count
        weight = weight_ref[:, cut].astype(F32)
        for half in range(2):
            sampled = jnp.dot(grid[half], ku, preferred_element_type=F32)
            predicted = jnp.sum(sampled * kv.astype(F32), axis=0, keepdims=True)
            observed = obs_ref[half : half + 1, cut].astype(F32)
            residual = jnp.where(live, weight * (observed - predicted), 0.0)
            if res_ref is not None:
                res_ref[half : half + 1, cut] = residual
            weighted = (residual * kv.astype(F32)).astype(BF)
            total = lax.dot_general(
                weighted, ku, (((1,), (1,)), ((), ())), preferred_element_type=F32
            )
            if part:
                total = total + acc_ref[half]
            if part + 1 < VCAP // VBLOCK:
                acc_ref[half] = total
            else:
                lines = total.astype(BF).reshape(FACETS, SLICE, SGW)
                gridded_ref[:, half * SLICE : (half + 1) * SLICE, :] = lines
    write_out([(gridded_ref, gridded_hbm, sem)])


def first_kernel(counts_ref, obs_ref, weight_ref, in_ref, uv_ref, gridded_hbm, ku_ref, kv_ref, acc_ref, gridded_ref, sem):
    def kernels(cut):
        ku_ref[:, cut] = kernel_columns(uv_ref[0:1, cut])
        kv_ref[:, cut] = kernel_columns(uv_ref[1:2, cut])
        return ku_ref[:, cut], kv_ref[:, cut]

    visibility_pass(counts_ref, obs_ref, weight_ref, in_ref, kernels, gridded_hbm, None, acc_ref, gridded_ref, sem)


def last_kernel(counts_ref, obs_ref, weight_ref, in_ref, ku_ref, kv_ref, gridded_hbm, res_ref, acc_ref, gridded_ref, sem):
    def kernels(cut):
        return ku_ref[:, cut], kv_ref[:, cut]

    visibility_pass(counts_ref, obs_ref, weight_ref, in_ref, kernels, gridded_hbm, res_ref, acc_ref, gridded_ref, sem)


VIS_SCRATCH = [
    pltpu.VMEM((2, SGW, SGW), F32),
    pltpu.VMEM((FACETS, 2 * SLICE, SGW), BF),
    pltpu.SemaphoreType.DMA,
]


def first_visibilities(counts, obs, weight, grid, uv):
    return pl.pallas_call(
        first_kernel,
        out_shape=(
            jax.ShapeDtypeStruct((FACETS, 2 * SLICE, SGW), BF),
            pltpu.VMEM((SGW, VCAP), BF),
            pltpu.VMEM((SGW, VCAP), BF),
        ),
        in_specs=[SMEM_SPEC] + [VMEM_SPEC] * 4,
        out_specs=(HBM_SPEC, VMEM_SPEC, VMEM_SPEC),
        scratch_shapes=VIS_SCRATCH,
        compiler_params=PARAMS,
        name="first_visibilities",
    )(counts, obs, weight, on_chip(grid), uv)


def last_visibilities(counts, obs, weight, grid, ku, kv):
    return pl.pallas_call(
        last_kernel,
        out_shape=(
            jax.ShapeDtypeStruct((FACETS, 2 * SLICE, SGW), BF),
            jax.ShapeDtypeStruct((2, VCAP), F32),
        ),
        in_specs=[SMEM_SPEC] + [VMEM_SPEC] * 5,
        out_specs=(HBM_SPEC, VMEM_SPEC),
        scratch_shapes=VIS_SCRATCH,
        compiler_params=PARAMS,
        name="last_visibilities",
    )(counts, obs, weight, on_chip(grid), on_chip(ku), on_chip(kv))


def dirichlet(distance, pixel_start):
    distance = ((distance & (NIMG - 1)) ^ (NIMG // 2)) - NIMG // 2
    top = cos_sin((distance * (NIMG // (NIMG // FW * 2))) & (NIMG - 1))[1]
    bottom = cos_sin(distance, 17)[1]
    ratio = jnp.where(distance == 0, float(FW), top / jnp.where(distance == 0, 1.0, bottom))
    c, s = cos_sin((distance * (2 * pixel_start + FW - 1)) & (2 * NIMG - 1), 17)
    return c * ratio, s * ratio


def gram_kernel(step_ref, starts_ref, column_ref, offsets_ref, mine_ref, theirs_ref, first_ref, out_hbm, flip_ref, v_ref, out_ref, sem):
    wide = 2 * SGW
    pixel_start = offsets_ref[1, lax.axis_index("facet")]
    own = column_ref[0]
    row = iota((NCOL, wide), 0)
    starts = jnp.zeros((NCOL, wide), I32)
    for c in range(NCOL):
        starts = jnp.where(row == c, starts_ref[c], starts)
    lane = iota((NCOL, wide), 1)
    v_ref[0], v_ref[1] = dirichlet(starts - own + (lane - (SGW - 1)), pixel_start)
    v_ref[2], v_ref[3] = dirichlet(starts + own + (2 * (SGW - 1) - lane), pixel_start)
    anti = (iota((SGW, SGW), 0) + iota((SGW, SGW), 1)) == SGW - 1
    flip_ref[...] = jnp.where(anti, 1.0, 0.0).astype(BF)
    totals = [None] * 4
    for c in range(NCOL):
        lines = [half_ref[:, c].reshape(SGW, FROWS) for half_ref in (mine_ref, theirs_ref)]
        lines = jnp.concatenate(lines, axis=1)
        turned = jnp.dot(flip_ref[...], lines, preferred_element_type=F32).astype(BF)
        for k in range(4):
            spread = jnp.broadcast_to(v_ref[k, c : c + 1, :], (SGW, wide))
            band = pltpu.roll(spread, SGW + 1, 1, stride=1, stride_axis=0)[:, :SGW].astype(BF)
            term = jnp.dot(band, lines if k < 2 else turned, preferred_element_type=F32)
            totals[k] = term if c == 0 else totals[k] + term
    scale = step_ref[0] * (0.5 * NORM)
    p1, p2, p3, p4 = totals
    upper = (lax.axis_index("sub") & 1) == 1
    left = iota((SGW, FROWS), 1) < HALF

    def joined(straight, crossed):
        mine, theirs = [
            straight[:, k * FROWS : (k + 1) * FROWS] + pltpu.roll(crossed[:, k * FROWS : (k + 1) * FROWS], HALF, 1)
            for k in range(2)
        ]
        low = jnp.where(upper, theirs, mine)
        high = jnp.where(upper, mine, theirs)
        return jnp.where(left, low, pltpu.roll(high, HALF, 1))

    re = joined(p1 + p3, -(p2 + p4))
    im = joined(p2 - p4, p1 - p3)
    first = first_ref[...].astype(F32)
    out_ref[:, :SLICE, :] = (first[:, :SLICE] + (scale * re).reshape(FACETS, SLICE, FROWS)).astype(BF)
    out_ref[:, SLICE:, :] = (first[:, SLICE:] + (scale * im).reshape(FACETS, SLICE, FROWS)).astype(BF)
    write_out([(out_ref, out_hbm, sem)])


def gram(steps, column_starts, column_start, offsets, mine, theirs, first):
    shape = (FACETS, NCOL, SLICE, FROWS)
    return pl.pallas_call(
        gram_kernel,
        out_shape=jax.ShapeDtypeStruct((FACETS, 2 * SLICE, FROWS), BF),
        in_specs=[SMEM_SPEC] * 4 + [VMEM_SPEC] * 3,
        out_specs=HBM_SPEC,
        scratch_shapes=[
            pltpu.VMEM((SGW, SGW), BF),
            pltpu.VMEM((4, NCOL, 2 * SGW), F32),
            pltpu.VMEM((FACETS, 2 * SLICE, FROWS), BF),
            pltpu.SemaphoreType.DMA,
        ],
        compiler_params=PARAMS,
        name="gram",
    )(steps, column_starts, column_start, offsets, on_chip(mine.reshape(shape)), on_chip(theirs.reshape(shape)), first)


def update_kernel(step_ref, adj0_ref, adj1_ref, table_hbm, pc_ref, ps_ref, out_ref, table_ref, both_ref, even_ref, odd_ref, sem):
    part = pl.program_id(0)
    fetch = pltpu.make_async_copy(table_hbm, table_ref, sem)

    def turn(group, target_ref):
        re = both_ref[:HALF, :]
        im = both_ref[HALF:, :]
        for p in range(PAIR5):
            pc = pc_ref[pl.ds(group * PAIR5 + p, 1), :]
            ps = ps_ref[pl.ds(group * PAIR5 + p, 1), :]
            lines = slice(p * HALF, (p + 1) * HALF)
            target_ref[lines, :COLUMNS] = (re * pc - im * ps).astype(BF)
            target_ref[lines, COLUMNS:] = (im * pc + re * ps).astype(BF)

    def put(place, source_ref):
        gradient = jnp.dot(source_ref[...], table_ref[...], preferred_element_type=F32).astype(BF)
        for p in range(PAIR5):
            left = (place * PAIR5 + p) * STEP5
            out_ref[:, left : left + STEP5] = gradient[p * HALF : (p + 1) * HALF]

    @pl.when(part == 0)
    def _():
        fetch.start()
        first = step_ref[0] * NORM
        second = step_ref[1] * NORM
        group = NCOL * SLICE
        for j in range(FACETS):
            lines0 = adj0_ref[j * NCOL : (j + 1) * NCOL].reshape(group, FROWS).astype(F32)
            lines1 = adj1_ref[j * NCOL : (j + 1) * NCOL].reshape(group, FROWS).astype(F32)
            both_ref[:, j * group : (j + 1) * group] = (first * lines0 + second * lines1).T
        turn(0, even_ref)
        fetch.wait()

    turn(2 * part + 1, odd_ref)
    put(0, even_ref)
    turn(jnp.minimum(2 * part + 2, HIGH5 // PAIR5 - 2), even_ref)
    put(1, odd_ref)


def update(steps, adj0, adj1, tables):
    table, pc, ps = tables
    return pl.pallas_call(
        update_kernel,
        grid=(HIGH5 // PAIR5 // 2,),
        out_shape=jax.ShapeDtypeStruct((HALF, FW), BF),
        in_specs=[SMEM_SPEC, VMEM_SPEC, VMEM_SPEC, HBM_SPEC, VMEM_SPEC, VMEM_SPEC],
        out_specs=pl.BlockSpec((HALF, 2 * PAIR5 * STEP5), lambda i: (0, i)),
        scratch_shapes=[
            pltpu.VMEM((2 * COLUMNS, STEP5), BF),
            pltpu.VMEM((FROWS, COLUMNS), F32),
            pltpu.VMEM((PAIR5 * HALF, 2 * COLUMNS), BF),
            pltpu.VMEM((PAIR5 * HALF, 2 * COLUMNS), BF),
            pltpu.SemaphoreType.DMA,
        ],
        compiler_params=WIDE_PARAMS,
        name="update",
    )(steps, on_chip(adj0), on_chip(adj1), off_chip(table), on_chip(pc), on_chip(ps))


def step_kernel(mine_ref, theirs_ref, model_ref, out_hbm, out_ref, sems):
    upper = (lax.axis_index("sub") & 1) == 1
    wide = FW // PARTS7
    sent = []
    for part in range(PARTS7):
        cut = slice(part * wide, (part + 1) * wide)
        mine = mine_ref[:, cut].astype(F32)
        theirs = theirs_ref[:, cut].astype(F32)
        out_ref[:HALF, cut] = model_ref[:HALF, cut] + jnp.where(upper, theirs, mine)
        out_ref[HALF:, cut] = model_ref[HALF:, cut] + jnp.where(upper, mine, theirs)
        lanes = pl.ds(part * wide, wide)
        sent.append(pltpu.make_async_copy(out_ref.at[:, lanes], out_hbm.at[:, lanes], sems.at[part]))
        sent[-1].start()
    for copy in sent:
        copy.wait()


def take_step(mine, theirs, model):
    return pl.pallas_call(
        step_kernel,
        out_shape=jax.ShapeDtypeStruct((FROWS, FW), F32),
        in_specs=[VMEM_SPEC] * 3,
        out_specs=HBM_SPEC,
        scratch_shapes=[pltpu.VMEM((FROWS, FW), F32), pltpu.SemaphoreType.DMA((PARTS7,))],
        compiler_params=PARAMS,
        name="take_step",
    )(on_chip(mine), on_chip(theirs), on_chip(model))


def update_table_kernel(starts_ref, offsets_ref, table_hbm, pc_ref, ps_ref, table_ref, base_ref, turn_ref, sem):
    group = NCOL * SLICE
    line = iota((group, STEP5), 0)
    freq = line & (SLICE - 1)
    for c in range(NCOL):
        freq = freq + jnp.where((line >> 4) == c, starts_ref[c], 0)
    base_ref[0], base_ref[1] = phase(freq, iota((group, STEP5), 1))
    turn_ref[0], turn_ref[1] = phase(SLICE * iota((FACETS, STEP5), 0), iota((FACETS, STEP5), 1))

    def one(j, carry):
        c = turn_ref[0, pl.ds(j, 1), :]
        s = turn_ref[1, pl.ds(j, 1), :]
        cut = pl.ds(pl.multiple_of(j * group, group), group)
        table_ref[cut, :] = (base_ref[0] * c - base_ref[1] * s).astype(BF)
        cut = pl.ds(pl.multiple_of(COLUMNS + j * group, group), group)
        table_ref[cut, :] = (-(base_ref[1] * c + base_ref[0] * s)).astype(BF)
        return carry

    lax.fori_loop(0, FACETS, one, 0)
    lane = iota((HIGH5, COLUMNS), 1)
    freq = SLICE * (lane >> 7) + (lane & (SLICE - 1))
    for c in range(NCOL):
        freq = freq + jnp.where(((lane >> 4) & (NCOL - 1)) == c, starts_ref[c], 0)
    pixel_start = offsets_ref[1, lax.axis_index("facet")]
    pc_ref[...], ps_ref[...] = phase(freq, pixel_start + STEP5 * iota((HIGH5, COLUMNS), 0))
    write_out([(table_ref, table_hbm, sem)])


def update_tables(column_starts, offsets):
    return pl.pallas_call(
        update_table_kernel,
        out_shape=(
            pltpu.HBM((2 * COLUMNS, STEP5), BF),
            pltpu.VMEM((HIGH5, COLUMNS), F32),
            pltpu.VMEM((HIGH5, COLUMNS), F32),
        ),
        in_specs=[SMEM_SPEC, SMEM_SPEC],
        out_specs=(HBM_SPEC, VMEM_SPEC, VMEM_SPEC),
        scratch_shapes=[
            pltpu.VMEM((2 * COLUMNS, STEP5), BF),
            pltpu.VMEM((2, NCOL * SLICE, STEP5), F32),
            pltpu.VMEM((2, FACETS, STEP5), F32),
            pltpu.SemaphoreType.DMA,
        ],
        compiler_params=PARAMS,
        name="update_tables",
    )(column_starts, offsets)


def exchange(value):
    return lax.all_to_all(value, "facet", split_axis=0, concat_axis=0, tiled=True)


def swapped(value, bit):
    return lax.ppermute(value, "sub", [(i, i ^ bit) for i in range(NCOL)])


def to_facets(value):
    copies = value.reshape(FACETS * NCOL, *value.shape[2:])
    return lax.all_to_all(copies, ("facet", "sub"), split_axis=0, concat_axis=0, tiled=True)


def local(
    model_image,
    step_sizes,
    facet_offsets,
    col_offsets,
    row_offsets,
    counts,
    vis_uv,
    vis_obs,
    vis_weight,
):
    mine = jnp.arange(NCOL, dtype=I32) == lax.axis_index("sub")
    column_starts = jnp.where(mine, col_offsets[0], 0)
    column_starts = column_starts + swapped(column_starts, 1)
    uv = vis_uv.reshape(2, VCAP)
    obs = vis_obs.reshape(2, VCAP)
    weight = vis_weight.reshape(1, VCAP)
    model = model_image[0]
    first = section(col_offsets, facet_offsets, model)
    rows = row_tables(facet_offsets, row_offsets)
    sections, column_starts = lax.optimization_barrier((exchange(first), column_starts))
    for bit in (2, 4):
        column_starts = column_starts + swapped(column_starts, bit)
    grid = exchange(grids(sections, rows))
    gridded, ku, kv = first_visibilities(counts, obs, weight, grid, uv)
    gridded, column_starts = lax.optimization_barrier((gridded, column_starts))
    adj0 = to_facets(adjoint(exchange(gridded), rows))
    second = gram(step_sizes, column_starts, col_offsets, facet_offsets, adj0, swapped(adj0, 1), first)
    grid = exchange(grids(exchange(second), rows))
    gridded, residual = last_visibilities(counts, obs, weight, grid, ku, kv)
    adj1 = to_facets(adjoint(exchange(gridded), rows))
    tables = update_tables(column_starts, facet_offsets)
    step = update(step_sizes, adj0, adj1, tables)
    model = take_step(step, swapped(step, 1), model)
    return model[None], residual.reshape(2, 1, 1, VCAP)


def solution(mesh):
    in_specs = (
        P("facet", None, None),
        P(),
        P(),
        P("sub"),
        P("sub", None),
        P("sub", None),
        P(None, "sub", "facet", None),
        P(None, "sub", "facet", None),
        P("sub", "facet", None),
    )
    out_specs = (P("facet", None, None), P(None, "sub", "facet", None))
    return jax.shard_map(local, mesh=mesh, in_specs=in_specs, out_specs=out_specs, check_vma=False)
```

```python
import math

import jax
import jax.numpy as jnp
from jax import lax
from jax.experimental import pallas as pl
from jax.experimental.pallas import tpu as pltpu
from jax.sharding import PartitionSpec as P

NIMG = 65536
FW = 8192
FROWS = 128
SGW = 256
VCAP = 4096
OS = 8
KSUP = 4
FACETS = 16
NCOL = 8
NROWSG = 16
SLICE = SGW // FACETS
COLUMNS = NCOL * SGW

STEP1 = 256
HIGH1 = FW // STEP1
PARTS1 = 4
GROUP1 = 4
ROWS1 = 32
STEP5 = 512
HIGH5 = FW // STEP5
PAIR5 = 4
HALF = FROWS // 2
PARTS7 = 4
VBLOCK = 1024
CHUNK = 4
UNROLL4 = 8

BF = jnp.bfloat16
F32 = jnp.float32
I32 = jnp.int32
NORM = 1.0 / math.sqrt(FACETS * FROWS * FW)
PARAMS = pltpu.CompilerParams(vmem_limit_bytes=16 << 20)
WIDE_PARAMS = pltpu.CompilerParams(vmem_limit_bytes=24 << 20)
SMEM_SPEC = pl.BlockSpec(memory_space=pltpu.SMEM)
VMEM_SPEC = pl.BlockSpec(memory_space=pltpu.VMEM)
HBM_SPEC = pl.BlockSpec(memory_space=pltpu.HBM)


def cos_sin(index, bits=16):
    quadrant = (index + (1 << (bits - 3))) >> (bits - 2)
    angle = (index - (quadrant << (bits - 2))).astype(F32) * (2.0 * math.pi / (1 << bits))
    square = angle * angle
    sine = angle * (1.0 + square * (-1.0 / 6 + square * (1.0 / 120 + square * (-1.0 / 5040 + square / 362880))))
    cosine = 1.0 + square * (-0.5 + square * (1.0 / 24 + square * (-1.0 / 720 + square / 40320)))
    swapped = (quadrant & 1) != 0
    c = jnp.where(swapped, sine, cosine)
    s = jnp.where(swapped, cosine, sine)
    c = jnp.where(((quadrant + 1) & 2) != 0, -c, c)
    s = jnp.where((quadrant & 2) != 0, -s, s)
    return c, s


def phase(frequency, pixel):
    return cos_sin((frequency * pixel) & (NIMG - 1))


def on_chip(value):
    return pltpu.with_memory_space_constraint(value, pltpu.VMEM)


def off_chip(value):
    return pltpu.with_memory_space_constraint(value, pltpu.HBM)


def write_out(pairs):
    copies = [pltpu.make_async_copy(source, target, sem) for source, target, sem in pairs]
    for copy in copies:
        copy.start()
    for copy in copies:
        copy.wait()


def iota(shape, dim):
    return lax.broadcasted_iota(I32, shape, dim)


def column_of(ref, count, lanes):
    row = iota((count, lanes), 0)
    value = jnp.zeros((count, lanes), I32)
    for i in range(count):
        value = jnp.where(row == i, ref[i], value)
    return value


def section_kernel(column_ref, offsets_ref, model_hbm, out_hbm, model_ref, table_ref, pc_ref, ps_ref, block_ref, acc_ref, out_ref, sems, sem):
    wide = FW // PARTS1
    fetches = []
    for part in range(PARTS1):
        cut = pl.ds(part * wide, wide)
        fetches.append(pltpu.make_async_copy(model_hbm.at[:, cut], model_ref.at[:, cut], sems.at[part]))
        fetches[-1].start()
    column_start = column_ref[0]
    pixel_start = offsets_ref[1, lax.axis_index("facet")]
    freq = column_start + iota((STEP1, SGW), 1)
    c, s = phase(freq, iota((STEP1, SGW), 0))
    table_ref[:, :SGW] = c.astype(BF)
    table_ref[:, SGW:] = (-s).astype(BF)
    freq = column_start + iota((HIGH1, SGW), 1)
    pc_ref[...], ps_ref[...] = phase(freq, pixel_start + STEP1 * iota((HIGH1, SGW), 0))
    for first in range(0, HIGH1, GROUP1):
        if first % (HIGH1 // PARTS1) == 0:
            fetches[first // (HIGH1 // PARTS1)].wait()
        for k in range(GROUP1):
            cut = slice((first + k) * STEP1, (first + k + 1) * STEP1)
            block_ref[k * FROWS : (k + 1) * FROWS] = model_ref[:, cut].astype(BF)
        product = jnp.dot(block_ref[...], table_ref[...], preferred_element_type=F32)
        for row in range(0, FROWS, ROWS1):
            lines = slice(row, row + ROWS1)
            acc_re = acc_ref[0, lines, :] if first else 0.0
            acc_im = acc_ref[1, lines, :] if first else 0.0
            for k in range(GROUP1):
                re = product[k * FROWS + row : k * FROWS + row + ROWS1, :SGW]
                im = product[k * FROWS + row : k * FROWS + row + ROWS1, SGW:]
                pc = pc_ref[first + k : first + k + 1, :]
                ps = ps_ref[first + k : first + k + 1, :]
                acc_re = acc_re + (re * pc + im * ps)
                acc_im = acc_im + (im * pc - re * ps)
            acc_ref[0, lines, :] = acc_re
            acc_ref[1, lines, :] = acc_im
    out_ref[:, :SLICE, :] = acc_ref[0].T.astype(BF).reshape(FACETS, SLICE, FROWS)
    out_ref[:, SLICE:, :] = acc_ref[1].T.astype(BF).reshape(FACETS, SLICE, FROWS)
    write_out([(out_ref, out_hbm, sem)])


def section(column_start, offsets, model):
    return pl.pallas_call(
        section_kernel,
        out_shape=jax.ShapeDtypeStruct((FACETS, 2 * SLICE, FROWS), BF),
        in_specs=[SMEM_SPEC, SMEM_SPEC, HBM_SPEC],
        out_specs=HBM_SPEC,
        scratch_shapes=[
            pltpu.VMEM((FROWS, FW), F32),
            pltpu.VMEM((STEP1, 2 * SGW), BF),
            pltpu.VMEM((HIGH1, SGW), F32),
            pltpu.VMEM((HIGH1, SGW), F32),
            pltpu.VMEM((GROUP1 * FROWS, STEP1), BF),
            pltpu.VMEM((2, FROWS, SGW), F32),
            pltpu.VMEM((FACETS, 2 * SLICE, FROWS), BF),
            pltpu.SemaphoreType.DMA((PARTS1,)),
            pltpu.SemaphoreType.DMA,
        ],
        compiler_params=PARAMS,
        name="section",
    )(column_start, off_chip(offsets), off_chip(model))


def kernel_columns(position):
    cells = (iota((SGW, position.shape[1]), 0) * OS + OS // 2).astype(F32)
    offset = cells - position.astype(F32)
    square = offset * offset
    value = jnp.exp2(square * (-0.5 / (OS * OS) / math.log(2.0)))
    return jnp.where(square <= float((KSUP * OS) ** 2), value, 0.0).astype(BF)


def row_table_kernel(offsets_ref, rows_ref, table_ref, c_ref, s_ref, base_ref, turn_ref):
    base_ref[0], base_ref[1] = phase(iota((FROWS, SGW), 1), iota((FROWS, SGW), 0))
    row = iota((FACETS, SGW), 0)
    start = jnp.zeros((FACETS, SGW), I32)
    for f in range(FACETS):
        start = jnp.where(row == f, offsets_ref[0, f], start)
    turn_ref[0], turn_ref[1] = phase(iota((FACETS, SGW), 1), start)
    row = iota((NROWSG, FROWS), 0)
    freq = jnp.zeros((NROWSG, FROWS), I32)
    for r in range(NROWSG):
        freq = jnp.where(row == r, rows_ref[0, r], freq)

    def one(f, carry):
        cf = turn_ref[0, pl.ds(f, 1), :]
        sf = turn_ref[1, pl.ds(f, 1), :]
        lines = pl.ds(pl.multiple_of(f * FROWS, FROWS), FROWS)
        table_ref[0, lines, :] = (base_ref[0] * cf - base_ref[1] * sf).astype(BF)
        table_ref[1, lines, :] = (base_ref[1] * cf + base_ref[0] * sf).astype(BF)
        c_ref[f], s_ref[f] = phase(freq, offsets_ref[0, f] + iota((NROWSG, FROWS), 1))
        return carry

    lax.fori_loop(0, FACETS, one, 0)


def row_tables(offsets, rows):
    return pl.pallas_call(
        row_table_kernel,
        out_shape=(
            pltpu.VMEM((2, FACETS * FROWS, SGW), BF),
            pltpu.VMEM((FACETS, NROWSG, FROWS), F32),
            pltpu.VMEM((FACETS, NROWSG, FROWS), F32),
        ),
        in_specs=[SMEM_SPEC, SMEM_SPEC],
        out_specs=(VMEM_SPEC,) * 3,
        scratch_shapes=[
            pltpu.VMEM((2, FROWS, SGW), F32),
            pltpu.VMEM((2, FACETS, SGW), F32),
        ],
        compiler_params=PARAMS,
        name="row_tables",
    )(offsets, rows)


def grid_kernel(in_ref, c_ref, s_ref, table_ref, out_hbm, turned_ref, out_ref, sem):
    half = NROWSG * SLICE
    for f in range(FACETS):
        re = in_ref[f, :SLICE, :].astype(F32)
        im = in_ref[f, SLICE:, :].astype(F32)
        cut = slice(f * FROWS, (f + 1) * FROWS)
        for r in range(NROWSG):
            c = c_ref[f, r : r + 1, :]
            s = s_ref[f, r : r + 1, :]
            turned_ref[r * SLICE : (r + 1) * SLICE, cut] = (re * c + im * s).astype(BF)
            turned_ref[half + r * SLICE : half + (r + 1) * SLICE, cut] = (im * c - re * s).astype(BF)
    by_c = jnp.dot(turned_ref[...], table_ref[0], preferred_element_type=F32)
    by_s = jnp.dot(turned_ref[...], table_ref[1], preferred_element_type=F32)
    re = (NORM * (by_c[:half] + by_s[half:])).astype(BF)
    im = (NORM * (by_c[half:] - by_s[:half])).astype(BF)
    out_ref[:, :SLICE, :] = re.reshape(NROWSG, SLICE, SGW)
    out_ref[:, SLICE:, :] = im.reshape(NROWSG, SLICE, SGW)
    write_out([(out_ref, out_hbm, sem)])


def grids(sections, tables):
    table, c, s = tables
    return pl.pallas_call(
        grid_kernel,
        out_shape=jax.ShapeDtypeStruct((NROWSG, 2 * SLICE, SGW), BF),
        in_specs=[VMEM_SPEC] * 4,
        out_specs=HBM_SPEC,
        scratch_shapes=[
            pltpu.VMEM((2 * NROWSG * SLICE, FACETS * FROWS), BF),
            pltpu.VMEM((NROWSG, 2 * SLICE, SGW), BF),
            pltpu.SemaphoreType.DMA,
        ],
        compiler_params=PARAMS,
        name="grids",
    )(on_chip(sections), on_chip(c), on_chip(s), on_chip(table))


def adjoint_kernel(in_ref, c_ref, s_ref, table_ref, out_hbm, lines_ref, out_ref, sems):
    half = NROWSG * SLICE
    lines_ref[:half] = in_ref[:, :SLICE, :].reshape(half, SGW)
    lines_ref[half:] = in_ref[:, SLICE:, :].reshape(half, SGW)

    def one(pair, carry):
        cut = pl.ds(pl.multiple_of(pair * 2 * FROWS, 2 * FROWS), 2 * FROWS)
        dims = (((1,), (1,)), ((), ()))
        by_c = lax.dot_general(lines_ref[...], table_ref[0, cut, :], dims, preferred_element_type=F32)
        by_s = lax.dot_general(lines_ref[...], table_ref[1, cut, :], dims, preferred_element_type=F32)
        for k in range(2):
            f = 2 * pair + k
            lanes = slice(k * FROWS, (k + 1) * FROWS)
            acc_re = jnp.zeros((SLICE, FROWS), F32)
            acc_im = jnp.zeros((SLICE, FROWS), F32)
            for r in range(NROWSG):
                top = slice(r * SLICE, (r + 1) * SLICE)
                low = slice(half + r * SLICE, half + (r + 1) * SLICE)
                re = by_c[top, lanes] - by_s[low, lanes]
                im = by_c[low, lanes] + by_s[top, lanes]
                c = c_ref[f, r : r + 1, :]
                s = s_ref[f, r : r + 1, :]
                acc_re = acc_re + (re * c - im * s)
                acc_im = acc_im + (im * c + re * s)
            lower = iota((SLICE, FROWS), 1) < HALF
            out_ref[0, f] = jnp.where(lower, acc_re, pltpu.roll(acc_im, HALF, 1)).astype(BF)
            out_ref[1, f] = jnp.where(lower, pltpu.roll(acc_re, HALF, 1), acc_im).astype(BF)
        return carry

    lax.fori_loop(0, FACETS // 2, one, 0, unroll=UNROLL4)
    write_out([(out_ref.at[copy % 2], out_hbm.at[:, copy], sems.at[copy]) for copy in range(NCOL)])


def adjoint(gridded, tables):
    table, c, s = tables
    return pl.pallas_call(
        adjoint_kernel,
        out_shape=jax.ShapeDtypeStruct((FACETS, NCOL, SLICE, FROWS), BF),
        in_specs=[VMEM_SPEC] * 4,
        out_specs=HBM_SPEC,
        scratch_shapes=[
            pltpu.VMEM((2 * NROWSG * SLICE, SGW), BF),
            pltpu.VMEM((2, FACETS, SLICE, FROWS), BF),
            pltpu.SemaphoreType.DMA((NCOL,)),
        ],
        compiler_params=PARAMS,
        name="adjoint",
    )(on_chip(gridded), on_chip(c), on_chip(s), on_chip(table))


def visibility_pass(counts_ref, obs_ref, weight_ref, in_ref, kernels, gridded_hbm, res_ref, acc_ref, gridded_ref, sem):
    count = counts_ref[0, lax.axis_index("facet")]
    grid = [in_ref[:, half * SLICE : (half + 1) * SLICE, :].reshape(SGW, SGW) for half in range(2)]
    for part in range(VCAP // VBLOCK):
        cut = slice(part * VBLOCK, (part + 1) * VBLOCK)
        ku, kv = kernels(cut)
        live = part * VBLOCK + iota((1, VBLOCK), 1) < count
        weight = weight_ref[:, cut].astype(F32)
        for half in range(2):
            sampled = jnp.dot(grid[half], ku, preferred_element_type=F32)
            predicted = jnp.sum(sampled * kv.astype(F32), axis=0, keepdims=True)
            observed = obs_ref[half : half + 1, cut].astype(F32)
            residual = jnp.where(live, weight * (observed - predicted), 0.0)
            if res_ref is not None:
                res_ref[half : half + 1, cut] = residual
            weighted = (residual * kv.astype(F32)).astype(BF)
            total = lax.dot_general(
                weighted, ku, (((1,), (1,)), ((), ())), preferred_element_type=F32
            )
            if part:
                total = total + acc_ref[half]
            if part + 1 < VCAP // VBLOCK:
                acc_ref[half] = total
            else:
                lines = total.astype(BF).reshape(FACETS, SLICE, SGW)
                gridded_ref[:, half * SLICE : (half + 1) * SLICE, :] = lines
    write_out([(gridded_ref, gridded_hbm, sem)])


def first_kernel(counts_ref, obs_ref, weight_ref, in_ref, uv_ref, gridded_hbm, ku_ref, kv_ref, acc_ref, gridded_ref, sem):
    def kernels(cut):
        ku_ref[:, cut] = kernel_columns(uv_ref[0:1, cut])
        kv_ref[:, cut] = kernel_columns(uv_ref[1:2, cut])
        return ku_ref[:, cut], kv_ref[:, cut]

    visibility_pass(counts_ref, obs_ref, weight_ref, in_ref, kernels, gridded_hbm, None, acc_ref, gridded_ref, sem)


def last_kernel(counts_ref, obs_ref, weight_ref, in_ref, ku_ref, kv_ref, gridded_hbm, res_ref, acc_ref, gridded_ref, sem):
    def kernels(cut):
        return ku_ref[:, cut], kv_ref[:, cut]

    visibility_pass(counts_ref, obs_ref, weight_ref, in_ref, kernels, gridded_hbm, res_ref, acc_ref, gridded_ref, sem)


VIS_SCRATCH = [
    pltpu.VMEM((2, SGW, SGW), F32),
    pltpu.VMEM((FACETS, 2 * SLICE, SGW), BF),
    pltpu.SemaphoreType.DMA,
]


def first_visibilities(counts, obs, weight, grid, uv):
    return pl.pallas_call(
        first_kernel,
        out_shape=(
            jax.ShapeDtypeStruct((FACETS, 2 * SLICE, SGW), BF),
            pltpu.VMEM((SGW, VCAP), BF),
            pltpu.VMEM((SGW, VCAP), BF),
        ),
        in_specs=[SMEM_SPEC] + [VMEM_SPEC] * 4,
        out_specs=(HBM_SPEC, VMEM_SPEC, VMEM_SPEC),
        scratch_shapes=VIS_SCRATCH,
        compiler_params=PARAMS,
        name="first_visibilities",
    )(counts, obs, weight, on_chip(grid), uv)


def last_visibilities(counts, obs, weight, grid, ku, kv):
    return pl.pallas_call(
        last_kernel,
        out_shape=(
            jax.ShapeDtypeStruct((FACETS, 2 * SLICE, SGW), BF),
            jax.ShapeDtypeStruct((2, VCAP), F32),
        ),
        in_specs=[SMEM_SPEC] + [VMEM_SPEC] * 5,
        out_specs=(HBM_SPEC, VMEM_SPEC),
        scratch_shapes=VIS_SCRATCH,
        compiler_params=PARAMS,
        name="last_visibilities",
    )(counts, obs, weight, on_chip(grid), on_chip(ku), on_chip(kv))


def dirichlet(distance, pixel_start):
    distance = ((distance & (NIMG - 1)) ^ (NIMG // 2)) - NIMG // 2
    top = cos_sin((distance * (NIMG // (NIMG // FW * 2))) & (NIMG - 1))[1]
    bottom = cos_sin(distance, 17)[1]
    ratio = jnp.where(distance == 0, float(FW), top / jnp.where(distance == 0, 1.0, bottom))
    c, s = cos_sin((distance * (2 * pixel_start + FW - 1)) & (2 * NIMG - 1), 17)
    return c * ratio, s * ratio


def gram_kernel(step_ref, starts_ref, column_ref, offsets_ref, mine_ref, theirs_ref, first_ref, out_hbm, flip_ref, v_ref, out_ref, sem):
    wide = 2 * SGW
    pixel_start = offsets_ref[1, lax.axis_index("facet")]
    own = column_ref[0]
    row = iota((NCOL, wide), 0)
    starts = jnp.zeros((NCOL, wide), I32)
    for c in range(NCOL):
        starts = jnp.where(row == c, starts_ref[c], starts)
    lane = iota((NCOL, wide), 1)
    v_ref[0], v_ref[1] = dirichlet(starts - own + (lane - (SGW - 1)), pixel_start)
    v_ref[2], v_ref[3] = dirichlet(starts + own + (2 * (SGW - 1) - lane), pixel_start)
    anti = (iota((SGW, SGW), 0) + iota((SGW, SGW), 1)) == SGW - 1
    flip_ref[...] = jnp.where(anti, 1.0, 0.0).astype(BF)
    totals = [None] * 4
    for c in range(NCOL):
        lines = [half_ref[:, c].reshape(SGW, FROWS) for half_ref in (mine_ref, theirs_ref)]
        lines = jnp.concatenate(lines, axis=1)
        turned = jnp.dot(flip_ref[...], lines, preferred_element_type=F32).astype(BF)
        for k in range(4):
            spread = jnp.broadcast_to(v_ref[k, c : c + 1, :], (SGW, wide))
            band = pltpu.roll(spread, SGW + 1, 1, stride=1, stride_axis=0)[:, :SGW].astype(BF)
            term = jnp.dot(band, lines if k < 2 else turned, preferred_element_type=F32)
            totals[k] = term if c == 0 else totals[k] + term
    scale = step_ref[0] * (0.5 * NORM)
    p1, p2, p3, p4 = totals
    upper = (lax.axis_index("sub") & 1) == 1
    left = iota((SGW, FROWS), 1) < HALF

    def joined(straight, crossed):
        mine, theirs = [
            straight[:, k * FROWS : (k + 1) * FROWS] + pltpu.roll(crossed[:, k * FROWS : (k + 1) * FROWS], HALF, 1)
            for k in range(2)
        ]
        low = jnp.where(upper, theirs, mine)
        high = jnp.where(upper, mine, theirs)
        return jnp.where(left, low, pltpu.roll(high, HALF, 1))

    re = joined(p1 + p3, -(p2 + p4))
    im = joined(p2 - p4, p1 - p3)
    first = first_ref[...].astype(F32)
    out_ref[:, :SLICE, :] = (first[:, :SLICE] + (scale * re).reshape(FACETS, SLICE, FROWS)).astype(BF)
    out_ref[:, SLICE:, :] = (first[:, SLICE:] + (scale * im).reshape(FACETS, SLICE, FROWS)).astype(BF)
    write_out([(out_ref, out_hbm, sem)])


def gram(steps, column_starts, column_start, offsets, mine, theirs, first):
    shape = (FACETS, NCOL, SLICE, FROWS)
    return pl.pallas_call(
        gram_kernel,
        out_shape=jax.ShapeDtypeStruct((FACETS, 2 * SLICE, FROWS), BF),
        in_specs=[SMEM_SPEC] * 4 + [VMEM_SPEC] * 3,
        out_specs=HBM_SPEC,
        scratch_shapes=[
            pltpu.VMEM((SGW, SGW), BF),
            pltpu.VMEM((4, NCOL, 2 * SGW), F32),
            pltpu.VMEM((FACETS, 2 * SLICE, FROWS), BF),
            pltpu.SemaphoreType.DMA,
        ],
        compiler_params=PARAMS,
        name="gram",
    )(steps, column_starts, column_start, offsets, on_chip(mine.reshape(shape)), on_chip(theirs.reshape(shape)), first)


def update_kernel(step_ref, adj0_ref, adj1_ref, table_hbm, pc_ref, ps_ref, out_ref, table_ref, both_ref, even_ref, odd_ref, sem):
    part = pl.program_id(0)
    fetch = pltpu.make_async_copy(table_hbm, table_ref, sem)

    def turn(group, target_ref):
        re = both_ref[:HALF, :]
        im = both_ref[HALF:, :]
        for p in range(PAIR5):
            pc = pc_ref[pl.ds(group * PAIR5 + p, 1), :]
            ps = ps_ref[pl.ds(group * PAIR5 + p, 1), :]
            lines = slice(p * HALF, (p + 1) * HALF)
            target_ref[lines, :COLUMNS] = (re * pc - im * ps).astype(BF)
            target_ref[lines, COLUMNS:] = (im * pc + re * ps).astype(BF)

    def put(place, source_ref):
        gradient = jnp.dot(source_ref[...], table_ref[...], preferred_element_type=F32).astype(BF)
        for p in range(PAIR5):
            left = (place * PAIR5 + p) * STEP5
            out_ref[:, left : left + STEP5] = gradient[p * HALF : (p + 1) * HALF]

    @pl.when(part == 0)
    def _():
        fetch.start()
        first = step_ref[0] * NORM
        second = step_ref[1] * NORM
        group = NCOL * SLICE
        for j in range(FACETS):
            lines0 = adj0_ref[j * NCOL : (j + 1) * NCOL].reshape(group, FROWS).astype(F32)
            lines1 = adj1_ref[j * NCOL : (j + 1) * NCOL].reshape(group, FROWS).astype(F32)
            both_ref[:, j * group : (j + 1) * group] = (first * lines0 + second * lines1).T
        turn(0, even_ref)
        fetch.wait()

    turn(2 * part + 1, odd_ref)
    put(0, even_ref)
    turn(jnp.minimum(2 * part + 2, HIGH5 // PAIR5 - 2), even_ref)
    put(1, odd_ref)


def update(steps, adj0, adj1, tables):
    table, pc, ps = tables
    return pl.pallas_call(
        update_kernel,
        grid=(HIGH5 // PAIR5 // 2,),
        out_shape=jax.ShapeDtypeStruct((HALF, FW), BF),
        in_specs=[SMEM_SPEC, VMEM_SPEC, VMEM_SPEC, HBM_SPEC, VMEM_SPEC, VMEM_SPEC],
        out_specs=pl.BlockSpec((HALF, 2 * PAIR5 * STEP5), lambda i: (0, i)),
        scratch_shapes=[
            pltpu.VMEM((2 * COLUMNS, STEP5), BF),
            pltpu.VMEM((FROWS, COLUMNS), F32),
            pltpu.VMEM((PAIR5 * HALF, 2 * COLUMNS), BF),
            pltpu.VMEM((PAIR5 * HALF, 2 * COLUMNS), BF),
            pltpu.SemaphoreType.DMA,
        ],
        compiler_params=WIDE_PARAMS,
        name="update",
    )(steps, on_chip(adj0), on_chip(adj1), off_chip(table), on_chip(pc), on_chip(ps))


def step_kernel(mine_ref, theirs_ref, model_ref, out_hbm, out_ref, sems):
    upper = (lax.axis_index("sub") & 1) == 1
    wide = FW // PARTS7
    sent = []
    for part in range(PARTS7):
        cut = slice(part * wide, (part + 1) * wide)
        mine = mine_ref[:, cut].astype(F32)
        theirs = theirs_ref[:, cut].astype(F32)
        out_ref[:HALF, cut] = model_ref[:HALF, cut] + jnp.where(upper, theirs, mine)
        out_ref[HALF:, cut] = model_ref[HALF:, cut] + jnp.where(upper, mine, theirs)
        lanes = pl.ds(part * wide, wide)
        sent.append(pltpu.make_async_copy(out_ref.at[:, lanes], out_hbm.at[:, lanes], sems.at[part]))
        sent[-1].start()
    for copy in sent:
        copy.wait()


def take_step(mine, theirs, model):
    return pl.pallas_call(
        step_kernel,
        out_shape=jax.ShapeDtypeStruct((FROWS, FW), F32),
        in_specs=[VMEM_SPEC] * 3,
        out_specs=HBM_SPEC,
        scratch_shapes=[pltpu.VMEM((FROWS, FW), F32), pltpu.SemaphoreType.DMA((PARTS7,))],
        compiler_params=PARAMS,
        name="take_step",
    )(on_chip(mine), on_chip(theirs), on_chip(model))


def update_table_kernel(starts_ref, offsets_ref, table_hbm, pc_ref, ps_ref, table_ref, base_ref, turn_ref, sem):
    group = NCOL * SLICE
    line = iota((group, STEP5), 0)
    freq = line & (SLICE - 1)
    for c in range(NCOL):
        freq = freq + jnp.where((line >> 4) == c, starts_ref[c], 0)
    base_ref[0], base_ref[1] = phase(freq, iota((group, STEP5), 1))
    turn_ref[0], turn_ref[1] = phase(SLICE * iota((FACETS, STEP5), 0), iota((FACETS, STEP5), 1))

    def one(j, carry):
        c = turn_ref[0, pl.ds(j, 1), :]
        s = turn_ref[1, pl.ds(j, 1), :]
        cut = pl.ds(pl.multiple_of(j * group, group), group)
        table_ref[cut, :] = (base_ref[0] * c - base_ref[1] * s).astype(BF)
        cut = pl.ds(pl.multiple_of(COLUMNS + j * group, group), group)
        table_ref[cut, :] = (-(base_ref[1] * c + base_ref[0] * s)).astype(BF)
        return carry

    lax.fori_loop(0, FACETS, one, 0)
    lane = iota((HIGH5, COLUMNS), 1)
    freq = SLICE * (lane >> 7) + (lane & (SLICE - 1))
    for c in range(NCOL):
        freq = freq + jnp.where(((lane >> 4) & (NCOL - 1)) == c, starts_ref[c], 0)
    pixel_start = offsets_ref[1, lax.axis_index("facet")]
    pc_ref[...], ps_ref[...] = phase(freq, pixel_start + STEP5 * iota((HIGH5, COLUMNS), 0))
    write_out([(table_ref, table_hbm, sem)])


def update_tables(column_starts, offsets):
    return pl.pallas_call(
        update_table_kernel,
        out_shape=(
            pltpu.HBM((2 * COLUMNS, STEP5), BF),
            pltpu.VMEM((HIGH5, COLUMNS), F32),
            pltpu.VMEM((HIGH5, COLUMNS), F32),
        ),
        in_specs=[SMEM_SPEC, SMEM_SPEC],
        out_specs=(HBM_SPEC, VMEM_SPEC, VMEM_SPEC),
        scratch_shapes=[
            pltpu.VMEM((2 * COLUMNS, STEP5), BF),
            pltpu.VMEM((2, NCOL * SLICE, STEP5), F32),
            pltpu.VMEM((2, FACETS, STEP5), F32),
            pltpu.SemaphoreType.DMA,
        ],
        compiler_params=PARAMS,
        name="update_tables",
    )(column_starts, offsets)


def exchange(value):
    return lax.all_to_all(value, "facet", split_axis=0, concat_axis=0, tiled=True)


def swapped(value, bit):
    return lax.ppermute(value, "sub", [(i, i ^ bit) for i in range(NCOL)])


def to_facets(value):
    copies = value.reshape(FACETS * NCOL, *value.shape[2:])
    return lax.all_to_all(copies, ("facet", "sub"), split_axis=0, concat_axis=0, tiled=True)


def local(
    model_image,
    step_sizes,
    facet_offsets,
    col_offsets,
    row_offsets,
    counts,
    vis_uv,
    vis_obs,
    vis_weight,
):
    mine = jnp.arange(NCOL, dtype=I32) == lax.axis_index("sub")
    column_starts = jnp.where(mine, col_offsets[0], 0)
    for bit in (1, 2):
        column_starts = column_starts + swapped(column_starts, bit)
    uv = vis_uv.reshape(2, VCAP)
    obs = vis_obs.reshape(2, VCAP)
    weight = vis_weight.reshape(1, VCAP)
    model = model_image[0]
    first = section(col_offsets, facet_offsets, model)
    rows = row_tables(facet_offsets, row_offsets)
    sections, column_starts = lax.optimization_barrier((exchange(first), column_starts))
    column_starts = column_starts + swapped(column_starts, 4)
    grid = exchange(grids(sections, rows))
    gridded, ku, kv = first_visibilities(counts, obs, weight, grid, uv)
    gridded, column_starts = lax.optimization_barrier((gridded, column_starts))
    adj0 = to_facets(adjoint(exchange(gridded), rows))
    second = gram(step_sizes, column_starts, col_offsets, facet_offsets, adj0, swapped(adj0, 1), first)
    grid = exchange(grids(exchange(second), rows))
    gridded, residual = last_visibilities(counts, obs, weight, grid, ku, kv)
    adj1 = to_facets(adjoint(exchange(gridded), rows))
    tables = update_tables(column_starts, facet_offsets)
    step = update(step_sizes, adj0, adj1, tables)
    model = take_step(step, swapped(step, 1), model)
    return model[None], residual.reshape(2, 1, 1, VCAP)


def solution(mesh):
    in_specs = (
        P("facet", None, None),
        P(),
        P(),
        P("sub"),
        P("sub", None),
        P("sub", None),
        P(None, "sub", "facet", None),
        P(None, "sub", "facet", None),
        P("sub", "facet", None),
    )
    out_specs = (P("facet", None, None), P(None, "sub", "facet", None))
    return jax.shard_map(local, mesh=mesh, in_specs=in_specs, out_specs=out_specs, check_vma=False)
```

```python
import math

import jax
import jax.numpy as jnp
from jax import lax
from jax.experimental import pallas as pl
from jax.experimental.pallas import tpu as pltpu
from jax.sharding import PartitionSpec as P

NIMG = 65536
FW = 8192
FROWS = 128
SGW = 256
VCAP = 4096
OS = 8
KSUP = 4
FACETS = 16
NCOL = 8
NROWSG = 16
SLICE = SGW // FACETS
COLUMNS = NCOL * SGW

STEP1 = 256
HIGH1 = FW // STEP1
PARTS1 = 4
GROUP1 = 8
ROWS1 = 64
STEP5 = 512
HIGH5 = FW // STEP5
PAIR5 = 4
HALF = FROWS // 2
PARTS7 = 4
VBLOCK = 1024
CHUNK = 4
UNROLL4 = 8

BF = jnp.bfloat16
F32 = jnp.float32
I32 = jnp.int32
NORM = 1.0 / math.sqrt(FACETS * FROWS * FW)
PARAMS = pltpu.CompilerParams(vmem_limit_bytes=16 << 20)
WIDE_PARAMS = pltpu.CompilerParams(vmem_limit_bytes=24 << 20)
SMEM_SPEC = pl.BlockSpec(memory_space=pltpu.SMEM)
VMEM_SPEC = pl.BlockSpec(memory_space=pltpu.VMEM)
HBM_SPEC = pl.BlockSpec(memory_space=pltpu.HBM)


def cos_sin(index, bits=16):
    quadrant = (index + (1 << (bits - 3))) >> (bits - 2)
    angle = (index - (quadrant << (bits - 2))).astype(F32) * (2.0 * math.pi / (1 << bits))
    square = angle * angle
    sine = angle * (1.0 + square * (-1.0 / 6 + square * (1.0 / 120 + square * (-1.0 / 5040 + square / 362880))))
    cosine = 1.0 + square * (-0.5 + square * (1.0 / 24 + square * (-1.0 / 720 + square / 40320)))
    swapped = (quadrant & 1) != 0
    c = jnp.where(swapped, sine, cosine)
    s = jnp.where(swapped, cosine, sine)
    c = jnp.where(((quadrant + 1) & 2) != 0, -c, c)
    s = jnp.where((quadrant & 2) != 0, -s, s)
    return c, s


def phase(frequency, pixel):
    return cos_sin((frequency * pixel) & (NIMG - 1))


def on_chip(value):
    return pltpu.with_memory_space_constraint(value, pltpu.VMEM)


def off_chip(value):
    return pltpu.with_memory_space_constraint(value, pltpu.HBM)


def write_out(pairs):
    copies = [pltpu.make_async_copy(source, target, sem) for source, target, sem in pairs]
    for copy in copies:
        copy.start()
    for copy in copies:
        copy.wait()


def iota(shape, dim):
    return lax.broadcasted_iota(I32, shape, dim)


def column_of(ref, count, lanes):
    row = iota((count, lanes), 0)
    value = jnp.zeros((count, lanes), I32)
    for i in range(count):
        value = jnp.where(row == i, ref[i], value)
    return value


def section_kernel(column_ref, offsets_ref, model_hbm, out_hbm, model_ref, table_ref, pc_ref, ps_ref, block_ref, acc_ref, out_ref, sems, sem):
    wide = FW // PARTS1
    fetches = []
    for part in range(PARTS1):
        cut = pl.ds(part * wide, wide)
        fetches.append(pltpu.make_async_copy(model_hbm.at[:, cut], model_ref.at[:, cut], sems.at[part]))
        fetches[-1].start()
    column_start = column_ref[0]
    pixel_start = offsets_ref[1, lax.axis_index("facet")]
    freq = column_start + iota((STEP1, SGW), 1)
    c, s = phase(freq, iota((STEP1, SGW), 0))
    table_ref[:, :SGW] = c.astype(BF)
    table_ref[:, SGW:] = (-s).astype(BF)
    freq = column_start + iota((HIGH1, SGW), 1)
    pc_ref[...], ps_ref[...] = phase(freq, pixel_start + STEP1 * iota((HIGH1, SGW), 0))
    for first in range(0, HIGH1, GROUP1):
        if first % (HIGH1 // PARTS1) == 0:
            fetches[first // (HIGH1 // PARTS1)].wait()
        for k in range(GROUP1):
            cut = slice((first + k) * STEP1, (first + k + 1) * STEP1)
            block_ref[k * FROWS : (k + 1) * FROWS] = model_ref[:, cut].astype(BF)
        product = jnp.dot(block_ref[...], table_ref[...], preferred_element_type=F32)
        for row in range(0, FROWS, ROWS1):
            lines = slice(row, row + ROWS1)
            acc_re = acc_ref[0, lines, :] if first else 0.0
            acc_im = acc_ref[1, lines, :] if first else 0.0
            for k in range(GROUP1):
                re = product[k * FROWS + row : k * FROWS + row + ROWS1, :SGW]
                im = product[k * FROWS + row : k * FROWS + row + ROWS1, SGW:]
                pc = pc_ref[first + k : first + k + 1, :]
                ps = ps_ref[first + k : first + k + 1, :]
                acc_re = acc_re + (re * pc + im * ps)
                acc_im = acc_im + (im * pc - re * ps)
            acc_ref[0, lines, :] = acc_re
            acc_ref[1, lines, :] = acc_im
    out_ref[:, :SLICE, :] = acc_ref[0].T.astype(BF).reshape(FACETS, SLICE, FROWS)
    out_ref[:, SLICE:, :] = acc_ref[1].T.astype(BF).reshape(FACETS, SLICE, FROWS)
    write_out([(out_ref, out_hbm, sem)])


def section(column_start, offsets, model):
    return pl.pallas_call(
        section_kernel,
        out_shape=jax.ShapeDtypeStruct((FACETS, 2 * SLICE, FROWS), BF),
        in_specs=[SMEM_SPEC, SMEM_SPEC, HBM_SPEC],
        out_specs=HBM_SPEC,
        scratch_shapes=[
            pltpu.VMEM((FROWS, FW), F32),
            pltpu.VMEM((STEP1, 2 * SGW), BF),
            pltpu.VMEM((HIGH1, SGW), F32),
            pltpu.VMEM((HIGH1, SGW), F32),
            pltpu.VMEM((GROUP1 * FROWS, STEP1), BF),
            pltpu.VMEM((2, FROWS, SGW), F32),
            pltpu.VMEM((FACETS, 2 * SLICE, FROWS), BF),
            pltpu.SemaphoreType.DMA((PARTS1,)),
            pltpu.SemaphoreType.DMA,
        ],
        compiler_params=PARAMS,
        name="section",
    )(column_start, off_chip(offsets), off_chip(model))


def kernel_columns(position):
    cells = (iota((SGW, position.shape[1]), 0) * OS + OS // 2).astype(F32)
    offset = cells - position.astype(F32)
    square = offset * offset
    value = jnp.exp2(square * (-0.5 / (OS * OS) / math.log(2.0)))
    return jnp.where(square <= float((KSUP * OS) ** 2), value, 0.0).astype(BF)


def row_table_kernel(offsets_ref, rows_ref, table_ref, c_ref, s_ref, base_ref, turn_ref):
    base_ref[0], base_ref[1] = phase(iota((FROWS, SGW), 1), iota((FROWS, SGW), 0))
    row = iota((FACETS, SGW), 0)
    start = jnp.zeros((FACETS, SGW), I32)
    for f in range(FACETS):
        start = jnp.where(row == f, offsets_ref[0, f], start)
    turn_ref[0], turn_ref[1] = phase(iota((FACETS, SGW), 1), start)
    row = iota((NROWSG, FROWS), 0)
    freq = jnp.zeros((NROWSG, FROWS), I32)
    for r in range(NROWSG):
        freq = jnp.where(row == r, rows_ref[0, r], freq)

    def one(f, carry):
        cf = turn_ref[0, pl.ds(f, 1), :]
        sf = turn_ref[1, pl.ds(f, 1), :]
        lines = pl.ds(pl.multiple_of(f * FROWS, FROWS), FROWS)
        table_ref[0, lines, :] = (base_ref[0] * cf - base_ref[1] * sf).astype(BF)
        table_ref[1, lines, :] = (base_ref[1] * cf + base_ref[0] * sf).astype(BF)
        c_ref[f], s_ref[f] = phase(freq, offsets_ref[0, f] + iota((NROWSG, FROWS), 1))
        return carry

    lax.fori_loop(0, FACETS, one, 0)


def row_tables(offsets, rows):
    return pl.pallas_call(
        row_table_kernel,
        out_shape=(
            pltpu.VMEM((2, FACETS * FROWS, SGW), BF),
            pltpu.VMEM((FACETS, NROWSG, FROWS), F32),
            pltpu.VMEM((FACETS, NROWSG, FROWS), F32),
        ),
        in_specs=[SMEM_SPEC, SMEM_SPEC],
        out_specs=(VMEM_SPEC,) * 3,
        scratch_shapes=[
            pltpu.VMEM((2, FROWS, SGW), F32),
            pltpu.VMEM((2, FACETS, SGW), F32),
        ],
        compiler_params=PARAMS,
        name="row_tables",
    )(offsets, rows)


def grid_kernel(in_ref, c_ref, s_ref, table_ref, out_hbm, turned_ref, out_ref, sem):
    half = NROWSG * SLICE
    for f in range(FACETS):
        re = in_ref[f, :SLICE, :].astype(F32)
        im = in_ref[f, SLICE:, :].astype(F32)
        cut = slice(f * FROWS, (f + 1) * FROWS)
        for r in range(NROWSG):
            c = c_ref[f, r : r + 1, :]
            s = s_ref[f, r : r + 1, :]
            turned_ref[r * SLICE : (r + 1) * SLICE, cut] = (re * c + im * s).astype(BF)
            turned_ref[half + r * SLICE : half + (r + 1) * SLICE, cut] = (im * c - re * s).astype(BF)
    by_c = jnp.dot(turned_ref[...], table_ref[0], preferred_element_type=F32)
    by_s = jnp.dot(turned_ref[...], table_ref[1], preferred_element_type=F32)
    re = (NORM * (by_c[:half] + by_s[half:])).astype(BF)
    im = (NORM * (by_c[half:] - by_s[:half])).astype(BF)
    out_ref[:, :SLICE, :] = re.reshape(NROWSG, SLICE, SGW)
    out_ref[:, SLICE:, :] = im.reshape(NROWSG, SLICE, SGW)
    write_out([(out_ref, out_hbm, sem)])


def grids(sections, tables):
    table, c, s = tables
    return pl.pallas_call(
        grid_kernel,
        out_shape=jax.ShapeDtypeStruct((NROWSG, 2 * SLICE, SGW), BF),
        in_specs=[VMEM_SPEC] * 4,
        out_specs=HBM_SPEC,
        scratch_shapes=[
            pltpu.VMEM((2 * NROWSG * SLICE, FACETS * FROWS), BF),
            pltpu.VMEM((NROWSG, 2 * SLICE, SGW), BF),
            pltpu.SemaphoreType.DMA,
        ],
        compiler_params=PARAMS,
        name="grids",
    )(on_chip(sections), on_chip(c), on_chip(s), on_chip(table))


def adjoint_kernel(in_ref, c_ref, s_ref, table_ref, out_hbm, lines_ref, out_ref, sems):
    half = NROWSG * SLICE
    lines_ref[:half] = in_ref[:, :SLICE, :].reshape(half, SGW)
    lines_ref[half:] = in_ref[:, SLICE:, :].reshape(half, SGW)

    def one(pair, carry):
        cut = pl.ds(pl.multiple_of(pair * 2 * FROWS, 2 * FROWS), 2 * FROWS)
        dims = (((1,), (1,)), ((), ()))
        by_c = lax.dot_general(lines_ref[...], table_ref[0, cut, :], dims, preferred_element_type=F32)
        by_s = lax.dot_general(lines_ref[...], table_ref[1, cut, :], dims, preferred_element_type=F32)
        for k in range(2):
            f = 2 * pair + k
            lanes = slice(k * FROWS, (k + 1) * FROWS)
            acc_re = jnp.zeros((SLICE, FROWS), F32)
            acc_im = jnp.zeros((SLICE, FROWS), F32)
            for r in range(NROWSG):
                top = slice(r * SLICE, (r + 1) * SLICE)
                low = slice(half + r * SLICE, half + (r + 1) * SLICE)
                re = by_c[top, lanes] - by_s[low, lanes]
                im = by_c[low, lanes] + by_s[top, lanes]
                c = c_ref[f, r : r + 1, :]
                s = s_ref[f, r : r + 1, :]
                acc_re = acc_re + (re * c - im * s)
                acc_im = acc_im + (im * c + re * s)
            lower = iota((SLICE, FROWS), 1) < HALF
            out_ref[0, f] = jnp.where(lower, acc_re, pltpu.roll(acc_im, HALF, 1)).astype(BF)
            out_ref[1, f] = jnp.where(lower, pltpu.roll(acc_re, HALF, 1), acc_im).astype(BF)
        return carry

    lax.fori_loop(0, FACETS // 2, one, 0, unroll=UNROLL4)
    write_out([(out_ref.at[copy % 2], out_hbm.at[:, copy], sems.at[copy]) for copy in range(NCOL)])


def adjoint(gridded, tables):
    table, c, s = tables
    return pl.pallas_call(
        adjoint_kernel,
        out_shape=jax.ShapeDtypeStruct((FACETS, NCOL, SLICE, FROWS), BF),
        in_specs=[VMEM_SPEC] * 4,
        out_specs=HBM_SPEC,
        scratch_shapes=[
            pltpu.VMEM((2 * NROWSG * SLICE, SGW), BF),
            pltpu.VMEM((2, FACETS, SLICE, FROWS), BF),
            pltpu.SemaphoreType.DMA((NCOL,)),
        ],
        compiler_params=PARAMS,
        name="adjoint",
    )(on_chip(gridded), on_chip(c), on_chip(s), on_chip(table))


def visibility_pass(counts_ref, obs_ref, weight_ref, in_ref, kernels, gridded_hbm, res_ref, acc_ref, gridded_ref, sem):
    count = counts_ref[0, lax.axis_index("facet")]
    grid = [in_ref[:, half * SLICE : (half + 1) * SLICE, :].reshape(SGW, SGW) for half in range(2)]
    for part in range(VCAP // VBLOCK):
        cut = slice(part * VBLOCK, (part + 1) * VBLOCK)
        ku, kv = kernels(cut)
        live = part * VBLOCK + iota((1, VBLOCK), 1) < count
        weight = weight_ref[:, cut].astype(F32)
        for half in range(2):
            sampled = jnp.dot(grid[half], ku, preferred_element_type=F32)
            predicted = jnp.sum(sampled * kv.astype(F32), axis=0, keepdims=True)
            observed = obs_ref[half : half + 1, cut].astype(F32)
            residual = jnp.where(live, weight * (observed - predicted), 0.0)
            if res_ref is not None:
                res_ref[half : half + 1, cut] = residual
            weighted = (residual * kv.astype(F32)).astype(BF)
            total = lax.dot_general(
                weighted, ku, (((1,), (1,)), ((), ())), preferred_element_type=F32
            )
            if part:
                total = total + acc_ref[half]
            if part + 1 < VCAP // VBLOCK:
                acc_ref[half] = total
            else:
                lines = total.astype(BF).reshape(FACETS, SLICE, SGW)
                gridded_ref[:, half * SLICE : (half + 1) * SLICE, :] = lines
    write_out([(gridded_ref, gridded_hbm, sem)])


def first_kernel(counts_ref, obs_ref, weight_ref, in_ref, uv_ref, gridded_hbm, ku_ref, kv_ref, acc_ref, gridded_ref, sem):
    def kernels(cut):
        ku_ref[:, cut] = kernel_columns(uv_ref[0:1, cut])
        kv_ref[:, cut] = kernel_columns(uv_ref[1:2, cut])
        return ku_ref[:, cut], kv_ref[:, cut]

    visibility_pass(counts_ref, obs_ref, weight_ref, in_ref, kernels, gridded_hbm, None, acc_ref, gridded_ref, sem)


def last_kernel(counts_ref, obs_ref, weight_ref, in_ref, ku_ref, kv_ref, gridded_hbm, res_ref, acc_ref, gridded_ref, sem):
    def kernels(cut):
        return ku_ref[:, cut], kv_ref[:, cut]

    visibility_pass(counts_ref, obs_ref, weight_ref, in_ref, kernels, gridded_hbm, res_ref, acc_ref, gridded_ref, sem)


VIS_SCRATCH = [
    pltpu.VMEM((2, SGW, SGW), F32),
    pltpu.VMEM((FACETS, 2 * SLICE, SGW), BF),
    pltpu.SemaphoreType.DMA,
]


def first_visibilities(counts, obs, weight, grid, uv):
    return pl.pallas_call(
        first_kernel,
        out_shape=(
            jax.ShapeDtypeStruct((FACETS, 2 * SLICE, SGW), BF),
            pltpu.VMEM((SGW, VCAP), BF),
            pltpu.VMEM((SGW, VCAP), BF),
        ),
        in_specs=[SMEM_SPEC] + [VMEM_SPEC] * 4,
        out_specs=(HBM_SPEC, VMEM_SPEC, VMEM_SPEC),
        scratch_shapes=VIS_SCRATCH,
        compiler_params=PARAMS,
        name="first_visibilities",
    )(counts, obs, weight, on_chip(grid), uv)


def last_visibilities(counts, obs, weight, grid, ku, kv):
    return pl.pallas_call(
        last_kernel,
        out_shape=(
            jax.ShapeDtypeStruct((FACETS, 2 * SLICE, SGW), BF),
            jax.ShapeDtypeStruct((2, VCAP), F32),
        ),
        in_specs=[SMEM_SPEC] + [VMEM_SPEC] * 5,
        out_specs=(HBM_SPEC, VMEM_SPEC),
        scratch_shapes=VIS_SCRATCH,
        compiler_params=PARAMS,
        name="last_visibilities",
    )(counts, obs, weight, on_chip(grid), on_chip(ku), on_chip(kv))


def dirichlet(distance, pixel_start):
    distance = ((distance & (NIMG - 1)) ^ (NIMG // 2)) - NIMG // 2
    top = cos_sin((distance * (NIMG // (NIMG // FW * 2))) & (NIMG - 1))[1]
    bottom = cos_sin(distance, 17)[1]
    ratio = jnp.where(distance == 0, float(FW), top / jnp.where(distance == 0, 1.0, bottom))
    c, s = cos_sin((distance * (2 * pixel_start + FW - 1)) & (2 * NIMG - 1), 17)
    return c * ratio, s * ratio


def gram_kernel(step_ref, starts_ref, column_ref, offsets_ref, mine_ref, theirs_ref, first_ref, out_hbm, flip_ref, v_ref, out_ref, sem):
    wide = 2 * SGW
    pixel_start = offsets_ref[1, lax.axis_index("facet")]
    own = column_ref[0]
    row = iota((NCOL, wide), 0)
    starts = jnp.zeros((NCOL, wide), I32)
    for c in range(NCOL):
        starts = jnp.where(row == c, starts_ref[c], starts)
    lane = iota((NCOL, wide), 1)
    v_ref[0], v_ref[1] = dirichlet(starts - own + (lane - (SGW - 1)), pixel_start)
    v_ref[2], v_ref[3] = dirichlet(starts + own + (2 * (SGW - 1) - lane), pixel_start)
    anti = (iota((SGW, SGW), 0) + iota((SGW, SGW), 1)) == SGW - 1
    flip_ref[...] = jnp.where(anti, 1.0, 0.0).astype(BF)
    totals = [None] * 4
    for c in range(NCOL):
        lines = [half_ref[:, c].reshape(SGW, FROWS) for half_ref in (mine_ref, theirs_ref)]
        lines = jnp.concatenate(lines, axis=1)
        turned = jnp.dot(flip_ref[...], lines, preferred_element_type=F32).astype(BF)
        for k in range(4):
            spread = jnp.broadcast_to(v_ref[k, c : c + 1, :], (SGW, wide))
            band = pltpu.roll(spread, SGW + 1, 1, stride=1, stride_axis=0)[:, :SGW].astype(BF)
            term = jnp.dot(band, lines if k < 2 else turned, preferred_element_type=F32)
            totals[k] = term if c == 0 else totals[k] + term
    scale = step_ref[0] * (0.5 * NORM)
    p1, p2, p3, p4 = totals
    upper = (lax.axis_index("sub") & 1) == 1
    left = iota((SGW, FROWS), 1) < HALF

    def joined(straight, crossed):
        mine, theirs = [
            straight[:, k * FROWS : (k + 1) * FROWS] + pltpu.roll(crossed[:, k * FROWS : (k + 1) * FROWS], HALF, 1)
            for k in range(2)
        ]
        low = jnp.where(upper, theirs, mine)
        high = jnp.where(upper, mine, theirs)
        return jnp.where(left, low, pltpu.roll(high, HALF, 1))

    re = joined(p1 + p3, -(p2 + p4))
    im = joined(p2 - p4, p1 - p3)
    first = first_ref[...].astype(F32)
    out_ref[:, :SLICE, :] = (first[:, :SLICE] + (scale * re).reshape(FACETS, SLICE, FROWS)).astype(BF)
    out_ref[:, SLICE:, :] = (first[:, SLICE:] + (scale * im).reshape(FACETS, SLICE, FROWS)).astype(BF)
    write_out([(out_ref, out_hbm, sem)])


def gram(steps, column_starts, column_start, offsets, mine, theirs, first):
    shape = (FACETS, NCOL, SLICE, FROWS)
    return pl.pallas_call(
        gram_kernel,
        out_shape=jax.ShapeDtypeStruct((FACETS, 2 * SLICE, FROWS), BF),
        in_specs=[SMEM_SPEC] * 4 + [VMEM_SPEC] * 3,
        out_specs=HBM_SPEC,
        scratch_shapes=[
            pltpu.VMEM((SGW, SGW), BF),
            pltpu.VMEM((4, NCOL, 2 * SGW), F32),
            pltpu.VMEM((FACETS, 2 * SLICE, FROWS), BF),
            pltpu.SemaphoreType.DMA,
        ],
        compiler_params=PARAMS,
        name="gram",
    )(steps, column_starts, column_start, offsets, on_chip(mine.reshape(shape)), on_chip(theirs.reshape(shape)), first)


def update_kernel(step_ref, adj0_ref, adj1_ref, table_hbm, pc_ref, ps_ref, out_ref, table_ref, both_ref, even_ref, odd_ref, sem):
    part = pl.program_id(0)
    fetch = pltpu.make_async_copy(table_hbm, table_ref, sem)

    def turn(group, target_ref):
        re = both_ref[:HALF, :]
        im = both_ref[HALF:, :]
        for p in range(PAIR5):
            pc = pc_ref[pl.ds(group * PAIR5 + p, 1), :]
            ps = ps_ref[pl.ds(group * PAIR5 + p, 1), :]
            lines = slice(p * HALF, (p + 1) * HALF)
            target_ref[lines, :COLUMNS] = (re * pc - im * ps).astype(BF)
            target_ref[lines, COLUMNS:] = (im * pc + re * ps).astype(BF)

    def put(place, source_ref):
        gradient = jnp.dot(source_ref[...], table_ref[...], preferred_element_type=F32).astype(BF)
        for p in range(PAIR5):
            left = (place * PAIR5 + p) * STEP5
            out_ref[:, left : left + STEP5] = gradient[p * HALF : (p + 1) * HALF]

    @pl.when(part == 0)
    def _():
        fetch.start()
        first = step_ref[0] * NORM
        second = step_ref[1] * NORM
        group = NCOL * SLICE
        for j in range(FACETS):
            lines0 = adj0_ref[j * NCOL : (j + 1) * NCOL].reshape(group, FROWS).astype(F32)
            lines1 = adj1_ref[j * NCOL : (j + 1) * NCOL].reshape(group, FROWS).astype(F32)
            both_ref[:, j * group : (j + 1) * group] = (first * lines0 + second * lines1).T
        turn(0, even_ref)
        fetch.wait()

    turn(2 * part + 1, odd_ref)
    put(0, even_ref)
    turn(jnp.minimum(2 * part + 2, HIGH5 // PAIR5 - 2), even_ref)
    put(1, odd_ref)


def update(steps, adj0, adj1, tables):
    table, pc, ps = tables
    return pl.pallas_call(
        update_kernel,
        grid=(HIGH5 // PAIR5 // 2,),
        out_shape=jax.ShapeDtypeStruct((HALF, FW), BF),
        in_specs=[SMEM_SPEC, VMEM_SPEC, VMEM_SPEC, HBM_SPEC, VMEM_SPEC, VMEM_SPEC],
        out_specs=pl.BlockSpec((HALF, 2 * PAIR5 * STEP5), lambda i: (0, i)),
        scratch_shapes=[
            pltpu.VMEM((2 * COLUMNS, STEP5), BF),
            pltpu.VMEM((FROWS, COLUMNS), F32),
            pltpu.VMEM((PAIR5 * HALF, 2 * COLUMNS), BF),
            pltpu.VMEM((PAIR5 * HALF, 2 * COLUMNS), BF),
            pltpu.SemaphoreType.DMA,
        ],
        compiler_params=WIDE_PARAMS,
        name="update",
    )(steps, on_chip(adj0), on_chip(adj1), off_chip(table), on_chip(pc), on_chip(ps))


def step_kernel(mine_ref, theirs_ref, model_ref, out_hbm, out_ref, sems):
    upper = (lax.axis_index("sub") & 1) == 1
    wide = FW // PARTS7
    sent = []
    for part in range(PARTS7):
        cut = slice(part * wide, (part + 1) * wide)
        mine = mine_ref[:, cut].astype(F32)
        theirs = theirs_ref[:, cut].astype(F32)
        out_ref[:HALF, cut] = model_ref[:HALF, cut] + jnp.where(upper, theirs, mine)
        out_ref[HALF:, cut] = model_ref[HALF:, cut] + jnp.where(upper, mine, theirs)
        lanes = pl.ds(part * wide, wide)
        sent.append(pltpu.make_async_copy(out_ref.at[:, lanes], out_hbm.at[:, lanes], sems.at[part]))
        sent[-1].start()
    for copy in sent:
        copy.wait()


def take_step(mine, theirs, model):
    return pl.pallas_call(
        step_kernel,
        out_shape=jax.ShapeDtypeStruct((FROWS, FW), F32),
        in_specs=[VMEM_SPEC] * 3,
        out_specs=HBM_SPEC,
        scratch_shapes=[pltpu.VMEM((FROWS, FW), F32), pltpu.SemaphoreType.DMA((PARTS7,))],
        compiler_params=PARAMS,
        name="take_step",
    )(on_chip(mine), on_chip(theirs), on_chip(model))


def update_table_kernel(starts_ref, offsets_ref, table_hbm, pc_ref, ps_ref, table_ref, base_ref, turn_ref, sem):
    group = NCOL * SLICE
    line = iota((group, STEP5), 0)
    freq = line & (SLICE - 1)
    for c in range(NCOL):
        freq = freq + jnp.where((line >> 4) == c, starts_ref[c], 0)
    base_ref[0], base_ref[1] = phase(freq, iota((group, STEP5), 1))
    turn_ref[0], turn_ref[1] = phase(SLICE * iota((FACETS, STEP5), 0), iota((FACETS, STEP5), 1))

    def one(j, carry):
        c = turn_ref[0, pl.ds(j, 1), :]
        s = turn_ref[1, pl.ds(j, 1), :]
        cut = pl.ds(pl.multiple_of(j * group, group), group)
        table_ref[cut, :] = (base_ref[0] * c - base_ref[1] * s).astype(BF)
        cut = pl.ds(pl.multiple_of(COLUMNS + j * group, group), group)
        table_ref[cut, :] = (-(base_ref[1] * c + base_ref[0] * s)).astype(BF)
        return carry

    lax.fori_loop(0, FACETS, one, 0)
    lane = iota((HIGH5, COLUMNS), 1)
    freq = SLICE * (lane >> 7) + (lane & (SLICE - 1))
    for c in range(NCOL):
        freq = freq + jnp.where(((lane >> 4) & (NCOL - 1)) == c, starts_ref[c], 0)
    pixel_start = offsets_ref[1, lax.axis_index("facet")]
    pc_ref[...], ps_ref[...] = phase(freq, pixel_start + STEP5 * iota((HIGH5, COLUMNS), 0))
    write_out([(table_ref, table_hbm, sem)])


def update_tables(column_starts, offsets):
    return pl.pallas_call(
        update_table_kernel,
        out_shape=(
            pltpu.HBM((2 * COLUMNS, STEP5), BF),
            pltpu.VMEM((HIGH5, COLUMNS), F32),
            pltpu.VMEM((HIGH5, COLUMNS), F32),
        ),
        in_specs=[SMEM_SPEC, SMEM_SPEC],
        out_specs=(HBM_SPEC, VMEM_SPEC, VMEM_SPEC),
        scratch_shapes=[
            pltpu.VMEM((2 * COLUMNS, STEP5), BF),
            pltpu.VMEM((2, NCOL * SLICE, STEP5), F32),
            pltpu.VMEM((2, FACETS, STEP5), F32),
            pltpu.SemaphoreType.DMA,
        ],
        compiler_params=PARAMS,
        name="update_tables",
    )(column_starts, offsets)


def exchange(value):
    return lax.all_to_all(value, "facet", split_axis=0, concat_axis=0, tiled=True)


def swapped(value, bit):
    return lax.ppermute(value, "sub", [(i, i ^ bit) for i in range(NCOL)])


def to_facets(value):
    copies = value.reshape(FACETS * NCOL, *value.shape[2:])
    return lax.all_to_all(copies, ("facet", "sub"), split_axis=0, concat_axis=0, tiled=True)


def local(
    model_image,
    step_sizes,
    facet_offsets,
    col_offsets,
    row_offsets,
    counts,
    vis_uv,
    vis_obs,
    vis_weight,
):
    mine = jnp.arange(NCOL, dtype=I32) == lax.axis_index("sub")
    column_starts = jnp.where(mine, col_offsets[0], 0)
    for bit in (1, 2):
        column_starts = column_starts + swapped(column_starts, bit)
    uv = vis_uv.reshape(2, VCAP)
    obs = vis_obs.reshape(2, VCAP)
    weight = vis_weight.reshape(1, VCAP)
    model = model_image[0]
    first = section(col_offsets, facet_offsets, model)
    rows = row_tables(facet_offsets, row_offsets)
    sections, column_starts = lax.optimization_barrier((exchange(first), column_starts))
    column_starts = column_starts + swapped(column_starts, 4)
    grid = exchange(grids(sections, rows))
    gridded, ku, kv = first_visibilities(counts, obs, weight, grid, uv)
    gridded, column_starts = lax.optimization_barrier((gridded, column_starts))
    adj0 = to_facets(adjoint(exchange(gridded), rows))
    second = gram(step_sizes, column_starts, col_offsets, facet_offsets, adj0, swapped(adj0, 1), first)
    grid = exchange(grids(exchange(second), rows))
    gridded, residual = last_visibilities(counts, obs, weight, grid, ku, kv)
    adj1 = to_facets(adjoint(exchange(gridded), rows))
    tables = update_tables(column_starts, facet_offsets)
    step = update(step_sizes, adj0, adj1, tables)
    model = take_step(step, swapped(step, 1), model)
    return model[None], residual.reshape(2, 1, 1, VCAP)


def solution(mesh):
    in_specs = (
        P("facet", None, None),
        P(),
        P(),
        P("sub"),
        P("sub", None),
        P("sub", None),
        P(None, "sub", "facet", None),
        P(None, "sub", "facet", None),
        P("sub", "facet", None),
    )
    out_specs = (P("facet", None, None), P(None, "sub", "facet", None))
    return jax.shard_map(local, mesh=mesh, in_specs=in_specs, out_specs=out_specs, check_vma=False)
```
